32 devices in a mesh: dp: 2 (over core), rows: 4 (over y, x), cols: 4 (over z).
Axes of the slice: x: 2, y: 2, z: 4, core: 2. Of those that a mesh axis runs over, the one named last changes fastest.
Arguments:
- tokens: bfloat16 [8192, 2048], P(('dp', 'rows', 'cols')), may hold values from -6 to 6
- attention_gain: float32 [2048], replicated, may hold values from 0.5 to 1.5
- mlp_gain: float32 [2048], replicated, may hold values from 0.5 to 1.5
- w_query: bfloat16 [2048, 2048], P('rows', 'cols'), may hold values from -0.25 to 0.25
- w_key: bfloat16 [2048, 256], P('rows'), may hold values from -0.125 to 0.125
- w_value: bfloat16 [2048, 256], P('rows'), may hold values from -0.125 to 0.125
- w_out: bfloat16 [2048, 2048], P(None, 'rows'), may hold values from -0.5 to 0.5
- w_gate: bfloat16 [2048, 5632], P('rows', 'cols'), may hold values from -0.125 to 0.125
- w_up: bfloat16 [2048, 5632], P('rows', 'cols'), may hold values from -0.125 to 0.125
- w_down: bfloat16 [5632, 2048], P('cols', 'rows'), may hold values from -0.078125 to 0.078125
- segment_ids: int32 [8, 1024], P(('dp', 'rows')), may hold values from 0 to 3, never falling along the last dimension, each value on 1 to 512 neighbouring positions
- skip_mask: int32 [8], P(('dp', 'rows')), may hold values 0 or 1
- cotangent: float32 [8192, 2048], P(('dp', 'rows', 'cols')), may hold values from -6 to 6
Outputs:
- output: bfloat16 [8192, 2048], P(('dp', 'rows', 'cols'))
- input_grad: float32 [8192, 2048], P(('dp', 'rows', 'cols'))
- attention_gain_grad: float32 [2048], replicated
- mlp_gain_grad: float32 [2048], replicated
- query_grad: float32 [2048, 2048], P(('dp', 'rows'), 'cols')
- key_grad: float32 [2048, 256], replicated
- value_grad: float32 [2048, 256], replicated
- out_grad: float32 [2048, 2048], P('cols', ('dp', 'rows'))
- gate_grad: float32 [2048, 5632], P(('dp', 'rows'), 'cols')
- up_grad: float32 [2048, 5632], P(('dp', 'rows'), 'cols')
- down_grad: float32 [5632, 2048], P('cols', ('dp', 'rows'))
The draws below stay inside these ranges and needn't reach their ends.
Inputs may be any that keep to these rules, and one draw needn't show every extreme that they name: `segment_ids`: segment numbers never fall along a sequence of 1024 tokens; each sequence holds max(4, 4) documents, a document holds at most 512 tokens, and some document holds exactly that many.
All inputs are finite; a program needn't handle non-finite values. No bound on the sum of `skip_mask` on one device may be relied on, other than what follows from the above.
Results may differ from the reference program's by a relative error of at most 0.014.
Values may be sent and summed in bfloat16 or wider, within the bound.
No kernel may reach another device: no remote copies, remote signals or barrier semaphores. Data moves between devices by JAX's collectives and lax.ppermute only.
A program may use at most 320 MiB of HBM per device.

```python
import math
import jax
import jax.numpy as jnp
import numpy as np
from jax import lax

D = 2048
HEADS = 16
KV_HEADS = 2
HEAD_DIM = 128
FF = 5632
QD = 2048
KVD = 256
SEQ_LEN = 1024
TOKENS = 8192
NSEQ = 8


def with_ends(result, rng, low, high):
    longest = result.shape.index(max(result.shape))
    spots = []
    for shift in (0, 1):
        where = [jax.random.randint(jax.random.fold_in(rng, axis), (), 0, length) for axis, length in enumerate(result.shape)]
        where[longest] = (where[longest] + shift) % result.shape[longest]
        spots.append(tuple(where))
    return result.at[spots[0]].set(low).at[spots[1]].set(high)


def levels(rng, dims, shards, smallest, largest):
    gain = 1.0
    for position, parts in shards:
        draws = jax.random.uniform(jax.random.fold_in(jax.random.fold_in(rng, 6), position), (parts,), jnp.float32, smallest / len(shards), largest / len(shards))
        gain = gain * jnp.repeat(jnp.exp(draws), dims[position] // parts).reshape((-1,) + (1,) * (len(dims) - 1 - position))
    return gain


def length_profile(count, total, bound, lean):
    loads = [(1 << 20) // math.isqrt(rank ** lean) + 1 for rank in range(2, count + 1)]
    surplus, holding = total - bound - (count - 1), [1] * (count - 1)
    while surplus > 0:
        free = [i for i in range(count - 1) if holding[i] < bound]
        mass, budget = sum([loads[i] for i in free]), surplus
        for i in free:
            extra = min(bound - holding[i], max(1, budget * loads[i] // mass), surplus)
            holding[i] = holding[i] + extra
            surplus = surplus - extra
    return np.array([bound] + holding)


def uneven(key, amount, total, reach, lean):
    if amount == 2:
        one = jax.random.randint(key, (), max(1, total - reach), min(reach, total - 1) + 1)
        return jnp.stack([one, total - one])
    tallies = jnp.asarray(length_profile(amount, total, reach, lean), jnp.int32)
    pairs = (amount - 1) // 2
    donor, taker = tallies[1:1 + 2 * pairs:2], tallies[2:2 + 2 * pairs:2]
    room = jnp.minimum(donor - 1, reach - taker)
    passed = jax.random.randint(jax.random.fold_in(key, 1), (pairs,), 0, 1 << 20) % (room + 1)
    tallies = tallies.at[1:1 + 2 * pairs:2].set(donor - passed).at[2:2 + 2 * pairs:2].set(taker + passed)
    return tallies[jax.random.permutation(jax.random.fold_in(key, 2), amount)]


def noise(rng, dims, spread, limit, split=(), held_as=jnp.bfloat16):
    level = levels(rng, dims, split, -0.22, 0.18) if split else 1.0
    drawn = jax.random.normal(rng, dims, jnp.float32) * spread * level
    return jnp.minimum(jnp.maximum(drawn, -limit), limit).astype(held_as)


def setup_inputs(seed: int = 0) -> dict:
    seeds = jax.random.split(jax.random.key(seed), 14)
    tokens = noise(seeds[0], (TOKENS, D), 1.0, 6.0, ((0, 32),))
    attention_gain = jnp.clip(1.0 + 0.1 * jax.random.normal(seeds[1], (D,), jnp.float32), 0.5, 1.5)
    mlp_gain = jnp.clip(1.0 + 0.1 * jax.random.normal(seeds[2], (D,), jnp.float32), 0.5, 1.5)
    w_query = noise(seeds[3], (D, QD), (D // 4) ** -0.5, 0.25, ((0, 4), (1, 4)))
    w_key = noise(seeds[4], (D, KVD), D ** -0.5, 0.125, ((0, 4),))
    w_value = noise(seeds[5], (D, KVD), D ** -0.5, 0.125, ((0, 4),))
    w_out = noise(seeds[6], (QD, D), (QD // 16) ** -0.5, 0.5, ((1, 4),))
    w_gate = noise(seeds[7], (D, FF), D ** -0.5, 0.125, ((0, 4), (1, 4)))
    w_up = noise(seeds[8], (D, FF), D ** -0.5, 0.125, ((0, 4), (1, 4)))
    w_down = noise(seeds[9], (FF, D), FF ** -0.5, 0.078125, ((0, 4), (1, 4)))
    segment_ids = jax.vmap(lambda own: jnp.searchsorted(jnp.cumsum(uneven(own, max(4, SEQ_LEN // 256), SEQ_LEN, SEQ_LEN // 2, 2)), jnp.arange(SEQ_LEN), side="right"))(jax.random.split(seeds[10], NSEQ)).reshape((NSEQ, SEQ_LEN)).astype(jnp.int32)
    skip_mask = with_ends((jax.random.randint(seeds[11], (NSEQ,), 0, 4) < 1).astype(jnp.int32), jax.random.fold_in(seeds[11], 1), 0, 1)
    cotangent = noise(seeds[12], (TOKENS, D), 1.0, 6.0, ((0, 32),), jnp.float32)
    return {"tokens": tokens, "attention_gain": attention_gain, "mlp_gain": mlp_gain, "w_query": w_query, "w_key": w_key, "w_value": w_value, "w_out": w_out, "w_gate": w_gate, "w_up": w_up, "w_down": w_down, "segment_ids": segment_ids, "skip_mask": skip_mask, "cotangent": cotangent}


epsilon = 1e-05
negative = -1e+30
rope_base = 10000.0

@jax.custom_vjp
def low(v):
    return lax.optimization_barrier(v.astype(jnp.bfloat16)).astype(jnp.float32)

@jax.custom_vjp
def low_back(v):
    return v

def low_keep(v):
    return (low(v), None)

def low_pass(kept, grad):
    return (grad,)

def back_keep(v):
    return (v, None)

def back_low(kept, grad):
    return (low(grad),)
low.defvjp(low_keep, low_pass)
low_back.defvjp(back_keep, back_low)

def matmul(left_side, right_side):
    return jnp.dot(left_side, right_side, precision=lax.Precision.HIGHEST, preferred_element_type=jnp.float32)

def root_norm(values, gain_values):
    factor = lax.rsqrt(lax.optimization_barrier(jnp.mean(values * values, axis=-1, keepdims=True)) + epsilon)
    return values * factor * gain_values

def rotary(values, positions, direction):
    half_width = values.shape[-1] // 2
    frequency = rope_base ** (-2.0 * jnp.arange(half_width, dtype=jnp.float32) / values.shape[-1])
    angles = positions.astype(jnp.float32)[:, None] * frequency[None, :]
    cosine = jnp.cos(angles)[:, None, :]
    sine_part = direction * jnp.sin(angles)[:, None, :]
    leading = values[..., :half_width]
    trailing = values[..., half_width:]
    return jnp.concatenate([leading * cosine - trailing * sine_part, trailing * cosine + leading * sine_part], axis=-1)

def attend(query_rows, key_rows, value_rows, segments):
    length = segments.shape[0]
    group_size = HEADS // KV_HEADS
    key_full = jnp.repeat(key_rows, group_size, axis=1)
    value_full = jnp.repeat(value_rows, group_size, axis=1)
    scores = jnp.einsum('qhe,khe->hqk', query_rows, key_full, precision=lax.Precision.HIGHEST) * HEAD_DIM ** (-0.5)
    scores = low_back(scores)
    places = jnp.arange(length)
    allowed = (segments[:, None] == segments[None, :]) & (places[:, None] >= places[None, :])
    scores = jnp.where(allowed[None], scores, negative)
    attend_weights = low(jax.nn.softmax(scores, axis=-1))
    return jnp.einsum('hqk,khe->qhe', attend_weights, value_full, precision=lax.Precision.HIGHEST)

def residual_block(tokens, attention_gain, mlp_gain, w_query, w_key, w_value, w_out, w_gate, w_up, w_down, segment_ids, keep_rows):
    normed = low(root_norm(tokens, attention_gain))
    query_pre = low_back(matmul(normed, w_query))
    key_pre = low_back(matmul(normed, w_key))
    value_rows = low(low_back(matmul(normed, w_value)))
    sequences = segment_ids.shape[0]
    positions = jnp.arange(SEQ_LEN)

    def one_sequence(packed):
        query_part, key_part, value_part, segments = packed
        query_rows = low(rotary(query_part.reshape(SEQ_LEN, HEADS, HEAD_DIM), positions, 1.0))
        key_rows = low(rotary(key_part.reshape(SEQ_LEN, KV_HEADS, HEAD_DIM), positions, 1.0))
        mixed_heads = attend(query_rows, key_rows, value_part.reshape(SEQ_LEN, KV_HEADS, HEAD_DIM), segments)
        return low(low_back(mixed_heads.reshape(SEQ_LEN, HEADS * HEAD_DIM)))
    mixed_all = lax.map(jax.checkpoint(one_sequence), (query_pre.reshape(sequences, SEQ_LEN, HEADS * HEAD_DIM), key_pre.reshape(sequences, SEQ_LEN, KV_HEADS * HEAD_DIM), value_rows.reshape(sequences, SEQ_LEN, KV_HEADS * HEAD_DIM), segment_ids))
    mixed_all = mixed_all.reshape(sequences * SEQ_LEN, HEADS * HEAD_DIM)
    branch = low_back(matmul(mixed_all, w_out))
    middle = tokens + keep_rows * branch
    hidden_in = low(root_norm(middle, mlp_gain))
    gate_values = low_back(matmul(hidden_in, w_gate))
    up_values = low_back(matmul(hidden_in, w_up))
    hidden = low(jax.nn.silu(gate_values) * up_values)
    feed_values = low_back(matmul(hidden, w_down))
    return middle + keep_rows * feed_values

def reference(tokens, attention_gain, mlp_gain, w_query, w_key, w_value, w_out, w_gate, w_up, w_down, segment_ids, skip_mask, cotangent):
    keep_rows = jnp.repeat((1 - skip_mask).astype(jnp.float32), SEQ_LEN)[:, None]

    def forward(*floats):
        return residual_block(*floats, segment_ids, keep_rows)
    floats = (tokens.astype(jnp.float32), attention_gain.astype(jnp.float32), mlp_gain.astype(jnp.float32), w_query.astype(jnp.float32), w_key.astype(jnp.float32), w_value.astype(jnp.float32), w_out.astype(jnp.float32), w_gate.astype(jnp.float32), w_up.astype(jnp.float32), w_down.astype(jnp.float32))
    output, pullback = jax.vjp(forward, *floats)
    gradients = pullback(cotangent.astype(jnp.float32))
    return (output.astype(jnp.bfloat16), gradients[0], gradients[1], gradients[2], gradients[3], gradients[4], gradients[5], gradients[6], gradients[7], gradients[8], gradients[9])
```

```python
import jax
import jax.numpy as jnp
from jax import lax
from jax.sharding import PartitionSpec as P

HEADS = 16
KV_HEADS = 2
HEAD_DIM = 128

epsilon = 1e-05
negative = -1e30
rope_base = 10000.0
bf16 = jnp.bfloat16
f32 = jnp.float32


def dot(left, right, dims):
    return lax.dot_general(left, right, ((dims[:1], dims[1:]), ((), ())), preferred_element_type=f32)


def nn(left, right):
    return dot(left, right, (1, 0))


def nt(left, right):
    return dot(left, right, (1, 1))


def tn(left, right):
    return dot(left, right, (0, 0))


def after(value, *earlier):
    return lax.optimization_barrier((value,) + earlier)[0]


def xor_blocks(blocks, index):
    bit = 1
    while bit < len(blocks):
        swap = (index & bit) != 0
        blocks = [jnp.where(swap, blocks[j ^ bit], blocks[j]) for j in range(len(blocks))]
        bit *= 2
    return blocks


def xor_order(value, index, count, axis):
    return jnp.concatenate(xor_blocks(jnp.split(value, count, axis), index), axis)


def rotary_tables(positions):
    half = HEAD_DIM // 2
    frequency = rope_base ** (-2.0 * jnp.arange(half, dtype=f32) / HEAD_DIM)
    angles = positions.astype(f32)[:, None] * frequency[None, :]
    return jnp.cos(angles)[:, None, :], jnp.sin(angles)[:, None, :]


def rotate(values, cosine, sine, direction):
    heads = values.reshape(values.shape[0], -1, HEAD_DIM)
    half = HEAD_DIM // 2
    a, b = heads[..., :half], heads[..., half:]
    s = sine * direction
    turned = jnp.concatenate([a * cosine - b * s, b * cosine + a * s], axis=-1)
    return turned.reshape(values.shape)


def norm_factor(values):
    return lax.rsqrt(jnp.mean(values * values, axis=-1, keepdims=True) + epsilon)


def norm_back(grad, values, factor, gain):
    y = grad * gain
    pulled = factor * y - values * factor**3 * jnp.mean(y * values, axis=-1, keepdims=True)
    return pulled, jnp.sum(grad * values * factor, axis=0)


def local(
    tokens,
    attention_gain,
    mlp_gain,
    w_query,
    w_key,
    w_value,
    w_out,
    w_gate,
    w_up,
    w_down,
    segment_ids,
    skip_mask,
    cotangent,
):
    cols, rows = lax.axis_size("cols"), lax.axis_size("rows")
    c, r, d = lax.axis_index("cols"), lax.axis_index("rows"), lax.axis_index("dp")
    own, width = tokens.shape
    sequences, length = segment_ids.shape
    place = 2 * r + d
    blocks = 2 * rows
    step = width // blocks
    scale = HEAD_DIM ** (-0.5)

    def to_rows(value, a):
        return lax.ppermute(value, "rows", [(i, i ^ a) for i in range(rows)])

    def to_core(value):
        return lax.ppermute(value, "dp", [(0, 1), (1, 0)])

    def to_cols(value, k):
        return lax.ppermute(value, "cols", [(i, (i + k) % cols) for i in range(cols)])

    def along(value, k):
        return lax.ppermute(
            value, "cols", [(i, i + k) for i in range(cols) if 0 <= i + k < cols]
        )

    def to_xor_cols(value, k):
        return lax.ppermute(value, "cols", [(i, i ^ k) for i in range(cols)])

    def fetch_rows(piece, first):
        if rows != 4:
            return [piece] + [to_rows(piece, a) for a in range(1, rows)]
        other = 3 - first
        near = to_rows(piece, first)
        far = to_rows(piece, other)
        both = to_rows(near, other)
        got = [piece, None, None, both]
        got[first], got[other] = near, far
        return got

    def with_core(got, own_other):
        pairs = []
        for j, piece in enumerate(got):
            pairs += [piece, own_other if j == 0 else to_core(piece)]
        return pairs

    def halves(weight, axis):
        low, high = jnp.split(weight, 2, axis)
        return jnp.where(d == 0, low, high), jnp.where(d == 0, high, low)

    inputs = xor_order(tokens, place, blocks, 1).astype(f32)
    upstream = xor_order(cotangent, place, blocks, 1)
    gain_one = xor_order(attention_gain, place, blocks, 0)
    gain_two = xor_order(mlp_gain, place, blocks, 0)
    sequence = (c * own) // length
    start = (c * own) % length
    keep = (1 - lax.dynamic_index_in_dim(skip_mask, sequence, 0, False)).astype(f32)
    feed_own = (keep * upstream).astype(bf16)

    kv_mine, kv_other = halves(jnp.concatenate([w_key, w_value], 1), 0)
    kv_got = fetch_rows(kv_mine, 1)
    kv_matrix = jnp.concatenate(with_core(kv_got, kv_other), 0)
    q_mine, _ = halves(w_query, 0)
    q_parts = [q_mine] + [to_xor_cols(q_mine, k) for k in range(1, cols)]
    q_mine = jnp.concatenate(xor_blocks(q_parts, c), 1)
    q_lo, q_hi = jnp.split(q_mine, 2, 0)
    q_lo_got = fetch_rows(after(q_lo, kv_got[1]), 1)
    q_hi_got = fetch_rows(after(q_hi, kv_got[1]), 2)
    q_got = [jnp.concatenate([lo, hi], 0) for lo, hi in zip(q_lo_got, q_hi_got)]
    q_pairs = []
    for piece in q_got:
        q_pairs += [piece, to_core(piece)]
    q_matrix = jnp.concatenate(q_pairs, 0)
    o_mine, o_other = halves(w_out, 1)
    o_mine = after(o_mine, q_lo_got[1], q_hi_got[2])
    o_lo, o_hi = jnp.split(o_mine, 2, 0)
    o_lo_got, o_hi_got = fetch_rows(o_lo, 1), fetch_rows(o_hi, 2)
    o_got = [jnp.concatenate([lo, hi], 0) for lo, hi in zip(o_lo_got, o_hi_got)]
    o_matrix = jnp.concatenate(with_core(o_got, o_other), 1)

    g_mine, g_other = halves(w_gate, 0)
    u_mine, u_other = halves(w_up, 0)
    g_got = fetch_rows(after(g_mine, o_lo_got[1], o_hi_got[2]), 1)
    u_got = fetch_rows(after(u_mine, o_lo_got[1], o_hi_got[2]), 2)
    g_matrix = jnp.concatenate(with_core(g_got, g_other), 0)
    u_matrix = jnp.concatenate(with_core(u_got, u_other), 0)
    w_mine, w_other = halves(w_down, 1)
    w_mine = after(w_mine, g_got[1], u_got[2])
    w_lo, w_hi = jnp.split(w_mine, 2, 0)
    w_lo_got, w_hi_got = fetch_rows(w_lo, 1), fetch_rows(w_hi, 2)
    w_got = [jnp.concatenate([lo, hi], 0) for lo, hi in zip(w_lo_got, w_hi_got)]
    d_matrix = jnp.concatenate(with_core(w_got, w_other), 1)

    factor_one = norm_factor(inputs)
    normed = (inputs * factor_one * gain_one).astype(bf16)
    cosine, sine = rotary_tables(start + jnp.arange(own))
    kv_pre = nn(normed, kv_matrix)
    kv_width = KV_HEADS * HEAD_DIM
    kv_own = jnp.concatenate(
        [rotate(kv_pre[:, :kv_width], cosine, sine, 1.0), kv_pre[:, kv_width:]], 1
    ).astype(bf16)
    reach = min(-(-(length // 2 - 1) // own), length // own - 1)
    kv_before = [along(kv_own, k) for k in range(reach, 0, -1)]
    kv_all = jnp.concatenate(kv_before + [kv_own], 0)
    span = (reach + 1) * own
    q_rows = rotate(nn(normed, q_matrix), cosine, sine, 1.0).astype(bf16)

    feeds = [after(feed_own, q_parts[1])]
    for k in range(1, cols):
        feeds.append(to_cols(feeds[-1], 1))

    ids = lax.dynamic_index_in_dim(segment_ids, sequence, 0, False)
    ids_padded = jnp.concatenate([jnp.full((reach * own,), -1, ids.dtype), ids])
    ids_keys = lax.dynamic_slice_in_dim(ids_padded, start, span, 0)
    ids_rows = ids_keys[reach * own :]
    allowed = (ids_rows[:, None] == ids_keys[None, :]) & (
        (reach * own + jnp.arange(own))[:, None] >= jnp.arange(span)[None, :]
    )
    share = HEADS // KV_HEADS
    q_heads = q_rows.reshape(own, KV_HEADS, share, HEAD_DIM)
    k_heads = kv_all[:, :kv_width].reshape(span, KV_HEADS, HEAD_DIM)
    v_heads = kv_all[:, kv_width:].reshape(span, KV_HEADS, HEAD_DIM)

    def ein(form, a, b):
        return jnp.einsum(form, a, b, preferred_element_type=f32)

    scores = ein("bghe,kge->ghbk", q_heads, k_heads) * scale
    scores = jnp.where(allowed[None, None], scores, negative)
    top = jnp.max(scores, -1, keepdims=True)
    exponent = jnp.exp(scores - top)
    probs = exponent / jnp.sum(exponent, -1, keepdims=True)
    attend = probs.astype(bf16)
    mixed = ein("ghbk,kge->bghe", attend, v_heads).reshape(own, width).astype(bf16)
    branch = nn(mixed, o_matrix)
    middle = inputs + keep * branch
    factor_two = norm_factor(middle)
    hidden_own = (middle * factor_two * gain_two).astype(bf16)

    chunks = [hidden_own]
    for k in range(1, cols):
        chunks.append(to_cols(chunks[-1], 1))
    hiddens, gate_backs, up_backs, feed_parts, in_parts = {}, {}, {}, {}, {}
    carry_in = None
    for k in list(range(1, cols)) + [0]:
        gate = nn(chunks[k], g_matrix)
        up = nn(chunks[k], u_matrix)
        back = nt(feeds[k], d_matrix)
        s = jax.nn.sigmoid(gate)
        hiddens[k] = (gate * s * up).astype(bf16)
        gate_backs[k] = (back * up * s * (1.0 + gate * (1.0 - s))).astype(bf16)
        up_backs[k] = (back * gate * s).astype(bf16)
        part = nt(gate_backs[k], g_matrix) + nt(up_backs[k], u_matrix)
        if carry_in is not None:
            part = part + carry_in.astype(f32)
        if k != 0:
            carry_in = to_cols(part.astype(bf16), 1)
        else:
            hidden_in_back = part
    order = list(range(cols))
    h_all = jnp.concatenate([chunks[k] for k in order], 0)
    f_all = jnp.concatenate([feeds[k] for k in order], 0)
    hid_all = jnp.concatenate([hiddens[k] for k in order], 0)
    gb_all = jnp.concatenate([gate_backs[k] for k in order], 0)
    ub_all = jnp.concatenate([up_backs[k] for k in order], 0)
    down_part = tn(hid_all, f_all).astype(bf16)
    gate_part = tn(h_all, gb_all).astype(bf16)
    up_part = tn(h_all, ub_all).astype(bf16)

    from_norm, mlp_gain_part = norm_back(hidden_in_back, middle, factor_two, gain_two)
    middle_grad = upstream + from_norm
    branch_back = (keep * middle_grad).astype(bf16)
    mixed_back = nt(branch_back, o_matrix).astype(bf16)
    out_part = tn(mixed, branch_back).astype(bf16)

    carry_out = None
    for k in list(range(1, cols)) + [0]:
        part = nn(after(hiddens[k], hidden_in_back), d_matrix)
        if carry_out is not None:
            part = part + carry_out.astype(f32)
        if k != 0:
            carry_out = to_cols(part.astype(bf16), 1)
    feed_values = part
    output = (middle + keep * feed_values).astype(bf16)

    mb_heads = mixed_back.reshape(own, KV_HEADS, share, HEAD_DIM)
    weight_back = ein("bghe,kge->ghbk", mb_heads, v_heads)
    inner = jnp.sum(weight_back * probs, -1, keepdims=True)
    score_back = (probs * (weight_back - inner)).astype(bf16)
    q_turned = ein("ghbk,kge->bghe", score_back, k_heads).reshape(own, width) * scale
    k_turned = ein("ghbk,bghe->kge", score_back, q_heads).reshape(span, kv_width) * scale
    v_turned = ein("ghbk,bghe->kge", attend, mb_heads).reshape(span, kv_width)
    kv_turned = jnp.concatenate([k_turned, v_turned], 1)
    kv_back_pre = kv_turned[reach * own :]
    for k in range(1, reach + 1):
        part = kv_turned[(reach - k) * own : (reach - k + 1) * own].astype(bf16)
        kv_back_pre = kv_back_pre + along(part, -k).astype(f32)
    q_back = rotate(q_turned, cosine, sine, -1.0).astype(bf16)
    kv_back = jnp.concatenate(
        [rotate(kv_back_pre[:, :kv_width], cosine, sine, -1.0), kv_back_pre[:, kv_width:]], 1
    ).astype(bf16)
    q_part = tn(normed, q_back).astype(bf16)
    normed_back = nt(q_back, q_matrix) + nt(kv_back, kv_matrix)
    from_norm, attention_gain_part = norm_back(normed_back, inputs, factor_one, gain_one)
    input_grad = xor_order(middle_grad + from_norm, place, blocks, 1)
    kv_part = tn(normed, kv_back).astype(bf16)

    def scatter(part, axis, first):
        parts = xor_blocks(jnp.split(part, blocks, axis), place ^ (d * rows + r))
        keep_half = jnp.concatenate(parts[:rows], axis)
        send_half = jnp.concatenate(parts[rows:], axis)
        half = keep_half.astype(f32) + to_core(send_half).astype(f32)
        pieces = jnp.split(half, rows, axis)
        if rows != 4:
            total = pieces[0]
            for a in range(1, rows):
                total = total + to_rows(pieces[a].astype(bf16), a).astype(f32)
            return total
        other = 3 - first
        near = to_rows(jnp.concatenate([pieces[first], pieces[3]], axis).astype(bf16), first)
        near = jnp.split(near, 2, axis)
        mine = pieces[0] + near[0].astype(f32)
        theirs = pieces[other] + near[1].astype(f32)
        return mine + to_rows(theirs.astype(bf16), other).astype(f32)

    gate_grad = scatter(gate_part, 0, 1)
    up_grad = scatter(up_part, 0, 2)
    down_lo, down_hi = jnp.split(down_part, 2, 0)
    down_grad = jnp.concatenate([scatter(down_lo, 1, 1), scatter(down_hi, 1, 2)], 0)

    def scatter_cols(total, axis):
        pieces = xor_blocks(jnp.split(total.astype(bf16), cols, axis), c)
        result = pieces[0].astype(f32)
        for k in range(1, cols):
            result = result + to_xor_cols(pieces[k], k).astype(f32)
        return result

    out_lo, out_hi = jnp.split(out_part, 2, 0)
    out_sum = jnp.concatenate([scatter(out_lo, 1, 1), scatter(out_hi, 1, 2)], 0)
    out_grad = scatter_cols(out_sum, 0)
    q_lo, q_hi = jnp.split(q_part, 2, 1)
    q_sum = jnp.concatenate([scatter(q_lo, 0, 1), scatter(q_hi, 0, 2)], 1)
    query_grad = scatter_cols(q_sum, 1)

    kv_sum = scatter(kv_part, 0, 1).astype(bf16)
    total = kv_sum.astype(f32)
    for k in range(1, cols):
        total = total + to_xor_cols(kv_sum, k).astype(f32)
    total = total.astype(bf16)
    found = fetch_rows(total, 1)
    found = found + [to_core(x) for x in found]
    found = jnp.concatenate(xor_blocks(found, d * rows + r), 0).astype(f32)
    key_grad, value_grad = found[:, :kv_width], found[:, kv_width:]

    gains = jnp.stack([attention_gain_part, mlp_gain_part])
    gains = lax.psum(xor_order(gains, place, blocks, 1), ("dp", "rows", "cols"))
    return (
        xor_order(output, place, blocks, 1),
        input_grad,
        gains[0],
        gains[1],
        query_grad,
        key_grad,
        value_grad,
        out_grad,
        gate_grad,
        up_grad,
        down_grad,
    )


def solution(mesh):
    return jax.shard_map(
        local,
        mesh=mesh,
        in_specs=(
            P(("dp", "rows", "cols"), None),
            P(),
            P(),
            P("rows", "cols"),
            P("rows", None),
            P("rows", None),
            P(None, "rows"),
            P("rows", "cols"),
            P("rows", "cols"),
            P("cols", "rows"),
            P(("dp", "rows"), None),
            P(("dp", "rows")),
            P(("dp", "rows", "cols"), None),
        ),
        out_specs=(
            P(("dp", "rows", "cols"), None),
            P(("dp", "rows", "cols"), None),
            P(),
            P(),
            P(("dp", "rows"), "cols"),
            P(),
            P(),
            P("cols", ("dp", "rows")),
            P(("dp", "rows"), "cols"),
            P(("dp", "rows"), "cols"),
            P("cols", ("dp", "rows")),
        ),
        check_vma=False,
    )
```

```python
import jax
import jax.numpy as jnp
from jax import lax
from jax.experimental import pallas as pl
from jax.experimental.pallas import tpu as pltpu
from jax.sharding import PartitionSpec as P

HEADS = 16
KV_HEADS = 2
HEAD_DIM = 128

epsilon = 1e-05
negative = -1e30
rope_base = 10000.0
log2e = 1.4426950408889634
bf16 = jnp.bfloat16
f32 = jnp.float32


def dot(left, right, dims):
    return lax.dot_general(left, right, ((dims[:1], dims[1:]), ((), ())), preferred_element_type=f32)


def turn(values, cosine, sine):
    return values * cosine + pltpu.roll(values, HEAD_DIM // 2, 1) * sine


def mask_bias(row_ids, key_ids):
    span, own = key_ids.shape[0], row_ids.shape[1]
    key_place = lax.broadcasted_iota(jnp.int32, (span, own), 0)
    row_place = lax.broadcasted_iota(jnp.int32, (span, own), 1) + (span - own)
    return jnp.where((key_ids == row_ids) & (row_place >= key_place), 0.0, negative)


PER = 4


def forward_kernel(pre_ref, k_ref, v_ref, cos_ref, sin_ref, rid_ref, kid_ref, mixed_ref, q_ref, top_ref, bias_ref, vt_ref):
    head = pl.program_id(0) * PER

    @pl.when(head == 0)
    def _():
        bias_ref[...] = mask_bias(rid_ref[...], kid_ref[...])

    @pl.when(head % (HEADS // KV_HEADS) == 0)
    def _():
        vt_ref[...] = v_ref[...].astype(f32).T.astype(bf16)

    for n in range(PER):
        lanes = slice(n * HEAD_DIM, (n + 1) * HEAD_DIM)
        q = turn(pre_ref[:, lanes], cos_ref[...], sin_ref[...]).astype(bf16)
        q_ref[:, lanes] = q
        scores = dot(k_ref[...], q, (1, 1)) * (HEAD_DIM ** (-0.5) * log2e) + bias_ref[...]
        top = jnp.max(scores, axis=0, keepdims=True)
        exponent = jnp.exp2(scores - top)
        total = jnp.sum(exponent, axis=0, keepdims=True)
        mixed = dot(vt_ref[...], exponent.astype(bf16), (1, 0)) * (1.0 / total)
        mixed_ref[:, lanes] = mixed.T.astype(bf16)
        top_ref[n] = top + jnp.log2(total)


def attend_forward(pre, kv_all, cosine, sine, row_ids, key_ids):
    own, width = pre.shape
    span = kv_all.shape[0]
    share = HEADS // KV_HEADS
    whole = lambda shape: pl.BlockSpec(shape, lambda h: (0, 0))
    head = pl.BlockSpec((own, PER * HEAD_DIM), lambda h: (0, h))
    return pl.pallas_call(
        forward_kernel,
        grid=(HEADS // PER,),
        in_specs=[
            head,
            pl.BlockSpec((span, HEAD_DIM), lambda h: (0, h * PER // share)),
            pl.BlockSpec((span, HEAD_DIM), lambda h: (0, KV_HEADS + h * PER // share)),
            whole((own, HEAD_DIM)),
            whole((own, HEAD_DIM)),
            whole((1, own)),
            whole((span, 1)),
        ],
        out_specs=[head, head, pl.BlockSpec((PER, 1, own), lambda h: (h, 0, 0))],
        out_shape=[
            jax.ShapeDtypeStruct((own, width), bf16),
            jax.ShapeDtypeStruct((own, width), bf16),
            jax.ShapeDtypeStruct((HEADS, 1, own), f32),
        ],
        scratch_shapes=[pltpu.VMEM((span, own), f32), pltpu.VMEM((HEAD_DIM, span), bf16)],
        compiler_params=pltpu.CompilerParams(dimension_semantics=("arbitrary",), vmem_limit_bytes=32 << 20),
        cost_estimate=pl.CostEstimate(flops=0, transcendentals=0, bytes_accessed=0),
    )(pre, kv_all, kv_all, cosine, sine, row_ids[None, :], key_ids[:, None])


def backward_kernel(q_ref, k_ref, v_ref, back_ref, top_ref, cos_ref, sin_ref, rid_ref, kid_ref, dq_ref, dk_ref, dv_ref, bias_ref, kt_ref):
    step = pl.program_id(0)

    @pl.when(step == 0)
    def _():
        bias_ref[...] = mask_bias(rid_ref[...], kid_ref[...])

    @pl.when(step % (HEADS // KV_HEADS // PER) == 0)
    def _():
        kt_ref[...] = k_ref[...].astype(f32).T.astype(bf16)
        dk_ref[...] = jnp.zeros_like(dk_ref)
        dv_ref[...] = jnp.zeros_like(dv_ref)

    scale = HEAD_DIM ** (-0.5)
    for n in range(PER):
        lanes = slice(n * HEAD_DIM, (n + 1) * HEAD_DIM)
        q = q_ref[:, lanes]
        back = back_ref[:, lanes]
        scores = dot(k_ref[...], q, (1, 1)) * (scale * log2e) + bias_ref[...]
        probs = jnp.exp2(scores - top_ref[n])
        dv_ref[...] += dot(probs.astype(bf16), back, (1, 0))
        weight_back = dot(v_ref[...], back, (1, 1))
        inner = jnp.sum(weight_back * probs, axis=0, keepdims=True)
        score_back = (probs * (weight_back - inner)).astype(bf16)
        dk_ref[...] += dot(score_back, q, (1, 0)) * scale
        turned = (dot(kt_ref[...], score_back, (1, 0)) * scale).T
        dq_ref[:, lanes] = turn(turned, cos_ref[...], sin_ref[...]).astype(bf16)


def attend_backward(q_rows, kv_all, mixed_back, top, cosine, sine, row_ids, key_ids):
    own, width = q_rows.shape
    span = kv_all.shape[0]
    steps = HEADS // KV_HEADS // PER
    whole = lambda shape: pl.BlockSpec(shape, lambda h: (0, 0))
    head = pl.BlockSpec((own, PER * HEAD_DIM), lambda h: (0, h))
    shared = pl.BlockSpec((span, HEAD_DIM), lambda h: (0, h // steps))
    return pl.pallas_call(
        backward_kernel,
        grid=(HEADS // PER,),
        in_specs=[
            head,
            shared,
            pl.BlockSpec((span, HEAD_DIM), lambda h: (0, KV_HEADS + h // steps)),
            head,
            pl.BlockSpec((PER, 1, own), lambda h: (h, 0, 0)),
            whole((own, HEAD_DIM)),
            whole((own, HEAD_DIM)),
            whole((1, own)),
            whole((span, 1)),
        ],
        out_specs=[head, shared, shared],
        out_shape=[
            jax.ShapeDtypeStruct((own, width), bf16),
            jax.ShapeDtypeStruct((span, KV_HEADS * HEAD_DIM), f32),
            jax.ShapeDtypeStruct((span, KV_HEADS * HEAD_DIM), f32),
        ],
        scratch_shapes=[pltpu.VMEM((span, own), f32), pltpu.VMEM((HEAD_DIM, span), bf16)],
        compiler_params=pltpu.CompilerParams(dimension_semantics=("arbitrary",), vmem_limit_bytes=32 << 20),
        cost_estimate=pl.CostEstimate(flops=0, transcendentals=0, bytes_accessed=0),
    )(q_rows, kv_all, kv_all, mixed_back, top, cosine, sine, row_ids[None, :], key_ids[:, None])


FREE = pl.CostEstimate(flops=0, transcendentals=0, bytes_accessed=0)


def call(kernel, grid, in_specs, out_specs, out_shape, scratch=()):
    return pl.pallas_call(
        kernel,
        grid=grid,
        in_specs=in_specs,
        out_specs=out_specs,
        out_shape=out_shape,
        scratch_shapes=list(scratch),
        compiler_params=pltpu.CompilerParams(
            dimension_semantics=("arbitrary",) * len(grid), vmem_limit_bytes=48 << 20
        ),
        cost_estimate=FREE,
    )


def fixed(shape):
    return pl.BlockSpec(shape, lambda i: (0,) * len(shape))


def through_kernel(h_ref, f_ref, g_ref, u_ref, d_ref, hid_ref, gb_ref, ub_ref):
    gate = dot(h_ref[...], g_ref[...], (1, 0))
    up = dot(h_ref[...], u_ref[...], (1, 0))
    back = dot(f_ref[...], d_ref[...], (1, 1))
    s = jax.nn.sigmoid(gate)
    swish = gate * s
    hid_ref[...] = (swish * up).astype(bf16)
    ub_ref[...] = (back * swish).astype(bf16)
    gb_ref[...] = (back * up * s * (1.0 + gate * (1.0 - s))).astype(bf16)


def feed_through(hidden, feed, g_matrix, u_matrix, d_matrix):
    count, width = hidden.shape
    units = g_matrix.shape[1]
    tile = min(256, units)
    across = pl.BlockSpec((width, tile), lambda i: (0, i))
    out = pl.BlockSpec((count, tile), lambda i: (0, i))
    return call(
        through_kernel,
        (pl.cdiv(units, tile),),
        [fixed((count, width))] * 2 + [across, across, pl.BlockSpec((tile, width), lambda i: (i, 0))],
        [out] * 3,
        [jax.ShapeDtypeStruct((count, units), bf16)] * 3,
    )(hidden, feed, g_matrix, u_matrix, d_matrix)


def finish_kernel(f_ref, gate_ref, up_ref, d_ref, hid_ref, gb_ref, ub_ref):
    gate = gate_ref[...]
    back = dot(f_ref[...], d_ref[...], (1, 1))
    s = jax.nn.sigmoid(gate)
    swish = gate * s
    hid_ref[...] = (swish * up_ref[...]).astype(bf16)
    ub_ref[...] = (back * swish).astype(bf16)
    gb_ref[...] = (back * up_ref[...] * s * (1.0 + gate * (1.0 - s))).astype(bf16)


def feed_finish(feed, gate, up, d_matrix):
    count, units = gate.shape
    width = feed.shape[1]
    tile = min(256, units)
    out = pl.BlockSpec((count, tile), lambda i: (0, i))
    return call(
        finish_kernel,
        (pl.cdiv(units, tile),),
        [fixed((count, width)), out, out, pl.BlockSpec((tile, width), lambda i: (i, 0))],
        [out] * 3,
        [jax.ShapeDtypeStruct((count, units), bf16)] * 3,
    )(feed, gate, up, d_matrix)


def rows_product(lefts, rights, turned, dtype, block=0, count=None):
    n = len(lefts)
    count = lefts[0].shape[0] if count is None else count
    columns = rights[0].shape[0 if turned else 1]
    tile = min(512, columns)

    def kernel(*refs):
        total = 0.0
        for k in range(n):
            total = total + dot(refs[k][...], refs[n + k][...], (1, 1 if turned else 0))
        refs[-1][...] = total.astype(dtype)

    specs = [pl.BlockSpec((count, x.shape[1]), lambda i: (block, 0)) for x in lefts]
    for x in rights:
        if turned:
            specs.append(pl.BlockSpec((tile, x.shape[1]), lambda i: (i, 0)))
        else:
            specs.append(pl.BlockSpec((x.shape[0], tile), lambda i: (0, i)))
    return call(
        kernel,
        (columns // tile,),
        specs,
        pl.BlockSpec((count, tile), lambda i: (0, i)),
        jax.ShapeDtypeStruct((count, columns), dtype),
    )(*lefts, *rights)


def token_sum(lefts, left_lanes, rights, right_lanes, received=None):
    n = len(lefts)
    start, rows_out = left_lanes
    tile = min(256, rows_out)
    base, columns = right_lanes

    def kernel(*refs):
        total = dot(refs[0][...], refs[n][...], (0, 0))
        for k in range(1, n):
            total = total + dot(refs[k][...], refs[n + k][...], (0, 0))
        if received is not None:
            total = total + refs[2 * n][...].astype(f32)
        refs[-1][...] = total.astype(bf16)

    first, second = start // tile, base // columns
    specs = [pl.BlockSpec((x.shape[0], tile), lambda i: (0, first + i)) for x in lefts]
    specs += [pl.BlockSpec((x.shape[0], columns), lambda i: (0, second)) for x in rights]
    out = pl.BlockSpec((tile, columns), lambda i: (i, 0))
    operands = list(lefts) + list(rights)
    if received is not None:
        specs.append(out)
        operands.append(received)
    return call(
        kernel,
        (pl.cdiv(rows_out, tile),),
        specs,
        out,
        jax.ShapeDtypeStruct((rows_out, columns), bf16),
    )(*operands)


def nn(left, right):
    return dot(left, right, (1, 0))


def nt(left, right):
    return dot(left, right, (1, 1))


def tn(left, right):
    return dot(left, right, (0, 0))


def after(value, *earlier):
    return lax.optimization_barrier((value,) + earlier)[0]


def fence(*values):
    return lax.optimization_barrier(values)


def blank(shape):
    return pl.pallas_call(
        lambda out: None,
        out_specs=pl.BlockSpec(memory_space=pl.ANY),
        out_shape=jax.ShapeDtypeStruct(shape, bf16),
    )()


def xor_blocks(blocks, index):
    bit = 1
    while bit < len(blocks):
        swap = (index & bit) != 0
        blocks = [jnp.where(swap, blocks[j ^ bit], blocks[j]) for j in range(len(blocks))]
        bit *= 2
    return blocks


def xor_order(value, index, count, axis):
    return jnp.concatenate(xor_blocks(jnp.split(value, count, axis), index), axis)


def tree_sum(values):
    while len(values) > 1:
        values = [values[i] + values[i + 1] for i in range(0, len(values), 2)]
    return values[0]


def rotary_tables(positions):
    half = HEAD_DIM // 2
    frequency = rope_base ** (-2.0 * jnp.arange(half, dtype=f32) / HEAD_DIM)
    angles = positions.astype(f32)[:, None] * frequency[None, :]
    cosine, sine = jnp.cos(angles), jnp.sin(angles)
    return jnp.concatenate([cosine, cosine], 1), jnp.concatenate([-sine, sine], 1)


def rotate(values, cosine, sine):
    heads = jnp.split(values, values.shape[1] // HEAD_DIM, 1)
    half = HEAD_DIM // 2
    swapped = [jnp.concatenate([h[:, half:], h[:, :half]], 1) for h in heads]
    return jnp.concatenate([h * cosine + s * sine for h, s in zip(heads, swapped)], 1)


def norm_factor(values):
    return lax.rsqrt(jnp.mean(values * values, axis=-1, keepdims=True) + epsilon)


def norm_back(grad, values, factor, gain):
    y = grad * gain
    pulled = factor * y - values * factor**3 * jnp.mean(y * values, axis=-1, keepdims=True)
    return pulled, jnp.sum(grad * values * factor, axis=0)


def local(
    tokens,
    attention_gain,
    mlp_gain,
    w_query,
    w_key,
    w_value,
    w_out,
    w_gate,
    w_up,
    w_down,
    segment_ids,
    skip_mask,
    cotangent,
):
    cols, rows = lax.axis_size("cols"), lax.axis_size("rows")
    c, r, d = lax.axis_index("cols"), lax.axis_index("rows"), lax.axis_index("dp")
    own, width = tokens.shape
    half = width // 2
    sequences, length = segment_ids.shape
    blocks = 2 * rows
    step = width // blocks
    target = d * rows + r
    kv_width = KV_HEADS * HEAD_DIM

    def to_rows(value, a):
        return lax.ppermute(value, "rows", [(i, i ^ a) for i in range(rows)])

    def to_near(value, turn):
        pairs = []
        for core in range(2):
            a = 1 + (core ^ turn)
            pairs += [(core * rows + i, core * rows + (i ^ a)) for i in range(rows)]
        return lax.ppermute(value, ("dp", "rows"), pairs)

    first = 1 + d

    def to_core(value):
        return lax.ppermute(value, "dp", [(0, 1), (1, 0)])

    def to_cols(value, k):
        return lax.ppermute(value, "cols", [(i, (i + k) % cols) for i in range(cols)])

    def along(value, k):
        return lax.ppermute(
            value, "cols", [(i, i + k) for i in range(cols) if 0 <= i + k < cols]
        )

    def to_xor_cols(value, k):
        return lax.ppermute(value, "cols", [(i, i ^ k) for i in range(cols)])

    def spot(j, e):
        return ((2 * (r ^ j) + (d ^ e)) ^ target) * step

    def put(full, piece, axis, start, offset):
        at = (start + offset, 0) if axis == 0 else (offset, start)
        return lax.dynamic_update_slice(full, piece, at)

    def fill(full, axis, one, two, e):
        near, far = (first, 3 - first) if e == 0 else (3 - first, first)
        size = two.shape[0] // 2
        full = put(full, one, axis, spot(near, e), 0)
        full = put(full, two[:size], axis, spot(far, e), 0)
        return put(full, two[size:], axis, spot(3, e), 0)

    def halves(weight, axis):
        low, high = jnp.split(weight, 2, axis)
        return jnp.where(d == 0, low, high), jnp.where(d == 0, high, low)

    sequence = (c * own) // length
    start = (c * own) % length
    reach = min(-(-(length // 2 - 1) // own), length // own - 1)
    span = (reach + 1) * own
    units = w_gate.shape[1]

    kv_mine, kv_rest = halves(jnp.concatenate([w_key, w_value], 1), 0)
    q_mine, _ = halves(w_query, 0)
    kv_one = to_near(kv_mine, 0)
    q_parts = [q_mine] + [to_xor_cols(q_mine, k) for k in range(1, cols)]
    kv_one, tokens, attention_gain, mlp_gain, w_out, segment_ids, skip_mask, cotangent = fence(
        kv_one, tokens, attention_gain, mlp_gain, w_out, segment_ids, skip_mask, cotangent
    )
    kv_two = to_near(jnp.concatenate([kv_mine, kv_one], 0), 1)
    o_mine, o_rest = halves(w_out, 1)
    o_one = to_near(o_mine, 0)
    inputs = xor_order(tokens, target, blocks, 1).astype(f32)
    gain_one = xor_order(attention_gain, target, blocks, 0)
    gain_two = xor_order(mlp_gain, target, blocks, 0)
    factor_one = norm_factor(inputs)
    normed = (inputs * factor_one * gain_one).astype(bf16)
    cosine, sine = rotary_tables(start + jnp.arange(own))
    keep = (1 - lax.dynamic_index_in_dim(skip_mask, sequence, 0, False)).astype(f32)
    upstream = xor_order(cotangent, target, blocks, 1)
    feed_own = (keep * upstream).astype(bf16)

    (kv_two, q_parts, normed, o_one, cosine, sine, feed_own, upstream, w_down, w_gate, w_up) = fence(
        kv_two, q_parts, normed, o_one, cosine, sine, feed_own, upstream, w_down, w_gate, w_up
    )
    feeds = [feed_own, to_cols(feed_own, 1)]
    q_mine = jnp.concatenate(xor_blocks(q_parts, c), 1)
    q_one = to_near(q_mine, 0)
    kv_other = (to_core(kv_one), to_core(kv_two))
    q_own_other = to_core(q_mine)
    q_one, q_own_other, kv_other, w_down, o_one = fence(
        q_one, q_own_other, kv_other, w_down, o_one
    )
    q_sent = jnp.concatenate([q_mine, q_one], 0)
    q_two = to_near(q_sent, 1)
    kv_mine, kv_rest, kv_one, kv_two, kv_other, _ = fence(
        kv_mine, kv_rest, kv_one, kv_two, kv_other, q_sent
    )
    kv_matrix = blank((width, 2 * kv_width))
    kv_matrix = put(kv_matrix, kv_mine, 0, spot(0, 0), 0)
    kv_matrix = put(kv_matrix, kv_rest, 0, spot(0, 1), 0)
    kv_matrix = fill(kv_matrix, 0, kv_one, kv_two, 0)
    kv_matrix = fill(kv_matrix, 0, *kv_other, 1)
    kv_pre = nn(normed, kv_matrix)
    kv_own = jnp.concatenate(
        [rotate(kv_pre[:, :kv_width], cosine, sine), kv_pre[:, kv_width:]], 1
    ).astype(bf16)

    w_mine, w_rest = halves(w_down, 1)
    w_one = to_near(w_mine, 0)
    kv_own, feeds[1] = fence(kv_own, feeds[1])
    kv_before = [along(kv_own, k) for k in range(reach, 0, -1)]
    q_one_other = to_core(q_one)
    q_matrix = blank((width, width))
    q_matrix = put(q_matrix, q_mine, 0, spot(0, 0), 0)
    q_matrix = put(q_matrix, q_own_other, 0, spot(0, 1), 0)
    q_matrix = put(q_matrix, q_one, 0, spot(first, 0), 0)
    q_matrix = put(q_matrix, q_one_other, 0, spot(3 - first, 1), 0)
    ids = lax.dynamic_index_in_dim(segment_ids, sequence, 0, False)
    ids_padded = jnp.concatenate([jnp.full((reach * own,), -1, ids.dtype), ids])
    key_ids = lax.dynamic_slice_in_dim(ids_padded, start, span, 0)
    row_ids = key_ids[reach * own :]

    (q_two, w_one, q_matrix, o_mine, o_rest, o_one, w_gate, w_up) = fence(
        q_two, w_one, q_matrix, o_mine, o_rest, o_one, w_gate, w_up
    )
    feeds[1] = after(feeds[1], *kv_before)
    for k in range(2, cols - 1):
        feeds.append(to_cols(feeds[-1], 1))
    o_two = to_near(jnp.concatenate([o_mine, o_one], 0), 1)
    q_two_other = to_core(q_two)
    g_mine, g_rest = halves(w_gate, 0)
    u_mine, u_rest = halves(w_up, 0)
    gu_mine = jnp.concatenate([g_mine, u_mine], 0)
    gu_one = to_near(gu_mine, 0)
    o_one_other = to_core(o_one)
    kv_all = jnp.concatenate(list(kv_before) + [kv_own], 0)
    rows_two = q_two.shape[0] // 2
    for e, two in ((0, q_two), (1, q_two_other)):
        far = 3 - first if e == 0 else first
        q_matrix = put(q_matrix, two[:rows_two], 0, spot(far, e), 0)
        q_matrix = put(q_matrix, two[rows_two:], 0, spot(3, e), 0)
    q_pre = nn(normed, q_matrix)
    mixed, q_rows, top = attend_forward(q_pre, kv_all, cosine, sine, row_ids, key_ids)
    o_matrix = blank((width, width))
    o_matrix = put(o_matrix, o_mine, 1, spot(0, 0), 0)
    o_matrix = put(o_matrix, o_rest, 1, spot(0, 1), 0)
    o_matrix = put(o_matrix, o_one, 1, spot(first, 0), 0)
    o_matrix = put(o_matrix, o_one_other, 1, spot(3 - first, 1), 0)

    (o_two, gu_one, mixed, q_rows, top, feeds, o_matrix, w_mine, w_rest, w_one, gu_mine) = fence(
        o_two, gu_one, mixed, q_rows, top, feeds, o_matrix, w_mine, w_rest, w_one, gu_mine
    )
    feeds = list(feeds) + [to_cols(feeds[-1], 1)]
    gu_two = to_near(jnp.concatenate([gu_mine, gu_one], 0), 1)
    o_two_other = to_core(o_two)
    gu_one_other = to_core(gu_one)
    w_one_other = to_core(w_one)
    rows_two = o_two.shape[0] // 2
    for e, two in ((0, o_two), (1, o_two_other)):
        far = 3 - first if e == 0 else first
        o_matrix = put(o_matrix, two[:rows_two], 1, spot(far, e), 0)
        o_matrix = put(o_matrix, two[rows_two:], 1, spot(3, e), 0)
    branch = nn(mixed, o_matrix)
    middle = inputs + keep * branch
    factor_two = norm_factor(middle)
    hidden_own = (middle * factor_two * gain_two).astype(bf16)
    hidden_own, o_matrix, gu_one_other, w_one_other, gu_one, w_one, gu_mine, g_rest, u_rest, feeds = fence(
        hidden_own, o_matrix, gu_one_other, w_one_other, gu_one, w_one, gu_mine, g_rest, u_rest, feeds
    )
    chunks = [hidden_own, to_cols(hidden_own, 1)]
    g_matrix, u_matrix = blank((width, units)), blank((width, units))
    g_matrix = put(g_matrix, gu_mine[:step], 0, spot(0, 0), 0)
    u_matrix = put(u_matrix, gu_mine[step:], 0, spot(0, 0), 0)
    g_matrix = put(g_matrix, g_rest, 0, spot(0, 1), 0)
    u_matrix = put(u_matrix, u_rest, 0, spot(0, 1), 0)
    for e, one in ((0, gu_one), (1, gu_one_other)):
        near = first if e == 0 else 3 - first
        g_matrix = put(g_matrix, one[:step], 0, spot(near, e), 0)
        u_matrix = put(u_matrix, one[step:], 0, spot(near, e), 0)
    d_matrix = blank((units, width))
    d_matrix = put(d_matrix, w_mine, 1, spot(0, 0), 0)
    d_matrix = put(d_matrix, w_rest, 1, spot(0, 1), 0)
    d_matrix = put(d_matrix, w_one, 1, spot(first, 0), 0)
    d_matrix = put(d_matrix, w_one_other, 1, spot(3 - first, 1), 0)

    gu_two, g_matrix, u_matrix, d_matrix, w_mine, w_one, chunks = fence(
        gu_two, g_matrix, u_matrix, d_matrix, w_mine, w_one, chunks
    )
    chunks = list(chunks)
    w_two = to_near(jnp.concatenate([w_mine, w_one], 0), 1)
    gu_two_other = to_core(gu_two)
    for e, two in ((0, gu_two), (1, gu_two_other)):
        far = 3 - first if e == 0 else first
        for n, at in enumerate((spot(far, e), spot(3, e))):
            piece = two[n * 2 * step : (n + 1) * 2 * step]
            g_matrix = put(g_matrix, piece[:step], 0, at, 0)
            u_matrix = put(u_matrix, piece[step:], 0, at, 0)
    chunks.append(to_cols(chunks[1], 1))

    def gate_up(hidden):
        gate, up = nn(hidden, g_matrix), nn(hidden, u_matrix)
        return gate, up

    gate, up = gate_up(chunks[1])
    w_two, gate, up, d_matrix, arrived = fence(w_two, gate, up, d_matrix, chunks[2])
    chunks[2] = arrived
    chunks.append(to_cols(chunks[2], 1))
    w_two_other = to_core(w_two)
    rows_two = w_two.shape[0] // 2
    for e, two in ((0, w_two), (1, w_two_other)):
        far = 3 - first if e == 0 else first
        d_matrix = put(d_matrix, two[:rows_two], 1, spot(far, e), 0)
        d_matrix = put(d_matrix, two[rows_two:], 1, spot(3, e), 0)
    weights = (g_matrix, u_matrix)
    done = [feed_finish(feeds[1], gate, up, d_matrix)]
    part = rows_product(done[0][1:], weights, True, bf16)
    for k in range(2, cols - 1):
        done.append(feed_through(chunks[k], feeds[k], g_matrix, u_matrix, d_matrix))
        if k == 2:
            part, arrived, done = fence(part, chunks[3], done)
        else:
            part, carry, arrived, done = fence(part, carry, chunks[k + 1], done)
            part = (part + carry.astype(f32)).astype(bf16)
            part, done = fence(part, done)
        chunks[k + 1] = arrived
        carry = to_cols(part, 1)
        done = list(done)
        if k + 2 < cols:
            chunks.append(to_cols(chunks[k + 1], 1))
        part = rows_product(done[-1][1:], weights, True, f32)
    last_hidden = jnp.concatenate([chunks[cols - 1], chunks[0]], 0)
    last_feed = jnp.concatenate([feeds[cols - 1], feeds[0]], 0)
    done.append(feed_through(last_hidden, last_feed, g_matrix, u_matrix, d_matrix))
    hids, gbs, ubs = ([x[n] for x in done] for n in range(3))
    h_parts, f_parts = chunks[1 : cols - 1] + [last_hidden], feeds[1 : cols - 1] + [last_feed]
    low, high, full = (0, half), (half, half), (0, units)
    d_sent = token_sum(hids, full, f_parts, high)
    part, carry, d_sent, hids, gbs, ubs, h_parts, f_parts = fence(
        part, carry, d_sent, hids, gbs, ubs, h_parts, f_parts
    )
    part = (part + carry.astype(f32)).astype(bf16)
    part, d_sent, hids, gbs, ubs = fence(part, d_sent, hids, gbs, ubs)

    carry = to_cols(part, 1)
    d_received = to_core(d_sent)
    part = rows_product((gbs[-1], ubs[-1]), weights, True, f32, 0, own)
    g_sent = token_sum(h_parts, high, gbs, full)
    u_sent = token_sum(h_parts, high, ubs, full)
    d_sum = token_sum(hids, full, f_parts, low, d_received)
    part, carry, d_sum, g_sent, u_sent, hids, gbs, ubs = fence(
        part, carry, d_sum, g_sent, u_sent, hids, gbs, ubs
    )
    part = (part + carry.astype(f32)).astype(bf16)
    part, d_sum, g_sent, u_sent, gbs, ubs, hids = fence(
        part, d_sum, g_sent, u_sent, gbs, ubs, hids
    )

    def row_sum_start(total, axis):
        pieces = jnp.split(total, rows, axis)
        sent = jnp.concatenate([jnp.where(d == 0, pieces[1], pieces[2]), pieces[3]], axis)
        return [pieces, to_near(sent, 0), axis]

    def row_sum_next(state):
        pieces, near, axis = state
        mine, theirs = jnp.split(near, 2, axis)
        kept = jnp.where(d == 0, pieces[2], pieces[1])
        theirs = (kept.astype(f32) + theirs.astype(f32)).astype(bf16)
        return [pieces[0], mine, to_near(theirs, 1)]

    def row_sum_end(state):
        return state[0].astype(f32) + state[1].astype(f32) + state[2].astype(f32)

    def around(carry, part):
        return to_cols((part.astype(f32) + carry.astype(f32)).astype(bf16), 1)

    carry = to_cols(part, 1)
    d_state = row_sum_start(d_sum, 1)
    g_received = to_core(g_sent)
    u_received = to_core(u_sent)
    part = rows_product((gbs[-1], ubs[-1]), weights, True, f32, 1, own)
    outs = [rows_product([hids[0]], [d_matrix], False, bf16)]
    g_sum = token_sum(h_parts, low, gbs, full, g_received)
    u_sum = token_sum(h_parts, low, ubs, full, u_received)
    part, carry, d_state[1], g_sum, u_sum, outs, hids = fence(
        part, carry, d_state[1], g_sum, u_sum, outs, hids
    )
    outs = list(outs)

    d_state = row_sum_next(d_state)
    g_state = row_sum_start(g_sum, 0)
    out_carry = to_cols(outs[0], 1)
    hidden_in_back = part + carry.astype(f32)
    from_norm, mlp_gain_part = norm_back(hidden_in_back, middle, factor_two, gain_two)
    middle_grad = upstream + from_norm
    branch_back = (keep * middle_grad).astype(bf16)
    mixed_back = rows_product([branch_back], [o_matrix], True, bf16)
    o_sent = token_sum([mixed], (0, width), [branch_back], high)
    outs += [rows_product([x], [d_matrix], False, bf16) for x in hids[1:-1]]
    last_out = rows_product([hids[-1]], [d_matrix], False, bf16)
    outs += jnp.split(last_out, 2, 0)
    mixed_back, branch_back, o_sent, d_state[2], g_state[1], out_carry, outs = fence(
        mixed_back, branch_back, o_sent, d_state[2], g_state[1], out_carry, outs
    )

    g_state = row_sum_next(g_state)
    u_state = row_sum_start(u_sum, 0)
    for k in range(1, cols - 2):
        out_carry = around(out_carry, outs[k])
    o_received = to_core(o_sent)
    dq, dk, dv = attend_backward(
        q_rows, kv_all, mixed_back, top, cosine, -sine, row_ids, key_ids
    )
    q_sent = token_sum([normed], high, [dq], (0, width))
    o_sum = token_sum([mixed], (0, width), [branch_back], low, o_received)
    dq, dk, dv, q_sent, o_sum, g_state[2], u_state[1], out_carry = fence(
        dq, dk, dv, q_sent, o_sum, g_state[2], u_state[1], out_carry
    )

    u_state = row_sum_next(u_state)
    o_low, o_high = jnp.split(o_sum, 2, 0)
    o_low = row_sum_start(o_low, 1)
    kv_turned = jnp.concatenate([dk, dv], 1)
    kv_back_pre = kv_turned[reach * own :]
    back_parts = []
    for k in range(1, reach + 1):
        piece = kv_turned[(reach - k) * own : (reach - k + 1) * own].astype(bf16)
        back_parts.append(along(piece, -k))
    q_received = to_core(q_sent)
    down_grad = row_sum_end(d_state)
    back_parts, q_received, down_grad, u_state[2], o_low[1] = fence(
        back_parts, q_received, down_grad, u_state[2], o_low[1]
    )

    o_high = row_sum_start(o_high, 1)
    for piece in back_parts:
        kv_back_pre = kv_back_pre + piece.astype(f32)
    kv_back = jnp.concatenate(
        [rotate(kv_back_pre[:, :kv_width], cosine, -sine), kv_back_pre[:, kv_width:]], 1
    ).astype(bf16)
    kv_sent = token_sum([normed], high, [kv_back], (0, 2 * kv_width))
    kv_received = to_core(kv_sent)
    q_sum = token_sum([normed], low, [dq], (0, width), q_received)
    kv_sum = token_sum([normed], low, [kv_back], (0, 2 * kv_width), kv_received)
    kv_sum, q_sum, kv_back, o_high[1] = fence(kv_sum, q_sum, kv_back, o_high[1])

    kv_state = row_sum_start(kv_sum, 0)
    q_low, q_high = jnp.split(q_sum, 2, 1)
    q_low = row_sum_start(q_low, 0)
    out_carry = around(out_carry, outs[cols - 2])
    normed_back = rows_product([dq, kv_back], [q_matrix, kv_matrix], True, f32)
    from_norm, attention_gain_part = norm_back(normed_back, inputs, factor_one, gain_one)
    input_grad = xor_order(middle_grad + from_norm, target, blocks, 1)
    gains = xor_order(jnp.stack([attention_gain_part, mlp_gain_part]), target, blocks, 1)
    hops = [to_core, lambda x: to_rows(x, 1), lambda x: to_rows(x, 2)]
    hops += [(lambda x, k=1 << n: to_xor_cols(x, k)) for n in range(cols.bit_length() - 1)]

    def shared(values, some):
        for hop in some:
            values = values + hop(values)
        return values

    kv_state[1], q_low[1], input_grad, gains = fence(kv_state[1], q_low[1], input_grad, gains)

    kv_state = row_sum_next(kv_state)
    o_low = row_sum_next(o_low)
    gains = shared(gains, hops[:2])
    gate_grad = row_sum_end(g_state)
    kv_state[2], gains, o_low[2], gate_grad, out_carry = fence(
        kv_state[2], gains, o_low[2], gate_grad, out_carry
    )

    kv_sum = row_sum_end(kv_state).astype(bf16)
    o_high = row_sum_next(o_high)
    q_high = row_sum_start(q_high, 0)
    total = [kv_sum] + [to_xor_cols(kv_sum, k) for k in range(1, cols)]
    up_grad = row_sum_end(u_state)
    piece = outs[cols - 1].astype(f32) + out_carry.astype(f32)
    output = xor_order((middle + keep * piece).astype(bf16), target, blocks, 1)
    total, o_high[2], q_high[1], output, up_grad, gains = fence(
        total, o_high[2], q_high[1], output, up_grad, gains
    )

    def col_sum(total, axis):
        pieces = xor_blocks(jnp.split(total.astype(bf16), cols, axis), c)
        return [pieces[0]] + [to_xor_cols(pieces[k], k) for k in range(1, cols)]

    def added(values):
        return tree_sum([x.astype(f32) for x in values])

    total = tree_sum([x.astype(f32) for x in total]).astype(bf16)
    one = to_near(total, 0)
    q_low, q_high = row_sum_next(q_low), row_sum_next(q_high)
    out_sum = jnp.concatenate([row_sum_end(o_low), row_sum_end(o_high)], 0)
    gains = shared(gains, hops[2:4])
    one, q_low[2], q_high[2], out_sum, gains = fence(one, q_low[2], q_high[2], out_sum, gains)
    two = to_near(jnp.concatenate([total, one], 0), 1)
    gains = shared(gains, hops[4:])
    out_parts = col_sum(out_sum, 0)
    q_sum = jnp.concatenate([row_sum_end(q_low), row_sum_end(q_high)], 1)
    two, out_parts, q_sum, gains = fence(two, out_parts, q_sum, gains)
    mine = jnp.concatenate([total, one, two], 0)
    theirs = to_core(mine)
    q_parts = col_sum(q_sum, 1)
    out_grad = added(out_parts)
    theirs, out_grad = fence(theirs, out_grad)
    found = blank((width, 2 * kv_width))
    for e, part in enumerate((mine, theirs)):
        near, far = (first, 3 - first) if e == 0 else (3 - first, first)
        for n, j in enumerate((0, near, far, 3)):
            at = ((d ^ e) * rows + (r ^ j)) * step
            found = put(found, part[n * step : (n + 1) * step], 0, at, 0)
    found = found.astype(f32)
    key_grad, value_grad = found[:, :kv_width], found[:, kv_width:]
    q_parts, key_grad, value_grad = fence(q_parts, key_grad, value_grad)
    query_grad = added(q_parts)
    return (
        output,
        input_grad,
        gains[0],
        gains[1],
        query_grad,
        key_grad,
        value_grad,
        out_grad,
        gate_grad,
        up_grad,
        down_grad,
    )


def solution(mesh):
    return jax.shard_map(
        local,
        mesh=mesh,
        in_specs=(
            P(("dp", "rows", "cols"), None),
            P(),
            P(),
            P("rows", "cols"),
            P("rows", None),
            P("rows", None),
            P(None, "rows"),
            P("rows", "cols"),
            P("rows", "cols"),
            P("cols", "rows"),
            P(("dp", "rows"), None),
            P(("dp", "rows")),
            P(("dp", "rows", "cols"), None),
        ),
        out_specs=(
            P(("dp", "rows", "cols"), None),
            P(("dp", "rows", "cols"), None),
            P(),
            P(),
            P(("dp", "rows"), "cols"),
            P(),
            P(),
            P("cols", ("dp", "rows")),
            P(("dp", "rows"), "cols"),
            P(("dp", "rows"), "cols"),
            P("cols", ("dp", "rows")),
        ),
        check_vma=False,
    )
```

```python
import jax
import jax.numpy as jnp
from jax import lax
from jax.experimental import pallas as pl
from jax.experimental.pallas import tpu as pltpu
from jax.sharding import PartitionSpec as P

HEADS = 16
KV_HEADS = 2
HEAD_DIM = 128

epsilon = 1e-05
negative = -1e30
rope_base = 10000.0
log2e = 1.4426950408889634
bf16 = jnp.bfloat16
f32 = jnp.float32


def dot(left, right, dims):
    return lax.dot_general(left, right, ((dims[:1], dims[1:]), ((), ())), preferred_element_type=f32)


def turn(values, cosine, sine):
    return values * cosine + pltpu.roll(values, HEAD_DIM // 2, 1) * sine


def mask_bias(row_ids, key_ids):
    span, own = key_ids.shape[0], row_ids.shape[1]
    key_place = lax.broadcasted_iota(jnp.int32, (span, own), 0)
    row_place = lax.broadcasted_iota(jnp.int32, (span, own), 1) + (span - own)
    return jnp.where((key_ids == row_ids) & (row_place >= key_place), 0.0, negative)


PER = 4


def forward_kernel(pre_ref, k_ref, v_ref, cos_ref, sin_ref, rid_ref, kid_ref, mixed_ref, q_ref, top_ref, bias_ref, vt_ref):
    head = pl.program_id(0) * PER

    @pl.when(head == 0)
    def _():
        bias_ref[...] = mask_bias(rid_ref[...], kid_ref[...])

    @pl.when(head % (HEADS // KV_HEADS) == 0)
    def _():
        vt_ref[...] = v_ref[...].astype(f32).T.astype(bf16)

    for n in range(PER):
        lanes = slice(n * HEAD_DIM, (n + 1) * HEAD_DIM)
        q = turn(pre_ref[:, lanes], cos_ref[...], sin_ref[...]).astype(bf16)
        q_ref[:, lanes] = q
        scores = dot(k_ref[...], q, (1, 1)) * (HEAD_DIM ** (-0.5) * log2e) + bias_ref[...]
        top = jnp.max(scores, axis=0, keepdims=True)
        exponent = jnp.exp2(scores - top)
        total = jnp.sum(exponent, axis=0, keepdims=True)
        mixed = dot(vt_ref[...], exponent.astype(bf16), (1, 0)) * (1.0 / total)
        mixed_ref[:, lanes] = mixed.T.astype(bf16)
        top_ref[n] = top + jnp.log2(total)


def attend_forward(pre, kv_all, cosine, sine, row_ids, key_ids):
    own, width = pre.shape
    span = kv_all.shape[0]
    share = HEADS // KV_HEADS
    whole = lambda shape: pl.BlockSpec(shape, lambda h: (0, 0))
    head = pl.BlockSpec((own, PER * HEAD_DIM), lambda h: (0, h))
    return pl.pallas_call(
        forward_kernel,
        grid=(HEADS // PER,),
        in_specs=[
            head,
            pl.BlockSpec((span, HEAD_DIM), lambda h: (0, h * PER // share)),
            pl.BlockSpec((span, HEAD_DIM), lambda h: (0, KV_HEADS + h * PER // share)),
            whole((own, HEAD_DIM)),
            whole((own, HEAD_DIM)),
            whole((1, own)),
            whole((span, 1)),
        ],
        out_specs=[head, head, pl.BlockSpec((PER, 1, own), lambda h: (h, 0, 0))],
        out_shape=[
            jax.ShapeDtypeStruct((own, width), bf16),
            jax.ShapeDtypeStruct((own, width), bf16),
            jax.ShapeDtypeStruct((HEADS, 1, own), f32),
        ],
        scratch_shapes=[pltpu.VMEM((span, own), f32), pltpu.VMEM((HEAD_DIM, span), bf16)],
        compiler_params=pltpu.CompilerParams(dimension_semantics=("arbitrary",), vmem_limit_bytes=32 << 20),
        cost_estimate=pl.CostEstimate(flops=0, transcendentals=0, bytes_accessed=0),
    )(pre, kv_all, kv_all, cosine, sine, row_ids[None, :], key_ids[:, None])


def backward_kernel(q_ref, k_ref, v_ref, back_ref, top_ref, cos_ref, sin_ref, rid_ref, kid_ref, dq_ref, dk_ref, dv_ref, bias_ref, kt_ref):
    step = pl.program_id(0)

    @pl.when(step == 0)
    def _():
        bias_ref[...] = mask_bias(rid_ref[...], kid_ref[...])

    @pl.when(step % (HEADS // KV_HEADS // PER) == 0)
    def _():
        kt_ref[...] = k_ref[...].astype(f32).T.astype(bf16)
        dk_ref[...] = jnp.zeros_like(dk_ref)
        dv_ref[...] = jnp.zeros_like(dv_ref)

    scale = HEAD_DIM ** (-0.5)
    for n in range(PER):
        lanes = slice(n * HEAD_DIM, (n + 1) * HEAD_DIM)
        q = q_ref[:, lanes]
        back = back_ref[:, lanes]
        scores = dot(k_ref[...], q, (1, 1)) * (scale * log2e) + bias_ref[...]
        probs = jnp.exp2(scores - top_ref[n])
        dv_ref[...] += dot(probs.astype(bf16), back, (1, 0))
        weight_back = dot(v_ref[...], back, (1, 1))
        inner = jnp.sum(weight_back * probs, axis=0, keepdims=True)
        score_back = (probs * (weight_back - inner)).astype(bf16)
        dk_ref[...] += dot(score_back, q, (1, 0)) * scale
        turned = (dot(kt_ref[...], score_back, (1, 0)) * scale).T
        dq_ref[:, lanes] = turn(turned, cos_ref[...], sin_ref[...]).astype(bf16)


def attend_backward(q_rows, kv_all, mixed_back, top, cosine, sine, row_ids, key_ids):
    own, width = q_rows.shape
    span = kv_all.shape[0]
    steps = HEADS // KV_HEADS // PER
    whole = lambda shape: pl.BlockSpec(shape, lambda h: (0, 0))
    head = pl.BlockSpec((own, PER * HEAD_DIM), lambda h: (0, h))
    shared = pl.BlockSpec((span, HEAD_DIM), lambda h: (0, h // steps))
    return pl.pallas_call(
        backward_kernel,
        grid=(HEADS // PER,),
        in_specs=[
            head,
            shared,
            pl.BlockSpec((span, HEAD_DIM), lambda h: (0, KV_HEADS + h // steps)),
            head,
            pl.BlockSpec((PER, 1, own), lambda h: (h, 0, 0)),
            whole((own, HEAD_DIM)),
            whole((own, HEAD_DIM)),
            whole((1, own)),
            whole((span, 1)),
        ],
        out_specs=[head, shared, shared],
        out_shape=[
            jax.ShapeDtypeStruct((own, width), bf16),
            jax.ShapeDtypeStruct((span, KV_HEADS * HEAD_DIM), f32),
            jax.ShapeDtypeStruct((span, KV_HEADS * HEAD_DIM), f32),
        ],
        scratch_shapes=[pltpu.VMEM((span, own), f32), pltpu.VMEM((HEAD_DIM, span), bf16)],
        compiler_params=pltpu.CompilerParams(dimension_semantics=("arbitrary",), vmem_limit_bytes=32 << 20),
        cost_estimate=pl.CostEstimate(flops=0, transcendentals=0, bytes_accessed=0),
    )(q_rows, kv_all, kv_all, mixed_back, top, cosine, sine, row_ids[None, :], key_ids[:, None])


FREE = pl.CostEstimate(flops=0, transcendentals=0, bytes_accessed=0)


def call(kernel, grid, in_specs, out_specs, out_shape, scratch=()):
    return pl.pallas_call(
        kernel,
        grid=grid,
        in_specs=in_specs,
        out_specs=out_specs,
        out_shape=out_shape,
        scratch_shapes=list(scratch),
        compiler_params=pltpu.CompilerParams(
            dimension_semantics=("arbitrary",) * len(grid), vmem_limit_bytes=48 << 20
        ),
        cost_estimate=FREE,
    )


def fixed(shape):
    return pl.BlockSpec(shape, lambda i: (0,) * len(shape))


def through_kernel(h_ref, f_ref, g_ref, u_ref, d_ref, hid_ref, gb_ref, ub_ref):
    gate = dot(h_ref[...], g_ref[...], (1, 0))
    up = dot(h_ref[...], u_ref[...], (1, 0))
    back = dot(f_ref[...], d_ref[...], (1, 1))
    s = jax.nn.sigmoid(gate)
    swish = gate * s
    hid_ref[...] = (swish * up).astype(bf16)
    ub_ref[...] = (back * swish).astype(bf16)
    gb_ref[...] = (back * up * s * (1.0 + gate * (1.0 - s))).astype(bf16)


def feed_through(hidden, feed, g_matrix, u_matrix, d_matrix):
    count, width = hidden.shape
    units = g_matrix.shape[1]
    tile = min(256, units)
    across = pl.BlockSpec((width, tile), lambda i: (0, i))
    out = pl.BlockSpec((count, tile), lambda i: (0, i))
    return call(
        through_kernel,
        (pl.cdiv(units, tile),),
        [fixed((count, width))] * 2 + [across, across, pl.BlockSpec((tile, width), lambda i: (i, 0))],
        [out] * 3,
        [jax.ShapeDtypeStruct((count, units), bf16)] * 3,
    )(hidden, feed, g_matrix, u_matrix, d_matrix)


def finish_kernel(f_ref, gate_ref, up_ref, d_ref, hid_ref, gb_ref, ub_ref):
    gate = gate_ref[...]
    back = dot(f_ref[...], d_ref[...], (1, 1))
    s = jax.nn.sigmoid(gate)
    swish = gate * s
    hid_ref[...] = (swish * up_ref[...]).astype(bf16)
    ub_ref[...] = (back * swish).astype(bf16)
    gb_ref[...] = (back * up_ref[...] * s * (1.0 + gate * (1.0 - s))).astype(bf16)


def feed_finish(feed, gate, up, d_matrix):
    count, units = gate.shape
    width = feed.shape[1]
    tile = min(256, units)
    out = pl.BlockSpec((count, tile), lambda i: (0, i))
    return call(
        finish_kernel,
        (pl.cdiv(units, tile),),
        [fixed((count, width)), out, out, pl.BlockSpec((tile, width), lambda i: (i, 0))],
        [out] * 3,
        [jax.ShapeDtypeStruct((count, units), bf16)] * 3,
    )(feed, gate, up, d_matrix)


def rows_products(sets, rights, turned, dtype, count):
    n, many = len(rights), len(sets)
    columns = rights[0].shape[0 if turned else 1]
    tile = min(512, columns)

    def kernel(*refs):
        for m in range(many):
            total = 0.0
            for k in range(n):
                total = total + dot(refs[n + n * m + k][...], refs[k][...], (1, 1 if turned else 0))
            refs[m - many][...] = total.astype(dtype)

    specs = []
    for x in rights:
        if turned:
            specs.append(pl.BlockSpec((tile, x.shape[1]), lambda i: (i, 0)))
        else:
            specs.append(pl.BlockSpec((x.shape[0], tile), lambda i: (0, i)))
    operands = list(rights)
    for lefts, block in sets:
        specs += [pl.BlockSpec((count, x.shape[1]), lambda i, block=block: (block, 0)) for x in lefts]
        operands += list(lefts)
    return call(
        kernel,
        (columns // tile,),
        specs,
        [pl.BlockSpec((count, tile), lambda i: (0, i))] * many,
        [jax.ShapeDtypeStruct((count, columns), dtype)] * many,
    )(*operands)


def rows_product(lefts, rights, turned, dtype, block=0, count=None):
    count = lefts[0].shape[0] if count is None else count
    return rows_products([(lefts, block)], rights, turned, dtype, count)[0]


def token_sums(lefts, left_lanes, rights, right_lanes, received=None):
    n, many = len(lefts), len(rights)
    start, rows_out = left_lanes
    tile = min(256, rows_out)
    base, columns = right_lanes

    def kernel(*refs):
        for k in range(n):
            left = refs[k][...]
            for m in range(many):
                part = dot(left, refs[n * (m + 1) + k][...], (0, 0))
                totals = [part] * many if k == 0 and m == 0 else totals
                totals[m] = part if k == 0 else totals[m] + part
        for m in range(many):
            total = totals[m]
            if received is not None:
                total = total + refs[n * (many + 1) + m][...].astype(f32)
            refs[m - many][...] = total.astype(bf16)

    first, second = start // tile, base // columns
    specs = [pl.BlockSpec((x.shape[0], tile), lambda i: (0, first + i)) for x in lefts]
    operands = list(lefts)
    for group in rights:
        specs += [pl.BlockSpec((x.shape[0], columns), lambda i: (0, second)) for x in group]
        operands += list(group)
    out = pl.BlockSpec((tile, columns), lambda i: (i, 0))
    if received is not None:
        specs += [out] * many
        operands += list(received)
    return call(
        kernel,
        (pl.cdiv(rows_out, tile),),
        specs,
        [out] * many,
        [jax.ShapeDtypeStruct((rows_out, columns), bf16)] * many,
    )(*operands)


def token_sum(lefts, left_lanes, rights, right_lanes, received=None):
    received = None if received is None else [received]
    return token_sums(lefts, left_lanes, [rights], right_lanes, received)[0]


def nn(left, right):
    return dot(left, right, (1, 0))


def nt(left, right):
    return dot(left, right, (1, 1))


def tn(left, right):
    return dot(left, right, (0, 0))


def after(value, *earlier):
    return lax.optimization_barrier((value,) + earlier)[0]


def fence(*values):
    return lax.optimization_barrier(values)


def blank(shape):
    return pl.pallas_call(
        lambda out: None,
        out_specs=pl.BlockSpec(memory_space=pl.ANY),
        out_shape=jax.ShapeDtypeStruct(shape, bf16),
    )()


def xor_blocks(blocks, index):
    bit = 1
    while bit < len(blocks):
        swap = (index & bit) != 0
        blocks = [jnp.where(swap, blocks[j ^ bit], blocks[j]) for j in range(len(blocks))]
        bit *= 2
    return blocks


def xor_order(value, index, count, axis):
    return jnp.concatenate(xor_blocks(jnp.split(value, count, axis), index), axis)


def tree_sum(values):
    while len(values) > 1:
        values = [values[i] + values[i + 1] for i in range(0, len(values), 2)]
    return values[0]


def rotary_tables(positions):
    half = HEAD_DIM // 2
    frequency = rope_base ** (-2.0 * jnp.arange(half, dtype=f32) / HEAD_DIM)
    angles = positions.astype(f32)[:, None] * frequency[None, :]
    cosine, sine = jnp.cos(angles), jnp.sin(angles)
    return jnp.concatenate([cosine, cosine], 1), jnp.concatenate([-sine, sine], 1)


def rotate(values, cosine, sine):
    heads = jnp.split(values, values.shape[1] // HEAD_DIM, 1)
    half = HEAD_DIM // 2
    swapped = [jnp.concatenate([h[:, half:], h[:, :half]], 1) for h in heads]
    return jnp.concatenate([h * cosine + s * sine for h, s in zip(heads, swapped)], 1)


def norm_factor(values):
    return lax.rsqrt(jnp.mean(values * values, axis=-1, keepdims=True) + epsilon)


def norm_back(grad, values, factor, gain):
    y = grad * gain
    pulled = factor * y - values * factor**3 * jnp.mean(y * values, axis=-1, keepdims=True)
    return pulled, jnp.sum(grad * values * factor, axis=0)


def local(
    tokens,
    attention_gain,
    mlp_gain,
    w_query,
    w_key,
    w_value,
    w_out,
    w_gate,
    w_up,
    w_down,
    segment_ids,
    skip_mask,
    cotangent,
):
    cols, rows = lax.axis_size("cols"), lax.axis_size("rows")
    c, r, d = lax.axis_index("cols"), lax.axis_index("rows"), lax.axis_index("dp")
    own, width = tokens.shape
    half = width // 2
    sequences, length = segment_ids.shape
    blocks = 2 * rows
    step = width // blocks
    target = d * rows + r
    kv_width = KV_HEADS * HEAD_DIM

    def to_rows(value, a):
        return lax.ppermute(value, "rows", [(i, i ^ a) for i in range(rows)])

    def to_near(value, turn):
        pairs = []
        for core in range(2):
            a = 1 + (core ^ turn)
            pairs += [(core * rows + i, core * rows + (i ^ a)) for i in range(rows)]
        return lax.ppermute(value, ("dp", "rows"), pairs)

    first = 1 + d

    def to_core(value):
        return lax.ppermute(value, "dp", [(0, 1), (1, 0)])

    def to_cols(value, k):
        return lax.ppermute(value, "cols", [(i, (i + k) % cols) for i in range(cols)])

    def along(value, k):
        return lax.ppermute(
            value, "cols", [(i, i + k) for i in range(cols) if 0 <= i + k < cols]
        )

    def to_xor_cols(value, k):
        return lax.ppermute(value, "cols", [(i, i ^ k) for i in range(cols)])

    def spot(j, e):
        return ((2 * (r ^ j) + (d ^ e)) ^ target) * step

    def put(full, piece, axis, start, offset):
        at = (start + offset, 0) if axis == 0 else (offset, start)
        return lax.dynamic_update_slice(full, piece, at)

    def fill(full, axis, one, two, e):
        near, far = (first, 3 - first) if e == 0 else (3 - first, first)
        size = two.shape[0] // 2
        full = put(full, one, axis, spot(near, e), 0)
        full = put(full, two[:size], axis, spot(far, e), 0)
        return put(full, two[size:], axis, spot(3, e), 0)

    def halves(weight, axis):
        low, high = jnp.split(weight, 2, axis)
        return jnp.where(d == 0, low, high), jnp.where(d == 0, high, low)

    sequence = (c * own) // length
    start = (c * own) % length
    reach = min(-(-(length // 2 - 1) // own), length // own - 1)
    span = (reach + 1) * own
    units = w_gate.shape[1]

    kv_mine, kv_rest = halves(jnp.concatenate([w_key, w_value], 1), 0)
    q_mine, _ = halves(w_query, 0)
    kv_one = to_near(kv_mine, 0)
    q_parts = [q_mine] + [to_xor_cols(q_mine, k) for k in range(1, cols)]
    kv_one, tokens, attention_gain, mlp_gain, w_out, segment_ids, skip_mask, cotangent = fence(
        kv_one, tokens, attention_gain, mlp_gain, w_out, segment_ids, skip_mask, cotangent
    )
    kv_two = to_near(jnp.concatenate([kv_mine, kv_one], 0), 1)
    o_mine, o_rest = halves(w_out, 1)
    o_one = to_near(o_mine, 0)
    inputs = xor_order(tokens, target, blocks, 1).astype(f32)
    gain_one = xor_order(attention_gain, target, blocks, 0)
    gain_two = xor_order(mlp_gain, target, blocks, 0)
    factor_one = norm_factor(inputs)
    normed = (inputs * factor_one * gain_one).astype(bf16)
    cosine, sine = rotary_tables(start + jnp.arange(own))
    keep = (1 - lax.dynamic_index_in_dim(skip_mask, sequence, 0, False)).astype(f32)
    upstream = xor_order(cotangent, target, blocks, 1)
    feed_own = (keep * upstream).astype(bf16)

    (kv_two, q_parts, normed, cosine, sine, feed_own, upstream, w_down, w_gate, w_up) = fence(
        kv_two, q_parts, normed, cosine, sine, feed_own, upstream, w_down, w_gate, w_up
    )
    feeds = [feed_own, to_cols(feed_own, 1)]
    q_mine = jnp.concatenate(xor_blocks(q_parts, c), 1)
    q_one = to_near(q_mine, 0)
    kv_other = (to_core(kv_one), to_core(kv_two))
    q_own_other = to_core(q_mine)
    q_one, q_own_other, kv_other, w_down, o_one = fence(
        q_one, q_own_other, kv_other, w_down, o_one
    )
    q_sent = jnp.concatenate([q_mine, q_one], 0)
    q_two = to_near(q_sent, 1)
    kv_mine, kv_rest, kv_one, kv_two, kv_other, _ = fence(
        kv_mine, kv_rest, kv_one, kv_two, kv_other, q_sent
    )
    kv_matrix = blank((width, 2 * kv_width))
    kv_matrix = put(kv_matrix, kv_mine, 0, spot(0, 0), 0)
    kv_matrix = put(kv_matrix, kv_rest, 0, spot(0, 1), 0)
    kv_matrix = fill(kv_matrix, 0, kv_one, kv_two, 0)
    kv_matrix = fill(kv_matrix, 0, *kv_other, 1)
    kv_pre = nn(normed, kv_matrix)
    kv_own = jnp.concatenate(
        [rotate(kv_pre[:, :kv_width], cosine, sine), kv_pre[:, kv_width:]], 1
    ).astype(bf16)

    w_mine, w_rest = halves(w_down, 1)
    w_one = to_near(w_mine, 0)
    kv_own, feeds[1] = fence(kv_own, feeds[1])
    kv_before = [along(kv_own, k) for k in range(reach, 0, -1)]
    for k in range(2, cols - 1):
        feeds.append(to_cols(feeds[-1], 1))
    q_one_other = to_core(q_one)
    q_matrix = blank((width, width))
    q_matrix = put(q_matrix, q_mine, 0, spot(0, 0), 0)
    q_matrix = put(q_matrix, q_own_other, 0, spot(0, 1), 0)
    q_matrix = put(q_matrix, q_one, 0, spot(first, 0), 0)
    q_matrix = put(q_matrix, q_one_other, 0, spot(3 - first, 1), 0)
    ids = lax.dynamic_index_in_dim(segment_ids, sequence, 0, False)
    ids_padded = jnp.concatenate([jnp.full((reach * own,), -1, ids.dtype), ids])
    key_ids = lax.dynamic_slice_in_dim(ids_padded, start, span, 0)
    row_ids = key_ids[reach * own :]

    (q_two, w_one, q_matrix, o_mine, o_rest, o_one, w_gate, w_up) = fence(
        q_two, w_one, q_matrix, o_mine, o_rest, o_one, w_gate, w_up
    )
    feeds.append(to_cols(after(feeds[-1], q_two), 1))

    o_two = to_near(jnp.concatenate([o_mine, o_one], 0), 1)
    q_two_other = to_core(q_two)
    g_mine, g_rest = halves(w_gate, 0)
    u_mine, u_rest = halves(w_up, 0)
    gu_mine = jnp.concatenate([g_mine, u_mine], 0)
    gu_one = to_near(gu_mine, 0)
    o_one_other = to_core(o_one)
    kv_all = jnp.concatenate(list(kv_before) + [kv_own], 0)
    rows_two = q_two.shape[0] // 2
    for e, two in ((0, q_two), (1, q_two_other)):
        far = 3 - first if e == 0 else first
        q_matrix = put(q_matrix, two[:rows_two], 0, spot(far, e), 0)
        q_matrix = put(q_matrix, two[rows_two:], 0, spot(3, e), 0)
    q_pre = nn(normed, q_matrix)
    mixed, q_rows, top = attend_forward(q_pre, kv_all, cosine, sine, row_ids, key_ids)
    o_matrix = blank((width, width))
    o_matrix = put(o_matrix, o_mine, 1, spot(0, 0), 0)
    o_matrix = put(o_matrix, o_rest, 1, spot(0, 1), 0)
    o_matrix = put(o_matrix, o_one, 1, spot(first, 0), 0)
    o_matrix = put(o_matrix, o_one_other, 1, spot(3 - first, 1), 0)

    (o_two, gu_one, mixed, q_rows, top, feeds, o_matrix, w_mine, w_rest, w_one, gu_mine) = fence(
        o_two, gu_one, mixed, q_rows, top, feeds, o_matrix, w_mine, w_rest, w_one, gu_mine
    )
    gu_two = to_near(jnp.concatenate([gu_mine, gu_one], 0), 1)
    o_two_other = to_core(o_two)
    gu_one_other = to_core(gu_one)
    w_one_other = to_core(w_one)
    rows_two = o_two.shape[0] // 2
    for e, two in ((0, o_two), (1, o_two_other)):
        far = 3 - first if e == 0 else first
        o_matrix = put(o_matrix, two[:rows_two], 1, spot(far, e), 0)
        o_matrix = put(o_matrix, two[rows_two:], 1, spot(3, e), 0)
    branch = nn(mixed, o_matrix)
    middle = inputs + keep * branch
    factor_two = norm_factor(middle)
    hidden_own = (middle * factor_two * gain_two).astype(bf16)
    hidden_own, o_matrix, gu_one_other, w_one_other, gu_one, w_one, gu_mine, g_rest, u_rest = fence(
        hidden_own, o_matrix, gu_one_other, w_one_other, gu_one, w_one, gu_mine, g_rest, u_rest
    )
    chunks = [hidden_own, to_cols(hidden_own, 1)]
    g_matrix, u_matrix = blank((width, units)), blank((width, units))
    g_matrix = put(g_matrix, gu_mine[:step], 0, spot(0, 0), 0)
    u_matrix = put(u_matrix, gu_mine[step:], 0, spot(0, 0), 0)
    g_matrix = put(g_matrix, g_rest, 0, spot(0, 1), 0)
    u_matrix = put(u_matrix, u_rest, 0, spot(0, 1), 0)
    for e, one in ((0, gu_one), (1, gu_one_other)):
        near = first if e == 0 else 3 - first
        g_matrix = put(g_matrix, one[:step], 0, spot(near, e), 0)
        u_matrix = put(u_matrix, one[step:], 0, spot(near, e), 0)
    d_matrix = blank((units, width))
    d_matrix = put(d_matrix, w_mine, 1, spot(0, 0), 0)
    d_matrix = put(d_matrix, w_rest, 1, spot(0, 1), 0)
    d_matrix = put(d_matrix, w_one, 1, spot(first, 0), 0)
    d_matrix = put(d_matrix, w_one_other, 1, spot(3 - first, 1), 0)

    gu_two, g_matrix, u_matrix, d_matrix, w_mine, w_one, chunks = fence(
        gu_two, g_matrix, u_matrix, d_matrix, w_mine, w_one, chunks
    )
    chunks = list(chunks)
    w_two = to_near(jnp.concatenate([w_mine, w_one], 0), 1)
    gu_two_other = to_core(gu_two)
    for e, two in ((0, gu_two), (1, gu_two_other)):
        far = 3 - first if e == 0 else first
        for n, at in enumerate((spot(far, e), spot(3, e))):
            piece = two[n * 2 * step : (n + 1) * 2 * step]
            g_matrix = put(g_matrix, piece[:step], 0, at, 0)
            u_matrix = put(u_matrix, piece[step:], 0, at, 0)
    chunks.append(to_cols(chunks[1], 1))

    def gate_up(hidden):
        gate, up = nn(hidden, g_matrix), nn(hidden, u_matrix)
        return gate, up

    near_hidden = jnp.concatenate([chunks[1], chunks[0]], 0)
    near_feed = jnp.concatenate([feeds[1], feeds[0]], 0)
    gate, up = gate_up(near_hidden)
    w_two, gate, up, d_matrix, arrived = fence(w_two, gate, up, d_matrix, chunks[2])
    chunks[2] = arrived
    chunks.append(to_cols(chunks[2], 1))
    w_two_other = to_core(w_two)
    rows_two = w_two.shape[0] // 2
    for e, two in ((0, w_two), (1, w_two_other)):
        far = 3 - first if e == 0 else first
        d_matrix = put(d_matrix, two[:rows_two], 1, spot(far, e), 0)
        d_matrix = put(d_matrix, two[rows_two:], 1, spot(3, e), 0)
    weights = (g_matrix, u_matrix)
    done = [feed_finish(near_feed, gate, up, d_matrix)]
    part = rows_product(done[0][1:], weights, True, bf16, 0, own)
    part, arrived = fence(part, chunks[3])
    chunks[3] = arrived
    for k in range(2, cols - 2):
        carry = to_cols(part, 1)
        chunks.append(to_cols(chunks[k + 1], 1))
        done.append(feed_through(chunks[k], feeds[k], g_matrix, u_matrix, d_matrix))
        part = rows_product(done[-1][1:], weights, True, f32)
        part, carry, arrived, done = fence(part, carry, chunks[k + 2], done)
        done = list(done)
        chunks[k + 2] = arrived
        part = (part + carry.astype(f32)).astype(bf16)
        (part,) = fence(part)
    k = cols - 2
    carry = to_cols(part, 1)
    far_hidden = jnp.concatenate(chunks[k:], 0)
    far_feed = jnp.concatenate(feeds[k:], 0)
    done.append(feed_through(after(far_hidden, part), far_feed, g_matrix, u_matrix, d_matrix))
    hids, gbs, ubs = ([x[n] for x in done] for n in range(3))
    h_parts = [near_hidden] + chunks[2:k] + [far_hidden]
    f_parts = [near_feed] + feeds[2:k] + [far_feed]
    low, high, full = (0, half), (half, half), (0, units)
    part = rows_product((gbs[-1], ubs[-1]), weights, True, f32, 0, own)
    d_sent = token_sum(hids, full, f_parts, high)
    part, carry, d_sent, hids, gbs, ubs, h_parts, f_parts = fence(
        part, carry, d_sent, hids, gbs, ubs, h_parts, f_parts
    )
    part = (part + carry.astype(f32)).astype(bf16)
    part, d_sent, hids, gbs, ubs = fence(part, d_sent, hids, gbs, ubs)

    carry = to_cols(part, 1)
    d_received = to_core(d_sent)
    part, own_part = rows_products(
        [((gbs[-1], ubs[-1]), 1), ((gbs[0], ubs[0]), 1)], weights, True, f32, own
    )
    g_sent, u_sent = token_sums(h_parts, high, [gbs, ubs], full)
    d_sum = token_sum(hids, full, f_parts, low, d_received)
    part, own_part, carry, d_sum, g_sent, u_sent, hids, gbs, ubs = fence(
        part, own_part, carry, d_sum, g_sent, u_sent, hids, gbs, ubs
    )
    part = (part + carry.astype(f32)).astype(bf16)
    part, own_part, d_sum, g_sent, u_sent, gbs, ubs, hids = fence(
        part, own_part, d_sum, g_sent, u_sent, gbs, ubs, hids
    )

    def row_sum_start(total, axis):
        pieces = jnp.split(total, rows, axis)
        sent = jnp.concatenate([jnp.where(d == 0, pieces[1], pieces[2]), pieces[3]], axis)
        return [pieces, to_near(sent, 0), axis]

    def row_sum_next(state):
        pieces, near, axis = state
        mine, theirs = jnp.split(near, 2, axis)
        kept = jnp.where(d == 0, pieces[2], pieces[1])
        theirs = (kept.astype(f32) + theirs.astype(f32)).astype(bf16)
        return [pieces[0], mine, to_near(theirs, 1)]

    def row_sum_end(state):
        return state[0].astype(f32) + state[1].astype(f32) + state[2].astype(f32)

    def around(carry, part):
        return to_cols((part.astype(f32) + carry.astype(f32)).astype(bf16), 1)

    carry = to_cols(part, 1)
    d_state = row_sum_start(d_sum, 1)
    g_received = to_core(g_sent)
    u_received = to_core(u_sent)
    outs = jnp.split(rows_product([hids[0]], [d_matrix], False, bf16), 2, 0)
    g_sum, u_sum = token_sums(h_parts, low, [gbs, ubs], full, [g_received, u_received])
    part, carry, d_state[1], g_sum, u_sum, hids, outs = fence(
        own_part, carry, d_state[1], g_sum, u_sum, hids, outs
    )
    out_carry = to_cols(outs[0], 1)
    out_last = outs[1]

    d_state = row_sum_next(d_state)
    g_state = row_sum_start(g_sum, 0)
    hidden_in_back = part + carry.astype(f32)
    from_norm, mlp_gain_part = norm_back(hidden_in_back, middle, factor_two, gain_two)
    middle_grad = upstream + from_norm
    branch_back = (keep * middle_grad).astype(bf16)
    mixed_back = rows_product([branch_back], [o_matrix], True, bf16)
    o_sent = token_sum([mixed], (0, width), [branch_back], high)
    outs = [None] + [rows_product([x], [d_matrix], False, bf16) for x in hids[1:-1]]
    outs += jnp.split(rows_product([hids[-1]], [d_matrix], False, bf16), 2, 0)
    mixed_back, branch_back, o_sent, d_state[2], g_state[1], outs, hids, out_carry = fence(
        mixed_back, branch_back, o_sent, d_state[2], g_state[1], outs, hids, out_carry
    )
    outs = list(outs)
    for k in range(1, cols - 2):
        out_carry = around(out_carry, outs[k])

    g_state = row_sum_next(g_state)
    u_state = row_sum_start(u_sum, 0)
    o_received = to_core(o_sent)
    dq, dk, dv = attend_backward(
        q_rows, kv_all, mixed_back, top, cosine, -sine, row_ids, key_ids
    )
    q_sent = token_sum([normed], high, [dq], (0, width))
    o_sum = token_sum([mixed], (0, width), [branch_back], low, o_received)
    dq, dk, dv, q_sent, o_sum, g_state[2], u_state[1], out_carry = fence(
        dq, dk, dv, q_sent, o_sum, g_state[2], u_state[1], out_carry
    )

    u_state = row_sum_next(u_state)
    o_low, o_high = jnp.split(o_sum, 2, 0)
    o_low = row_sum_start(o_low, 1)
    kv_turned = jnp.concatenate([dk, dv], 1)
    kv_back_pre = kv_turned[reach * own :]
    back_parts = []
    for k in range(1, reach + 1):
        piece = kv_turned[(reach - k) * own : (reach - k + 1) * own].astype(bf16)
        back_parts.append(along(piece, -k))
    q_received = to_core(q_sent)
    back_parts, q_received, u_state[2], o_low[1] = fence(
        back_parts, q_received, u_state[2], o_low[1]
    )
    out_carry = around(out_carry, outs[cols - 2])

    o_high = row_sum_start(o_high, 1)
    for piece in back_parts:
        kv_back_pre = kv_back_pre + piece.astype(f32)
    kv_back = jnp.concatenate(
        [rotate(kv_back_pre[:, :kv_width], cosine, -sine), kv_back_pre[:, kv_width:]], 1
    ).astype(bf16)
    kv_sent = token_sum([normed], high, [kv_back], (0, 2 * kv_width))
    kv_received = to_core(kv_sent)
    q_sum = token_sum([normed], low, [dq], (0, width), q_received)
    kv_sum = token_sum([normed], low, [kv_back], (0, 2 * kv_width), kv_received)
    kv_sum, q_sum, kv_back, o_high[1] = fence(kv_sum, q_sum, kv_back, o_high[1])
    down_grad = row_sum_end(d_state)

    kv_state = row_sum_start(kv_sum, 0)
    q_low, q_high = jnp.split(q_sum, 2, 1)
    q_low = row_sum_start(q_low, 0)
    normed_back = rows_product([dq, kv_back], [q_matrix, kv_matrix], True, f32)
    from_norm, attention_gain_part = norm_back(normed_back, inputs, factor_one, gain_one)
    input_grad = xor_order(middle_grad + from_norm, target, blocks, 1)
    gains = xor_order(jnp.stack([attention_gain_part, mlp_gain_part]), target, blocks, 1)
    kv_state[1], q_low[1], input_grad, gains, out_carry, down_grad = fence(
        kv_state[1], q_low[1], input_grad, gains, out_carry, down_grad
    )
    kv_state = row_sum_next(kv_state)
    o_low = row_sum_next(o_low)
    for n in range(cols.bit_length() - 1):
        gains = gains + to_xor_cols(gains, 1 << n)
    gate_grad = row_sum_end(g_state)
    kv_state[2], gains, o_low[2], gate_grad, o_high[1], q_high = fence(
        kv_state[2], gains, o_low[2], gate_grad, o_high[1], q_high
    )

    kv_sum = row_sum_end(kv_state).astype(bf16)
    o_high = row_sum_next(o_high)
    q_high = row_sum_start(q_high, 0)
    total = [kv_sum] + [to_xor_cols(kv_sum, k) for k in range(1, cols)]
    up_grad = row_sum_end(u_state)
    total, o_high[2], q_high[1], up_grad = fence(total, o_high[2], q_high[1], up_grad)

    def col_sum(total, axis):
        pieces = xor_blocks(jnp.split(total.astype(bf16), cols, axis), c)
        return [pieces[0]] + [to_xor_cols(pieces[k], k) for k in range(1, cols)]

    def added(values):
        return tree_sum([x.astype(f32) for x in values])

    total = tree_sum([x.astype(f32) for x in total]).astype(bf16)
    one = to_near(total, 0)
    low_pieces, low_near, _ = q_low
    high_pieces, high_near, _ = q_high
    q_state = row_sum_next(
        [
            [jnp.concatenate(pair, 1) for pair in zip(low_pieces, high_pieces)],
            jnp.concatenate([low_near, high_near], 1),
            0,
        ]
    )
    out_parts = col_sum(jnp.concatenate([row_sum_end(o_low), row_sum_end(o_high)], 0), 0)
    piece = out_last.astype(f32) + out_carry.astype(f32)
    output = xor_order((middle + keep * piece).astype(bf16), target, blocks, 1)
    one, q_state[2], out_parts, output, gains = fence(one, q_state[2], out_parts, output, gains)
    two = to_near(jnp.concatenate([total, one], 0), 1)
    gains = gains + to_near(gains, 0)
    gains = gains + to_near(gains, 1)
    q_parts = col_sum(row_sum_end(q_state), 1)
    out_grad = added(out_parts)
    two, q_parts, out_grad, gains = fence(two, q_parts, out_grad, gains)
    mine = jnp.concatenate([total, one, two], 0)
    theirs = to_core(mine)
    gains = gains + to_core(gains)
    query_grad = added(q_parts)
    found = blank((width, 2 * kv_width))
    for e, part in enumerate((mine, theirs)):
        near, far = (first, 3 - first) if e == 0 else (3 - first, first)
        for n, j in enumerate((0, near, far, 3)):
            at = ((d ^ e) * rows + (r ^ j)) * step
            found = put(found, part[n * step : (n + 1) * step], 0, at, 0)
    found = found.astype(f32)
    key_grad, value_grad = found[:, :kv_width], found[:, kv_width:]
    return (
        output,
        input_grad,
        gains[0],
        gains[1],
        query_grad,
        key_grad,
        value_grad,
        out_grad,
        gate_grad,
        up_grad,
        down_grad,
    )


def solution(mesh):
    return jax.shard_map(
        local,
        mesh=mesh,
        in_specs=(
            P(("dp", "rows", "cols"), None),
            P(),
            P(),
            P("rows", "cols"),
            P("rows", None),
            P("rows", None),
            P(None, "rows"),
            P("rows", "cols"),
            P("rows", "cols"),
            P("cols", "rows"),
            P(("dp", "rows"), None),
            P(("dp", "rows")),
            P(("dp", "rows", "cols"), None),
        ),
        out_specs=(
            P(("dp", "rows", "cols"), None),
            P(("dp", "rows", "cols"), None),
            P(),
            P(),
            P(("dp", "rows"), "cols"),
            P(),
            P(),
            P("cols", ("dp", "rows")),
            P(("dp", "rows"), "cols"),
            P(("dp", "rows"), "cols"),
            P("cols", ("dp", "rows")),
        ),
        check_vma=False,
    )
```

```python
import jax
import jax.numpy as jnp
from jax import lax
from jax.experimental import pallas as pl
from jax.experimental.pallas import tpu as pltpu
from jax.sharding import PartitionSpec as P

HEADS = 16
KV_HEADS = 2
HEAD_DIM = 128

epsilon = 1e-05
negative = -1e30
rope_base = 10000.0
log2e = 1.4426950408889634
bf16 = jnp.bfloat16
f32 = jnp.float32


def dot(left, right, dims):
    return lax.dot_general(left, right, ((dims[:1], dims[1:]), ((), ())), preferred_element_type=f32)


def turn(values, cosine, sine):
    return values * cosine + pltpu.roll(values, HEAD_DIM // 2, 1) * sine


def mask_bias(row_ids, key_ids):
    span, own = key_ids.shape[0], row_ids.shape[1]
    key_place = lax.broadcasted_iota(jnp.int32, (span, own), 0)
    row_place = lax.broadcasted_iota(jnp.int32, (span, own), 1) + (span - own)
    return jnp.where((key_ids == row_ids) & (row_place >= key_place), 0.0, negative)


PER = 4


def forward_kernel(pre_ref, k_ref, v_ref, cos_ref, sin_ref, rid_ref, kid_ref, mixed_ref, q_ref, top_ref, bias_ref, vt_ref):
    head = pl.program_id(0) * PER

    @pl.when(head == 0)
    def _():
        bias_ref[...] = mask_bias(rid_ref[...], kid_ref[...])

    @pl.when(head % (HEADS // KV_HEADS) == 0)
    def _():
        vt_ref[...] = v_ref[...].astype(f32).T.astype(bf16)

    for n in range(PER):
        lanes = slice(n * HEAD_DIM, (n + 1) * HEAD_DIM)
        q = turn(pre_ref[:, lanes], cos_ref[...], sin_ref[...]).astype(bf16)
        q_ref[:, lanes] = q
        scores = dot(k_ref[...], q, (1, 1)) * (HEAD_DIM ** (-0.5) * log2e) + bias_ref[...]
        top = jnp.max(scores, axis=0, keepdims=True)
        exponent = jnp.exp2(scores - top)
        total = jnp.sum(exponent, axis=0, keepdims=True)
        mixed = dot(vt_ref[...], exponent.astype(bf16), (1, 0)) * (1.0 / total)
        mixed_ref[:, lanes] = mixed.T.astype(bf16)
        top_ref[n] = top + jnp.log2(total)


def attend_forward(pre, kv_all, cosine, sine, row_ids, key_ids):
    own, width = pre.shape
    span = kv_all.shape[0]
    share = HEADS // KV_HEADS
    whole = lambda shape: pl.BlockSpec(shape, lambda h: (0, 0))
    head = pl.BlockSpec((own, PER * HEAD_DIM), lambda h: (0, h))
    return pl.pallas_call(
        forward_kernel,
        grid=(HEADS // PER,),
        in_specs=[
            head,
            pl.BlockSpec((span, HEAD_DIM), lambda h: (0, h * PER // share)),
            pl.BlockSpec((span, HEAD_DIM), lambda h: (0, KV_HEADS + h * PER // share)),
            whole((own, HEAD_DIM)),
            whole((own, HEAD_DIM)),
            whole((1, own)),
            whole((span, 1)),
        ],
        out_specs=[head, head, pl.BlockSpec((PER, 1, own), lambda h: (h, 0, 0))],
        out_shape=[
            jax.ShapeDtypeStruct((own, width), bf16),
            jax.ShapeDtypeStruct((own, width), bf16),
            jax.ShapeDtypeStruct((HEADS, 1, own), f32),
        ],
        scratch_shapes=[pltpu.VMEM((span, own), f32), pltpu.VMEM((HEAD_DIM, span), bf16)],
        compiler_params=pltpu.CompilerParams(dimension_semantics=("arbitrary",), vmem_limit_bytes=32 << 20),
        cost_estimate=pl.CostEstimate(flops=0, transcendentals=0, bytes_accessed=0),
    )(pre, kv_all, kv_all, cosine, sine, row_ids[None, :], key_ids[:, None])


def backward_kernel(q_ref, k_ref, v_ref, back_ref, top_ref, cos_ref, sin_ref, rid_ref, kid_ref, dq_ref, dk_ref, dv_ref, bias_ref, kt_ref):
    step = pl.program_id(0)

    @pl.when(step == 0)
    def _():
        bias_ref[...] = mask_bias(rid_ref[...], kid_ref[...])

    @pl.when(step % (HEADS // KV_HEADS // PER) == 0)
    def _():
        kt_ref[...] = k_ref[...].astype(f32).T.astype(bf16)
        dk_ref[...] = jnp.zeros_like(dk_ref)
        dv_ref[...] = jnp.zeros_like(dv_ref)

    scale = HEAD_DIM ** (-0.5)
    for n in range(PER):
        lanes = slice(n * HEAD_DIM, (n + 1) * HEAD_DIM)
        q = q_ref[:, lanes]
        back = back_ref[:, lanes]
        scores = dot(k_ref[...], q, (1, 1)) * (scale * log2e) + bias_ref[...]
        probs = jnp.exp2(scores - top_ref[n])
        dv_ref[...] += dot(probs.astype(bf16), back, (1, 0))
        weight_back = dot(v_ref[...], back, (1, 1))
        inner = jnp.sum(weight_back * probs, axis=0, keepdims=True)
        score_back = (probs * (weight_back - inner)).astype(bf16)
        dk_ref[...] += dot(score_back, q, (1, 0)) * scale
        turned = (dot(kt_ref[...], score_back, (1, 0)) * scale).T
        dq_ref[:, lanes] = turn(turned, cos_ref[...], sin_ref[...]).astype(bf16)


def attend_backward(q_rows, kv_all, mixed_back, top, cosine, sine, row_ids, key_ids):
    own, width = q_rows.shape
    span = kv_all.shape[0]
    steps = HEADS // KV_HEADS // PER
    whole = lambda shape: pl.BlockSpec(shape, lambda h: (0, 0))
    head = pl.BlockSpec((own, PER * HEAD_DIM), lambda h: (0, h))
    shared = pl.BlockSpec((span, HEAD_DIM), lambda h: (0, h // steps))
    return pl.pallas_call(
        backward_kernel,
        grid=(HEADS // PER,),
        in_specs=[
            head,
            shared,
            pl.BlockSpec((span, HEAD_DIM), lambda h: (0, KV_HEADS + h // steps)),
            head,
            pl.BlockSpec((PER, 1, own), lambda h: (h, 0, 0)),
            whole((own, HEAD_DIM)),
            whole((own, HEAD_DIM)),
            whole((1, own)),
            whole((span, 1)),
        ],
        out_specs=[head, shared, shared],
        out_shape=[
            jax.ShapeDtypeStruct((own, width), bf16),
            jax.ShapeDtypeStruct((span, KV_HEADS * HEAD_DIM), f32),
            jax.ShapeDtypeStruct((span, KV_HEADS * HEAD_DIM), f32),
        ],
        scratch_shapes=[pltpu.VMEM((span, own), f32), pltpu.VMEM((HEAD_DIM, span), bf16)],
        compiler_params=pltpu.CompilerParams(dimension_semantics=("arbitrary",), vmem_limit_bytes=32 << 20),
        cost_estimate=pl.CostEstimate(flops=0, transcendentals=0, bytes_accessed=0),
    )(q_rows, kv_all, kv_all, mixed_back, top, cosine, sine, row_ids[None, :], key_ids[:, None])


FREE = pl.CostEstimate(flops=0, transcendentals=0, bytes_accessed=0)


def call(kernel, grid, in_specs, out_specs, out_shape, scratch=()):
    return pl.pallas_call(
        kernel,
        grid=grid,
        in_specs=in_specs,
        out_specs=out_specs,
        out_shape=out_shape,
        scratch_shapes=list(scratch),
        compiler_params=pltpu.CompilerParams(
            dimension_semantics=("arbitrary",) * len(grid), vmem_limit_bytes=48 << 20
        ),
        cost_estimate=FREE,
    )


def fixed(shape):
    return pl.BlockSpec(shape, lambda i: (0,) * len(shape))


def through_kernel(h_ref, f_ref, g_ref, u_ref, d_ref, hid_ref, gb_ref, ub_ref):
    gate = dot(h_ref[...], g_ref[...], (1, 0))
    up = dot(h_ref[...], u_ref[...], (1, 0))
    back = dot(f_ref[...], d_ref[...], (1, 1))
    s = jax.nn.sigmoid(gate)
    swish = gate * s
    hid_ref[...] = (swish * up).astype(bf16)
    ub_ref[...] = (back * swish).astype(bf16)
    gb_ref[...] = (back * up * s * (1.0 + gate * (1.0 - s))).astype(bf16)


def feed_through(hidden, feed, g_matrix, u_matrix, d_matrix):
    count, width = hidden.shape
    units = g_matrix.shape[1]
    tile = min(256, units)
    across = pl.BlockSpec((width, tile), lambda i: (0, i))
    out = pl.BlockSpec((count, tile), lambda i: (0, i))
    return call(
        through_kernel,
        (pl.cdiv(units, tile),),
        [fixed((count, width))] * 2 + [across, across, pl.BlockSpec((tile, width), lambda i: (i, 0))],
        [out] * 3,
        [jax.ShapeDtypeStruct((count, units), bf16)] * 3,
    )(hidden, feed, g_matrix, u_matrix, d_matrix)


def finish_kernel(f_ref, gate_ref, up_ref, d_ref, hid_ref, gb_ref, ub_ref):
    gate = gate_ref[...]
    back = dot(f_ref[...], d_ref[...], (1, 1))
    s = jax.nn.sigmoid(gate)
    swish = gate * s
    hid_ref[...] = (swish * up_ref[...]).astype(bf16)
    ub_ref[...] = (back * swish).astype(bf16)
    gb_ref[...] = (back * up_ref[...] * s * (1.0 + gate * (1.0 - s))).astype(bf16)


def feed_finish(feed, gate, up, d_matrix):
    count, units = gate.shape
    width = feed.shape[1]
    tile = min(256, units)
    out = pl.BlockSpec((count, tile), lambda i: (0, i))
    return call(
        finish_kernel,
        (pl.cdiv(units, tile),),
        [fixed((count, width)), out, out, pl.BlockSpec((tile, width), lambda i: (i, 0))],
        [out] * 3,
        [jax.ShapeDtypeStruct((count, units), bf16)] * 3,
    )(feed, gate, up, d_matrix)


def rows_products(sets, rights, turned, dtype, count):
    n, many = len(rights), len(sets)
    columns = rights[0].shape[0 if turned else 1]
    tile = min(512, columns)

    def kernel(*refs):
        for m in range(many):
            total = 0.0
            for k in range(n):
                total = total + dot(refs[n + n * m + k][...], refs[k][...], (1, 1 if turned else 0))
            refs[m - many][...] = total.astype(dtype)

    specs = []
    for x in rights:
        if turned:
            specs.append(pl.BlockSpec((tile, x.shape[1]), lambda i: (i, 0)))
        else:
            specs.append(pl.BlockSpec((x.shape[0], tile), lambda i: (0, i)))
    operands = list(rights)
    for lefts, block in sets:
        specs += [pl.BlockSpec((count, x.shape[1]), lambda i, block=block: (block, 0)) for x in lefts]
        operands += list(lefts)
    return call(
        kernel,
        (columns // tile,),
        specs,
        [pl.BlockSpec((count, tile), lambda i: (0, i))] * many,
        [jax.ShapeDtypeStruct((count, columns), dtype)] * many,
    )(*operands)


def rows_product(lefts, rights, turned, dtype, block=0, count=None):
    count = lefts[0].shape[0] if count is None else count
    return rows_products([(lefts, block)], rights, turned, dtype, count)[0]


def token_sums(lefts, left_lanes, rights, right_lanes, received=None):
    n, many = len(lefts), len(rights)
    start, rows_out = left_lanes
    tile = min(256, rows_out)
    base, columns = right_lanes

    def kernel(*refs):
        for k in range(n):
            left = refs[k][...]
            for m in range(many):
                part = dot(left, refs[n * (m + 1) + k][...], (0, 0))
                totals = [part] * many if k == 0 and m == 0 else totals
                totals[m] = part if k == 0 else totals[m] + part
        for m in range(many):
            total = totals[m]
            if received is not None:
                total = total + refs[n * (many + 1) + m][...].astype(f32)
            refs[m - many][...] = total.astype(bf16)

    first, second = start // tile, base // columns
    specs = [pl.BlockSpec((x.shape[0], tile), lambda i: (0, first + i)) for x in lefts]
    operands = list(lefts)
    for group in rights:
        specs += [pl.BlockSpec((x.shape[0], columns), lambda i: (0, second)) for x in group]
        operands += list(group)
    out = pl.BlockSpec((tile, columns), lambda i: (i, 0))
    if received is not None:
        specs += [out] * many
        operands += list(received)
    return call(
        kernel,
        (pl.cdiv(rows_out, tile),),
        specs,
        [out] * many,
        [jax.ShapeDtypeStruct((rows_out, columns), bf16)] * many,
    )(*operands)


def token_sum(lefts, left_lanes, rights, right_lanes, received=None):
    received = None if received is None else [received]
    return token_sums(lefts, left_lanes, [rights], right_lanes, received)[0]


def nn(left, right):
    return dot(left, right, (1, 0))


def nt(left, right):
    return dot(left, right, (1, 1))


def tn(left, right):
    return dot(left, right, (0, 0))


def after(value, *earlier):
    return lax.optimization_barrier((value,) + earlier)[0]


def fence(*values):
    return lax.optimization_barrier(values)


def blank(shape):
    return pl.pallas_call(
        lambda out: None,
        out_specs=pl.BlockSpec(memory_space=pl.ANY),
        out_shape=jax.ShapeDtypeStruct(shape, bf16),
    )()


def xor_blocks(blocks, index):
    bit = 1
    while bit < len(blocks):
        swap = (index & bit) != 0
        blocks = [jnp.where(swap, blocks[j ^ bit], blocks[j]) for j in range(len(blocks))]
        bit *= 2
    return blocks


def xor_order(value, index, count, axis):
    return jnp.concatenate(xor_blocks(jnp.split(value, count, axis), index), axis)


def tree_sum(values):
    while len(values) > 1:
        values = [values[i] + values[i + 1] for i in range(0, len(values), 2)]
    return values[0]


def rotary_tables(positions):
    half = HEAD_DIM // 2
    frequency = rope_base ** (-2.0 * jnp.arange(half, dtype=f32) / HEAD_DIM)
    angles = positions.astype(f32)[:, None] * frequency[None, :]
    cosine, sine = jnp.cos(angles), jnp.sin(angles)
    return jnp.concatenate([cosine, cosine], 1), jnp.concatenate([-sine, sine], 1)


def rotate(values, cosine, sine):
    heads = jnp.split(values, values.shape[1] // HEAD_DIM, 1)
    half = HEAD_DIM // 2
    swapped = [jnp.concatenate([h[:, half:], h[:, :half]], 1) for h in heads]
    return jnp.concatenate([h * cosine + s * sine for h, s in zip(heads, swapped)], 1)


def norm_factor(values):
    return lax.rsqrt(jnp.mean(values * values, axis=-1, keepdims=True) + epsilon)


def norm_back(grad, values, factor, gain):
    y = grad * gain
    pulled = factor * y - values * factor**3 * jnp.mean(y * values, axis=-1, keepdims=True)
    return pulled, jnp.sum(grad * values * factor, axis=0)


def local(
    tokens,
    attention_gain,
    mlp_gain,
    w_query,
    w_key,
    w_value,
    w_out,
    w_gate,
    w_up,
    w_down,
    segment_ids,
    skip_mask,
    cotangent,
):
    cols, rows = lax.axis_size("cols"), lax.axis_size("rows")
    c, r, d = lax.axis_index("cols"), lax.axis_index("rows"), lax.axis_index("dp")
    own, width = tokens.shape
    half = width // 2
    sequences, length = segment_ids.shape
    blocks = 2 * rows
    step = width // blocks
    target = d * rows + r
    kv_width = KV_HEADS * HEAD_DIM

    def to_rows(value, a):
        return lax.ppermute(value, "rows", [(i, i ^ a) for i in range(rows)])

    def to_near(value, turn):
        pairs = []
        for core in range(2):
            a = 1 + (core ^ turn)
            pairs += [(core * rows + i, core * rows + (i ^ a)) for i in range(rows)]
        return lax.ppermute(value, ("dp", "rows"), pairs)

    first = 1 + d

    def to_core(value):
        return lax.ppermute(value, "dp", [(0, 1), (1, 0)])

    def to_cols(value, k):
        return lax.ppermute(value, "cols", [(i, (i + k) % cols) for i in range(cols)])

    def along(value, k):
        return lax.ppermute(
            value, "cols", [(i, i + k) for i in range(cols) if 0 <= i + k < cols]
        )

    def to_xor_cols(value, k):
        return lax.ppermute(value, "cols", [(i, i ^ k) for i in range(cols)])

    def spot(j, e):
        return ((2 * (r ^ j) + (d ^ e)) ^ target) * step

    def put(full, piece, axis, start, offset):
        at = (start + offset, 0) if axis == 0 else (offset, start)
        return lax.dynamic_update_slice(full, piece, at)

    def fill(full, axis, one, two, e):
        near, far = (first, 3 - first) if e == 0 else (3 - first, first)
        size = two.shape[0] // 2
        full = put(full, one, axis, spot(near, e), 0)
        full = put(full, two[:size], axis, spot(far, e), 0)
        return put(full, two[size:], axis, spot(3, e), 0)

    def halves(weight, axis):
        low, high = jnp.split(weight, 2, axis)
        return jnp.where(d == 0, low, high), jnp.where(d == 0, high, low)

    sequence = (c * own) // length
    start = (c * own) % length
    reach = min(-(-(length // 2 - 1) // own), length // own - 1)
    span = (reach + 1) * own
    units = w_gate.shape[1]

    kv_mine, kv_rest = halves(jnp.concatenate([w_key, w_value], 1), 0)
    q_mine, _ = halves(w_query, 0)
    kv_one = to_near(kv_mine, 0)
    q_parts = [q_mine] + [to_xor_cols(q_mine, k) for k in range(1, cols)]
    kv_one, tokens, attention_gain, mlp_gain, w_out, segment_ids, skip_mask, cotangent = fence(
        kv_one, tokens, attention_gain, mlp_gain, w_out, segment_ids, skip_mask, cotangent
    )
    kv_two = to_near(jnp.concatenate([kv_mine, kv_one], 0), 1)
    o_mine, o_rest = halves(w_out, 1)
    o_one = to_near(o_mine, 0)
    inputs = xor_order(tokens, target, blocks, 1).astype(f32)
    gain_one = xor_order(attention_gain, target, blocks, 0)
    gain_two = xor_order(mlp_gain, target, blocks, 0)
    factor_one = norm_factor(inputs)
    normed = (inputs * factor_one * gain_one).astype(bf16)
    cosine, sine = rotary_tables(start + jnp.arange(own))
    keep = (1 - lax.dynamic_index_in_dim(skip_mask, sequence, 0, False)).astype(f32)
    upstream = xor_order(cotangent, target, blocks, 1)
    feed_own = (keep * upstream).astype(bf16)

    (kv_two, q_parts, normed, cosine, sine, feed_own, upstream, w_down, w_gate, w_up) = fence(
        kv_two, q_parts, normed, cosine, sine, feed_own, upstream, w_down, w_gate, w_up
    )
    feeds = [feed_own, to_cols(feed_own, 1)]
    q_mine = jnp.concatenate(xor_blocks(q_parts, c), 1)
    q_one = to_near(q_mine, 0)
    kv_other = (to_core(kv_one), to_core(kv_two))
    q_own_other = to_core(q_mine)
    q_one, q_own_other, kv_other, w_down, o_one = fence(
        q_one, q_own_other, kv_other, w_down, o_one
    )
    q_sent = jnp.concatenate([q_mine, q_one], 0)
    q_two = to_near(q_sent, 1)
    kv_mine, kv_rest, kv_one, kv_two, kv_other, _ = fence(
        kv_mine, kv_rest, kv_one, kv_two, kv_other, q_sent
    )
    kv_matrix = blank((width, 2 * kv_width))
    kv_matrix = put(kv_matrix, kv_mine, 0, spot(0, 0), 0)
    kv_matrix = put(kv_matrix, kv_rest, 0, spot(0, 1), 0)
    kv_matrix = fill(kv_matrix, 0, kv_one, kv_two, 0)
    kv_matrix = fill(kv_matrix, 0, *kv_other, 1)
    kv_pre = nn(normed, kv_matrix)
    kv_own = jnp.concatenate(
        [rotate(kv_pre[:, :kv_width], cosine, sine), kv_pre[:, kv_width:]], 1
    ).astype(bf16)

    w_mine, w_rest = halves(w_down, 1)
    w_one = to_near(w_mine, 0)
    kv_own, feeds[1] = fence(kv_own, feeds[1])
    kv_before = [along(kv_own, k) for k in range(reach, 0, -1)]
    for k in range(2, cols - 1):
        feeds.append(to_cols(feeds[-1], 1))
    q_one_other = to_core(q_one)
    q_matrix = blank((width, width))
    q_matrix = put(q_matrix, q_mine, 0, spot(0, 0), 0)
    q_matrix = put(q_matrix, q_own_other, 0, spot(0, 1), 0)
    q_matrix = put(q_matrix, q_one, 0, spot(first, 0), 0)
    q_matrix = put(q_matrix, q_one_other, 0, spot(3 - first, 1), 0)
    ids = lax.dynamic_index_in_dim(segment_ids, sequence, 0, False)
    ids_padded = jnp.concatenate([jnp.full((reach * own,), -1, ids.dtype), ids])
    key_ids = lax.dynamic_slice_in_dim(ids_padded, start, span, 0)
    row_ids = key_ids[reach * own :]

    (q_two, w_one, q_matrix, o_mine, o_rest, o_one, w_gate, w_up) = fence(
        q_two, w_one, q_matrix, o_mine, o_rest, o_one, w_gate, w_up
    )
    feeds.append(to_cols(after(feeds[-1], q_two), 1))

    o_two = to_near(jnp.concatenate([o_mine, o_one], 0), 1)
    q_two_other = to_core(q_two)
    g_mine, g_rest = halves(w_gate, 0)
    u_mine, u_rest = halves(w_up, 0)
    gu_mine = jnp.concatenate([g_mine, u_mine], 0)
    gu_one = to_near(gu_mine, 0)
    o_one_other = to_core(o_one)
    kv_all = jnp.concatenate(list(kv_before) + [kv_own], 0)
    rows_two = q_two.shape[0] // 2
    for e, two in ((0, q_two), (1, q_two_other)):
        far = 3 - first if e == 0 else first
        q_matrix = put(q_matrix, two[:rows_two], 0, spot(far, e), 0)
        q_matrix = put(q_matrix, two[rows_two:], 0, spot(3, e), 0)
    q_pre = nn(normed, q_matrix)
    mixed, q_rows, top = attend_forward(q_pre, kv_all, cosine, sine, row_ids, key_ids)
    o_matrix = blank((width, width))
    o_matrix = put(o_matrix, o_mine, 1, spot(0, 0), 0)
    o_matrix = put(o_matrix, o_rest, 1, spot(0, 1), 0)
    o_matrix = put(o_matrix, o_one, 1, spot(first, 0), 0)
    o_matrix = put(o_matrix, o_one_other, 1, spot(3 - first, 1), 0)

    (o_two, gu_one, mixed, q_rows, top, feeds, o_matrix, w_mine, w_rest, w_one, gu_mine) = fence(
        o_two, gu_one, mixed, q_rows, top, feeds, o_matrix, w_mine, w_rest, w_one, gu_mine
    )
    gu_two = to_near(jnp.concatenate([gu_mine, gu_one], 0), 1)
    o_two_other = to_core(o_two)
    gu_one_other = to_core(gu_one)
    w_one_other = to_core(w_one)
    rows_two = o_two.shape[0] // 2
    for e, two in ((0, o_two), (1, o_two_other)):
        far = 3 - first if e == 0 else first
        o_matrix = put(o_matrix, two[:rows_two], 1, spot(far, e), 0)
        o_matrix = put(o_matrix, two[rows_two:], 1, spot(3, e), 0)
    branch = nn(mixed, o_matrix)
    middle = inputs + keep * branch
    factor_two = norm_factor(middle)
    hidden_own = (middle * factor_two * gain_two).astype(bf16)
    hidden_own, o_matrix, gu_one_other, w_one_other, gu_one, w_one, gu_mine, g_rest, u_rest = fence(
        hidden_own, o_matrix, gu_one_other, w_one_other, gu_one, w_one, gu_mine, g_rest, u_rest
    )
    chunks = [hidden_own, to_cols(hidden_own, 1)]
    g_matrix, u_matrix = blank((width, units)), blank((width, units))
    g_matrix = put(g_matrix, gu_mine[:step], 0, spot(0, 0), 0)
    u_matrix = put(u_matrix, gu_mine[step:], 0, spot(0, 0), 0)
    g_matrix = put(g_matrix, g_rest, 0, spot(0, 1), 0)
    u_matrix = put(u_matrix, u_rest, 0, spot(0, 1), 0)
    for e, one in ((0, gu_one), (1, gu_one_other)):
        near = first if e == 0 else 3 - first
        g_matrix = put(g_matrix, one[:step], 0, spot(near, e), 0)
        u_matrix = put(u_matrix, one[step:], 0, spot(near, e), 0)
    d_matrix = blank((units, width))
    d_matrix = put(d_matrix, w_mine, 1, spot(0, 0), 0)
    d_matrix = put(d_matrix, w_rest, 1, spot(0, 1), 0)
    d_matrix = put(d_matrix, w_one, 1, spot(first, 0), 0)
    d_matrix = put(d_matrix, w_one_other, 1, spot(3 - first, 1), 0)

    gu_two, g_matrix, u_matrix, d_matrix, w_mine, w_one, chunks = fence(
        gu_two, g_matrix, u_matrix, d_matrix, w_mine, w_one, chunks
    )
    chunks = list(chunks)
    w_two = to_near(jnp.concatenate([w_mine, w_one], 0), 1)
    gu_two_other = to_core(gu_two)
    for e, two in ((0, gu_two), (1, gu_two_other)):
        far = 3 - first if e == 0 else first
        for n, at in enumerate((spot(far, e), spot(3, e))):
            piece = two[n * 2 * step : (n + 1) * 2 * step]
            g_matrix = put(g_matrix, piece[:step], 0, at, 0)
            u_matrix = put(u_matrix, piece[step:], 0, at, 0)
    chunks.append(to_cols(chunks[1], 1))

    def gate_up(hidden):
        gate, up = nn(hidden, g_matrix), nn(hidden, u_matrix)
        return gate, up

    near_hidden = jnp.concatenate([chunks[1], chunks[0]], 0)
    near_feed = jnp.concatenate([feeds[1], feeds[0]], 0)
    gate, up = gate_up(near_hidden)
    w_two, gate, up, d_matrix, arrived = fence(w_two, gate, up, d_matrix, chunks[2])
    chunks[2] = arrived
    chunks.append(to_cols(chunks[2], 1))
    w_two_other = to_core(w_two)
    rows_two = w_two.shape[0] // 2
    for e, two in ((0, w_two), (1, w_two_other)):
        far = 3 - first if e == 0 else first
        d_matrix = put(d_matrix, two[:rows_two], 1, spot(far, e), 0)
        d_matrix = put(d_matrix, two[rows_two:], 1, spot(3, e), 0)
    weights = (g_matrix, u_matrix)
    done = [feed_finish(near_feed, gate, up, d_matrix)]
    part = rows_product(done[0][1:], weights, True, bf16, 0, own)
    part, arrived = fence(part, chunks[3])
    chunks[3] = arrived
    for k in range(2, cols - 2):
        carry = to_cols(part, 1)
        chunks.append(to_cols(chunks[k + 1], 1))
        done.append(feed_through(chunks[k], feeds[k], g_matrix, u_matrix, d_matrix))
        part = rows_product(done[-1][1:], weights, True, f32)
        part, carry, arrived, done = fence(part, carry, chunks[k + 2], done)
        done = list(done)
        chunks[k + 2] = arrived
        part = (part + carry.astype(f32)).astype(bf16)
        (part,) = fence(part)
    k = cols - 2
    carry = to_cols(part, 1)
    far_hidden = jnp.concatenate(chunks[k:], 0)
    far_feed = jnp.concatenate(feeds[k:], 0)
    done.append(feed_through(after(far_hidden, part), far_feed, g_matrix, u_matrix, d_matrix))
    hids, gbs, ubs = ([x[n] for x in done] for n in range(3))
    h_parts = [near_hidden] + chunks[2:k] + [far_hidden]
    f_parts = [near_feed] + feeds[2:k] + [far_feed]
    low, high, full = (0, half), (half, half), (0, units)
    part = rows_product((gbs[-1], ubs[-1]), weights, True, f32, 0, own)
    d_sent = token_sum(hids, full, f_parts, high)
    part, carry, d_sent, hids, gbs, ubs, h_parts, f_parts = fence(
        part, carry, d_sent, hids, gbs, ubs, h_parts, f_parts
    )
    part = (part + carry.astype(f32)).astype(bf16)
    part, d_sent, hids, gbs, ubs = fence(part, d_sent, hids, gbs, ubs)

    carry = to_cols(part, 1)
    d_received = to_core(d_sent)
    part, own_part = rows_products(
        [((gbs[-1], ubs[-1]), 1), ((gbs[0], ubs[0]), 1)], weights, True, f32, own
    )
    g_sent, u_sent = token_sums(h_parts, high, [gbs, ubs], full)
    d_sum = token_sum(hids, full, f_parts, low, d_received)
    part, own_part, carry, d_sum, g_sent, u_sent, hids, gbs, ubs = fence(
        part, own_part, carry, d_sum, g_sent, u_sent, hids, gbs, ubs
    )
    part = (part + carry.astype(f32)).astype(bf16)
    part, own_part, d_sum, g_sent, u_sent, gbs, ubs, hids = fence(
        part, own_part, d_sum, g_sent, u_sent, gbs, ubs, hids
    )

    def prepare(total, axis):
        pieces = jnp.split(total, rows, axis)
        sent = jnp.concatenate([jnp.where(d == 0, pieces[1], pieces[2]), pieces[3]], axis)
        return pieces[0], jnp.where(d == 0, pieces[2], pieces[1]), sent

    def half_way(parts, near, axis):
        mine, theirs = jnp.split(near, 2, axis)
        return (parts[0], mine), (parts[1].astype(f32) + theirs.astype(f32)).astype(bf16)

    def finish(kept, far):
        return kept[0].astype(f32) + kept[1].astype(f32) + far.astype(f32)

    def around(carry, part):
        return to_cols((part.astype(f32) + carry.astype(f32)).astype(bf16), 1)

    def col_sum(total, axis):
        pieces = xor_blocks(jnp.split(total.astype(bf16), cols, axis), c)
        return [pieces[0]] + [to_xor_cols(pieces[k], k) for k in range(1, cols)]

    def added(values):
        return tree_sum([x.astype(f32) for x in values])

    carry = to_cols(part, 1)
    d_parts = prepare(d_sum, 1)
    d_near = to_near(d_parts[2], 0)
    g_received = to_core(g_sent)
    u_received = to_core(u_sent)
    outs = jnp.split(rows_product([hids[0]], [d_matrix], False, bf16), 2, 0)
    g_sum, u_sum = token_sums(h_parts, low, [gbs, ubs], full, [g_received, u_received])
    g_parts, u_parts = prepare(g_sum, 0), prepare(u_sum, 0)
    part, carry, d_near, g_parts, u_parts, hids, outs = fence(
        own_part, carry, d_near, g_parts, u_parts, hids, outs
    )

    out_carry = to_cols(outs[0], 1)
    out_last = outs[1]
    g_near = to_near(g_parts[2], 0)
    d_kept, d_theirs = half_way(d_parts, d_near, 1)
    d_far = to_near(d_theirs, 1)
    hidden_in_back = part + carry.astype(f32)
    from_norm, mlp_gain_part = norm_back(hidden_in_back, middle, factor_two, gain_two)
    middle_grad = upstream + from_norm
    branch_back = (keep * middle_grad).astype(bf16)
    mixed_back = rows_product([branch_back], [o_matrix], True, bf16)
    o_sent = token_sum([mixed], (0, width), [branch_back], high)
    outs = [None] + [rows_product([x], [d_matrix], False, bf16) for x in hids[1:-1]]
    outs += jnp.split(rows_product([hids[-1]], [d_matrix], False, bf16), 2, 0)
    mixed_back, branch_back, o_sent, d_far, g_near, outs, out_carry = fence(
        mixed_back, branch_back, o_sent, d_far, g_near, outs, out_carry
    )

    u_near = to_near(u_parts[2], 0)
    g_kept, g_theirs = half_way(g_parts, g_near, 0)
    g_far = to_near(g_theirs, 1)
    for k in range(1, cols - 2):
        out_carry = around(out_carry, outs[k])
    o_received = to_core(o_sent)
    dq, dk, dv = attend_backward(
        q_rows, kv_all, mixed_back, top, cosine, -sine, row_ids, key_ids
    )
    o_sum = token_sum([mixed], (0, width), [branch_back], low, o_received)
    o_low, o_high = jnp.split(o_sum, 2, 0)
    o_low = prepare(o_low, 1)
    dq, dk, dv, o_low, o_high, g_far, u_near, out_carry = fence(
        dq, dk, dv, o_low, o_high, g_far, u_near, out_carry
    )

    kv_turned = jnp.concatenate([dk, dv], 1)
    kv_back_pre = kv_turned[reach * own :]
    back_parts = []
    for k in range(1, reach + 1):
        piece = kv_turned[(reach - k) * own : (reach - k + 1) * own].astype(bf16)
        back_parts.append(along(piece, -k))
    u_kept, u_theirs = half_way(u_parts, u_near, 0)
    u_far = to_near(u_theirs, 1)
    o_low_near = to_near(o_low[2], 0)
    q_sent = token_sum([normed], high, [dq], (0, width))
    o_high = prepare(o_high, 1)
    back_parts, q_sent, u_far, o_low_near, o_high = fence(
        back_parts, q_sent, u_far, o_low_near, o_high
    )

    out_carry = around(out_carry, outs[cols - 2])
    o_low_kept, o_theirs = half_way(o_low, o_low_near, 1)
    o_low_far = to_near(o_theirs, 1)
    q_received = to_core(q_sent)
    for piece in back_parts:
        kv_back_pre = kv_back_pre + piece.astype(f32)
    kv_back = jnp.concatenate(
        [rotate(kv_back_pre[:, :kv_width], cosine, -sine), kv_back_pre[:, kv_width:]], 1
    ).astype(bf16)
    kv_sent = token_sum([normed], high, [kv_back], (0, 2 * kv_width))
    kv_received = to_core(kv_sent)
    kv_sum = token_sum([normed], low, [kv_back], (0, 2 * kv_width), kv_received)
    kv_parts = prepare(kv_sum, 0)
    kv_parts, kv_back, o_low_far, q_received, o_high = fence(
        kv_parts, kv_back, o_low_far, q_received, o_high
    )

    kv_near = to_near(kv_parts[2], 0)
    o_high_near = to_near(o_high[2], 0)
    normed_back = rows_product([dq, kv_back], [q_matrix, kv_matrix], True, f32)
    from_norm, attention_gain_part = norm_back(normed_back, inputs, factor_one, gain_one)
    input_grad = xor_order(middle_grad + from_norm, target, blocks, 1)
    gains = xor_order(jnp.stack([attention_gain_part, mlp_gain_part]), target, blocks, 1)
    q_sum = token_sum([normed], low, [dq], (0, width), q_received)
    kv_near, o_high_near, input_grad, gains, q_sum, out_carry = fence(
        kv_near, o_high_near, input_grad, gains, q_sum, out_carry
    )

    kv_kept, kv_theirs = half_way(kv_parts, kv_near, 0)
    kv_far = to_near(kv_theirs, 1)
    o_high_kept, o_theirs = half_way(o_high, o_high_near, 1)
    o_high_far = to_near(o_theirs, 1)
    hops = [1 << n for n in range(cols.bit_length() - 1)]
    gains = gains + to_xor_cols(gains, hops[0])
    q_parts = prepare(q_sum, 0)
    kv_far, o_high_far, gains, q_parts = fence(kv_far, o_high_far, gains, q_parts)

    q_near = to_near(q_parts[2], 0)
    kv_sum = finish(kv_kept, kv_far).astype(bf16)
    total = [kv_sum] + [to_xor_cols(kv_sum, k) for k in range(1, cols)]
    for hop in hops[1:]:
        gains = gains + to_xor_cols(gains, hop)
    out_sum = jnp.concatenate(
        [finish(o_low_kept, o_low_far), finish(o_high_kept, o_high_far)], 0
    ).astype(bf16)
    total, q_near, gains, out_sum = fence(total, q_near, gains, out_sum)

    total = added(total).astype(bf16)
    one = to_near(total, 0)
    q_kept, q_theirs = half_way(q_parts, q_near, 0)
    q_far = to_near(q_theirs, 1)
    out_parts = col_sum(out_sum, 0)
    one, d_far, g_far, u_far, out_carry = fence(one, d_far, g_far, u_far, out_carry)
    down_grad, gate_grad, up_grad = finish(d_kept, d_far), finish(g_kept, g_far), finish(u_kept, u_far)
    piece = out_last.astype(f32) + out_carry.astype(f32)
    output = xor_order((middle + keep * piece).astype(bf16), target, blocks, 1)
    one, q_far, out_parts, output, gains, down_grad, gate_grad, up_grad = fence(
        one, q_far, out_parts, output, gains, down_grad, gate_grad, up_grad
    )

    two = to_near(jnp.concatenate([total, one], 0), 1)
    gains = gains + to_near(gains, 0)
    gains = gains + to_near(gains, 1)
    q_cols = col_sum(finish(q_kept, q_far), 1)
    out_grad = added(out_parts)
    two, q_cols, out_grad, gains = fence(two, q_cols, out_grad, gains)
    mine = jnp.concatenate([total, one, two], 0)
    theirs = to_core(mine)
    gains = gains + to_core(gains)
    query_grad = added(q_cols)
    found = blank((width, 2 * kv_width))
    for e, part in enumerate((mine, theirs)):
        near, far = (first, 3 - first) if e == 0 else (3 - first, first)
        for n, j in enumerate((0, near, far, 3)):
            at = ((d ^ e) * rows + (r ^ j)) * step
            found = put(found, part[n * step : (n + 1) * step], 0, at, 0)
    found = found.astype(f32)
    key_grad, value_grad = found[:, :kv_width], found[:, kv_width:]
    return (
        output,
        input_grad,
        gains[0],
        gains[1],
        query_grad,
        key_grad,
        value_grad,
        out_grad,
        gate_grad,
        up_grad,
        down_grad,
    )


def solution(mesh):
    return jax.shard_map(
        local,
        mesh=mesh,
        in_specs=(
            P(("dp", "rows", "cols"), None),
            P(),
            P(),
            P("rows", "cols"),
            P("rows", None),
            P("rows", None),
            P(None, "rows"),
            P("rows", "cols"),
            P("rows", "cols"),
            P("cols", "rows"),
            P(("dp", "rows"), None),
            P(("dp", "rows")),
            P(("dp", "rows", "cols"), None),
        ),
        out_specs=(
            P(("dp", "rows", "cols"), None),
            P(("dp", "rows", "cols"), None),
            P(),
            P(),
            P(("dp", "rows"), "cols"),
            P(),
            P(),
            P("cols", ("dp", "rows")),
            P(("dp", "rows"), "cols"),
            P(("dp", "rows"), "cols"),
            P("cols", ("dp", "rows")),
        ),
        check_vma=False,
    )
```

```python
import jax
import jax.numpy as jnp
from jax import lax
from jax.experimental import pallas as pl
from jax.experimental.pallas import tpu as pltpu
from jax.sharding import PartitionSpec as P

HEADS = 16
KV_HEADS = 2
HEAD_DIM = 128

epsilon = 1e-05
negative = -1e30
rope_base = 10000.0
log2e = 1.4426950408889634
bf16 = jnp.bfloat16
f32 = jnp.float32


def dot(left, right, dims):
    return lax.dot_general(left, right, ((dims[:1], dims[1:]), ((), ())), preferred_element_type=f32)


def turn(values, cosine, sine):
    return values * cosine + pltpu.roll(values, HEAD_DIM // 2, 1) * sine


def mask_bias(row_ids, key_ids):
    span, own = key_ids.shape[0], row_ids.shape[1]
    key_place = lax.broadcasted_iota(jnp.int32, (span, own), 0)
    row_place = lax.broadcasted_iota(jnp.int32, (span, own), 1) + (span - own)
    return jnp.where((key_ids == row_ids) & (row_place >= key_place), 0.0, negative)


PER = 4


def forward_kernel(pre_ref, k_ref, v_ref, cos_ref, sin_ref, rid_ref, kid_ref, mixed_ref, q_ref, top_ref, bias_ref, vt_ref):
    head = pl.program_id(0) * PER

    @pl.when(head == 0)
    def _():
        bias_ref[...] = mask_bias(rid_ref[...], kid_ref[...])

    @pl.when(head % (HEADS // KV_HEADS) == 0)
    def _():
        vt_ref[...] = v_ref[...].astype(f32).T.astype(bf16)

    for n in range(PER):
        lanes = slice(n * HEAD_DIM, (n + 1) * HEAD_DIM)
        q = turn(pre_ref[:, lanes], cos_ref[...], sin_ref[...]).astype(bf16)
        q_ref[:, lanes] = q
        scores = dot(k_ref[...], q, (1, 1)) * (HEAD_DIM ** (-0.5) * log2e) + bias_ref[...]
        top = jnp.max(scores, axis=0, keepdims=True)
        exponent = jnp.exp2(scores - top)
        total = jnp.sum(exponent, axis=0, keepdims=True)
        mixed = dot(vt_ref[...], exponent.astype(bf16), (1, 0)) * (1.0 / total)
        mixed_ref[:, lanes] = mixed.T.astype(bf16)
        top_ref[n] = top + jnp.log2(total)


def attend_forward(pre, kv_all, cosine, sine, row_ids, key_ids):
    own, width = pre.shape
    span = kv_all.shape[0]
    share = HEADS // KV_HEADS
    whole = lambda shape: pl.BlockSpec(shape, lambda h: (0, 0))
    head = pl.BlockSpec((own, PER * HEAD_DIM), lambda h: (0, h))
    return pl.pallas_call(
        forward_kernel,
        grid=(HEADS // PER,),
        in_specs=[
            head,
            pl.BlockSpec((span, HEAD_DIM), lambda h: (0, h * PER // share)),
            pl.BlockSpec((span, HEAD_DIM), lambda h: (0, KV_HEADS + h * PER // share)),
            whole((own, HEAD_DIM)),
            whole((own, HEAD_DIM)),
            whole((1, own)),
            whole((span, 1)),
        ],
        out_specs=[head, head, pl.BlockSpec((PER, 1, own), lambda h: (h, 0, 0))],
        out_shape=[
            jax.ShapeDtypeStruct((own, width), bf16),
            jax.ShapeDtypeStruct((own, width), bf16),
            jax.ShapeDtypeStruct((HEADS, 1, own), f32),
        ],
        scratch_shapes=[pltpu.VMEM((span, own), f32), pltpu.VMEM((HEAD_DIM, span), bf16)],
        compiler_params=pltpu.CompilerParams(dimension_semantics=("arbitrary",), vmem_limit_bytes=32 << 20),
        cost_estimate=pl.CostEstimate(flops=0, transcendentals=0, bytes_accessed=0),
    )(pre, kv_all, kv_all, cosine, sine, row_ids[None, :], key_ids[:, None])


def backward_kernel(q_ref, k_ref, v_ref, back_ref, top_ref, cos_ref, sin_ref, rid_ref, kid_ref, dq_ref, dk_ref, dv_ref, bias_ref, kt_ref):
    step = pl.program_id(0)

    @pl.when(step == 0)
    def _():
        bias_ref[...] = mask_bias(rid_ref[...], kid_ref[...])

    @pl.when(step % (HEADS // KV_HEADS // PER) == 0)
    def _():
        kt_ref[...] = k_ref[...].astype(f32).T.astype(bf16)
        dk_ref[...] = jnp.zeros_like(dk_ref)
        dv_ref[...] = jnp.zeros_like(dv_ref)

    scale = HEAD_DIM ** (-0.5)
    for n in range(PER):
        lanes = slice(n * HEAD_DIM, (n + 1) * HEAD_DIM)
        q = q_ref[:, lanes]
        back = back_ref[:, lanes]
        scores = dot(k_ref[...], q, (1, 1)) * (scale * log2e) + bias_ref[...]
        probs = jnp.exp2(scores - top_ref[n])
        dv_ref[...] += dot(probs.astype(bf16), back, (1, 0))
        weight_back = dot(v_ref[...], back, (1, 1))
        inner = jnp.sum(weight_back * probs, axis=0, keepdims=True)
        score_back = (probs * (weight_back - inner)).astype(bf16)
        dk_ref[...] += dot(score_back, q, (1, 0)) * scale
        turned = (dot(kt_ref[...], score_back, (1, 0)) * scale).T
        dq_ref[:, lanes] = turn(turned, cos_ref[...], sin_ref[...]).astype(bf16)


def attend_backward(q_rows, kv_all, mixed_back, top, cosine, sine, row_ids, key_ids):
    own, width = q_rows.shape
    span = kv_all.shape[0]
    steps = HEADS // KV_HEADS // PER
    whole = lambda shape: pl.BlockSpec(shape, lambda h: (0, 0))
    head = pl.BlockSpec((own, PER * HEAD_DIM), lambda h: (0, h))
    shared = pl.BlockSpec((span, HEAD_DIM), lambda h: (0, h // steps))
    return pl.pallas_call(
        backward_kernel,
        grid=(HEADS // PER,),
        in_specs=[
            head,
            shared,
            pl.BlockSpec((span, HEAD_DIM), lambda h: (0, KV_HEADS + h // steps)),
            head,
            pl.BlockSpec((PER, 1, own), lambda h: (h, 0, 0)),
            whole((own, HEAD_DIM)),
            whole((own, HEAD_DIM)),
            whole((1, own)),
            whole((span, 1)),
        ],
        out_specs=[head, shared, shared],
        out_shape=[
            jax.ShapeDtypeStruct((own, width), bf16),
            jax.ShapeDtypeStruct((span, KV_HEADS * HEAD_DIM), f32),
            jax.ShapeDtypeStruct((span, KV_HEADS * HEAD_DIM), f32),
        ],
        scratch_shapes=[pltpu.VMEM((span, own), f32), pltpu.VMEM((HEAD_DIM, span), bf16)],
        compiler_params=pltpu.CompilerParams(dimension_semantics=("arbitrary",), vmem_limit_bytes=32 << 20),
        cost_estimate=pl.CostEstimate(flops=0, transcendentals=0, bytes_accessed=0),
    )(q_rows, kv_all, kv_all, mixed_back, top, cosine, sine, row_ids[None, :], key_ids[:, None])


FREE = pl.CostEstimate(flops=0, transcendentals=0, bytes_accessed=0)


def call(kernel, grid, in_specs, out_specs, out_shape, scratch=()):
    return pl.pallas_call(
        kernel,
        grid=grid,
        in_specs=in_specs,
        out_specs=out_specs,
        out_shape=out_shape,
        scratch_shapes=list(scratch),
        compiler_params=pltpu.CompilerParams(
            dimension_semantics=("arbitrary",) * len(grid), vmem_limit_bytes=48 << 20
        ),
        cost_estimate=FREE,
    )


def fixed(shape):
    return pl.BlockSpec(shape, lambda i: (0,) * len(shape))


def through_kernel(h_ref, f_ref, g_ref, u_ref, d_ref, hid_ref, gb_ref, ub_ref):
    gate = dot(h_ref[...], g_ref[...], (1, 0))
    up = dot(h_ref[...], u_ref[...], (1, 0))
    back = dot(f_ref[...], d_ref[...], (1, 1))
    s = jax.nn.sigmoid(gate)
    swish = gate * s
    hid_ref[...] = (swish * up).astype(bf16)
    ub_ref[...] = (back * swish).astype(bf16)
    gb_ref[...] = (back * up * s * (1.0 + gate * (1.0 - s))).astype(bf16)


def feed_through(hidden, feed, g_matrix, u_matrix, d_matrix):
    count, width = hidden.shape
    units = g_matrix.shape[1]
    tile = min(256, units)
    across = pl.BlockSpec((width, tile), lambda i: (0, i))
    out = pl.BlockSpec((count, tile), lambda i: (0, i))
    return call(
        through_kernel,
        (pl.cdiv(units, tile),),
        [fixed((count, width))] * 2 + [across, across, pl.BlockSpec((tile, width), lambda i: (i, 0))],
        [out] * 3,
        [jax.ShapeDtypeStruct((count, units), bf16)] * 3,
    )(hidden, feed, g_matrix, u_matrix, d_matrix)


def finish_kernel(f_ref, gate_ref, up_ref, d_ref, hid_ref, gb_ref, ub_ref):
    gate = gate_ref[...]
    back = dot(f_ref[...], d_ref[...], (1, 1))
    s = jax.nn.sigmoid(gate)
    swish = gate * s
    hid_ref[...] = (swish * up_ref[...]).astype(bf16)
    ub_ref[...] = (back * swish).astype(bf16)
    gb_ref[...] = (back * up_ref[...] * s * (1.0 + gate * (1.0 - s))).astype(bf16)


def feed_finish(feed, gate, up, d_matrix):
    count, units = gate.shape
    width = feed.shape[1]
    tile = min(256, units)
    out = pl.BlockSpec((count, tile), lambda i: (0, i))
    return call(
        finish_kernel,
        (pl.cdiv(units, tile),),
        [fixed((count, width)), out, out, pl.BlockSpec((tile, width), lambda i: (i, 0))],
        [out] * 3,
        [jax.ShapeDtypeStruct((count, units), bf16)] * 3,
    )(feed, gate, up, d_matrix)


def rows_products(sets, rights, turned, dtype, count):
    n, many = len(rights), len(sets)
    columns = rights[0].shape[0 if turned else 1]
    tile = min(512, columns)

    def kernel(*refs):
        for m in range(many):
            total = 0.0
            for k in range(n):
                total = total + dot(refs[n + n * m + k][...], refs[k][...], (1, 1 if turned else 0))
            refs[m - many][...] = total.astype(dtype)

    specs = []
    for x in rights:
        if turned:
            specs.append(pl.BlockSpec((tile, x.shape[1]), lambda i: (i, 0)))
        else:
            specs.append(pl.BlockSpec((x.shape[0], tile), lambda i: (0, i)))
    operands = list(rights)
    for lefts, block in sets:
        specs += [pl.BlockSpec((count, x.shape[1]), lambda i, block=block: (block, 0)) for x in lefts]
        operands += list(lefts)
    return call(
        kernel,
        (columns // tile,),
        specs,
        [pl.BlockSpec((count, tile), lambda i: (0, i))] * many,
        [jax.ShapeDtypeStruct((count, columns), dtype)] * many,
    )(*operands)


def rows_product(lefts, rights, turned, dtype, block=0, count=None):
    count = lefts[0].shape[0] if count is None else count
    return rows_products([(lefts, block)], rights, turned, dtype, count)[0]


def token_sums(lefts, left_lanes, rights, right_lanes, received=None):
    n, many = len(lefts), len(rights)
    start, rows_out = left_lanes
    tile = min(256, rows_out)
    base, columns = right_lanes

    def kernel(*refs):
        for k in range(n):
            left = refs[k][...]
            for m in range(many):
                part = dot(left, refs[n * (m + 1) + k][...], (0, 0))
                totals = [part] * many if k == 0 and m == 0 else totals
                totals[m] = part if k == 0 else totals[m] + part
        for m in range(many):
            total = totals[m]
            if received is not None:
                total = total + refs[n * (many + 1) + m][...].astype(f32)
            refs[m - many][...] = total.astype(bf16)

    first, second = start // tile, base // columns
    specs = [pl.BlockSpec((x.shape[0], tile), lambda i: (0, first + i)) for x in lefts]
    operands = list(lefts)
    for group in rights:
        specs += [pl.BlockSpec((x.shape[0], columns), lambda i: (0, second)) for x in group]
        operands += list(group)
    out = pl.BlockSpec((tile, columns), lambda i: (i, 0))
    if received is not None:
        specs += [out] * many
        operands += list(received)
    return call(
        kernel,
        (pl.cdiv(rows_out, tile),),
        specs,
        [out] * many,
        [jax.ShapeDtypeStruct((rows_out, columns), bf16)] * many,
    )(*operands)


def token_sum(lefts, left_lanes, rights, right_lanes, received=None):
    received = None if received is None else [received]
    return token_sums(lefts, left_lanes, [rights], right_lanes, received)[0]


def nn(left, right):
    return dot(left, right, (1, 0))


def nt(left, right):
    return dot(left, right, (1, 1))


def tn(left, right):
    return dot(left, right, (0, 0))


def after(value, *earlier):
    return lax.optimization_barrier((value,) + earlier)[0]


def fence(*values):
    return lax.optimization_barrier(values)


def blank(shape):
    return pl.pallas_call(
        lambda out: None,
        out_specs=pl.BlockSpec(memory_space=pl.ANY),
        out_shape=jax.ShapeDtypeStruct(shape, bf16),
    )()


def xor_blocks(blocks, index):
    bit = 1
    while bit < len(blocks):
        swap = (index & bit) != 0
        blocks = [jnp.where(swap, blocks[j ^ bit], blocks[j]) for j in range(len(blocks))]
        bit *= 2
    return blocks


def xor_order(value, index, count, axis):
    return jnp.concatenate(xor_blocks(jnp.split(value, count, axis), index), axis)


def tree_sum(values):
    while len(values) > 1:
        values = [values[i] + values[i + 1] for i in range(0, len(values), 2)]
    return values[0]


def rotary_tables(positions):
    half = HEAD_DIM // 2
    frequency = rope_base ** (-2.0 * jnp.arange(half, dtype=f32) / HEAD_DIM)
    angles = positions.astype(f32)[:, None] * frequency[None, :]
    cosine, sine = jnp.cos(angles), jnp.sin(angles)
    return jnp.concatenate([cosine, cosine], 1), jnp.concatenate([-sine, sine], 1)


def rotate(values, cosine, sine):
    heads = jnp.split(values, values.shape[1] // HEAD_DIM, 1)
    half = HEAD_DIM // 2
    swapped = [jnp.concatenate([h[:, half:], h[:, :half]], 1) for h in heads]
    return jnp.concatenate([h * cosine + s * sine for h, s in zip(heads, swapped)], 1)


def norm_factor(values):
    return lax.rsqrt(jnp.mean(values * values, axis=-1, keepdims=True) + epsilon)


def norm_back(grad, values, factor, gain):
    y = grad * gain
    pulled = factor * y - values * factor**3 * jnp.mean(y * values, axis=-1, keepdims=True)
    return pulled, jnp.sum(grad * values * factor, axis=0)


def local(
    tokens,
    attention_gain,
    mlp_gain,
    w_query,
    w_key,
    w_value,
    w_out,
    w_gate,
    w_up,
    w_down,
    segment_ids,
    skip_mask,
    cotangent,
):
    cols, rows = lax.axis_size("cols"), lax.axis_size("rows")
    c, r, d = lax.axis_index("cols"), lax.axis_index("rows"), lax.axis_index("dp")
    own, width = tokens.shape
    half = width // 2
    sequences, length = segment_ids.shape
    blocks = 2 * rows
    step = width // blocks
    target = d * rows + r
    kv_width = KV_HEADS * HEAD_DIM

    def to_rows(value, a):
        return lax.ppermute(value, "rows", [(i, i ^ a) for i in range(rows)])

    def to_near(value, turn):
        pairs = []
        for core in range(2):
            a = 1 + (core ^ turn)
            pairs += [(core * rows + i, core * rows + (i ^ a)) for i in range(rows)]
        return lax.ppermute(value, ("dp", "rows"), pairs)

    first = 1 + d

    def to_core(value):
        return lax.ppermute(value, "dp", [(0, 1), (1, 0)])

    def to_cols(value, k):
        return lax.ppermute(value, "cols", [(i, (i + k) % cols) for i in range(cols)])

    def along(value, k):
        return lax.ppermute(
            value, "cols", [(i, i + k) for i in range(cols) if 0 <= i + k < cols]
        )

    def to_xor_cols(value, k):
        return lax.ppermute(value, "cols", [(i, i ^ k) for i in range(cols)])

    def spot(j, e):
        return ((2 * (r ^ j) + (d ^ e)) ^ target) * step

    def put(full, piece, axis, start, offset):
        at = (start + offset, 0) if axis == 0 else (offset, start)
        return lax.dynamic_update_slice(full, piece, at)

    def fill(full, axis, one, two, e):
        near, far = (first, 3 - first) if e == 0 else (3 - first, first)
        size = two.shape[0] // 2
        full = put(full, one, axis, spot(near, e), 0)
        full = put(full, two[:size], axis, spot(far, e), 0)
        return put(full, two[size:], axis, spot(3, e), 0)

    def halves(weight, axis):
        low, high = jnp.split(weight, 2, axis)
        return jnp.where(d == 0, low, high), jnp.where(d == 0, high, low)

    sequence = (c * own) // length
    start = (c * own) % length
    reach = min(-(-(length // 2 - 1) // own), length // own - 1)
    span = (reach + 1) * own
    units = w_gate.shape[1]

    kv_mine, kv_rest = halves(jnp.concatenate([w_key, w_value], 1), 0)
    q_mine, _ = halves(w_query, 0)
    kv_one = to_near(kv_mine, 0)
    q_parts = [q_mine] + [to_xor_cols(q_mine, k) for k in range(1, cols)]
    kv_one, tokens, attention_gain, mlp_gain, w_out, segment_ids, skip_mask, cotangent = fence(
        kv_one, tokens, attention_gain, mlp_gain, w_out, segment_ids, skip_mask, cotangent
    )
    kv_two = to_near(jnp.concatenate([kv_mine, kv_one], 0), 1)
    o_mine, o_rest = halves(w_out, 1)
    o_one = to_near(o_mine, 0)
    inputs = xor_order(tokens, target, blocks, 1).astype(f32)
    gain_one = xor_order(attention_gain, target, blocks, 0)
    gain_two = xor_order(mlp_gain, target, blocks, 0)
    factor_one = norm_factor(inputs)
    normed = (inputs * factor_one * gain_one).astype(bf16)
    cosine, sine = rotary_tables(start + jnp.arange(own))
    keep = (1 - lax.dynamic_index_in_dim(skip_mask, sequence, 0, False)).astype(f32)
    upstream = xor_order(cotangent, target, blocks, 1)
    feed_own = (keep * upstream).astype(bf16)

    (kv_two, q_parts, normed, cosine, sine, feed_own, upstream, w_down, w_gate, w_up) = fence(
        kv_two, q_parts, normed, cosine, sine, feed_own, upstream, w_down, w_gate, w_up
    )
    feeds = [feed_own, to_cols(feed_own, 1)]
    q_mine = jnp.concatenate(xor_blocks(q_parts, c), 1)
    q_one = to_near(q_mine, 0)
    kv_other = (to_core(kv_one), to_core(kv_two))
    q_own_other = to_core(q_mine)
    q_one, q_own_other, kv_other, w_down, o_one = fence(
        q_one, q_own_other, kv_other, w_down, o_one
    )
    q_sent = jnp.concatenate([q_mine, q_one], 0)
    q_two = to_near(q_sent, 1)
    kv_mine, kv_rest, kv_one, kv_two, kv_other, _ = fence(
        kv_mine, kv_rest, kv_one, kv_two, kv_other, q_sent
    )
    kv_matrix = blank((width, 2 * kv_width))
    kv_matrix = put(kv_matrix, kv_mine, 0, spot(0, 0), 0)
    kv_matrix = put(kv_matrix, kv_rest, 0, spot(0, 1), 0)
    kv_matrix = fill(kv_matrix, 0, kv_one, kv_two, 0)
    kv_matrix = fill(kv_matrix, 0, *kv_other, 1)
    kv_pre = nn(normed, kv_matrix)
    kv_own = jnp.concatenate(
        [rotate(kv_pre[:, :kv_width], cosine, sine), kv_pre[:, kv_width:]], 1
    ).astype(bf16)

    kv_own, feeds[1] = fence(kv_own, feeds[1])
    kv_before = [along(kv_own, k) for k in range(reach, 0, -1)]
    for k in range(2, cols - 1):
        feeds.append(to_cols(feeds[-1], 1))
    q_one_other = to_core(q_one)
    q_matrix = blank((width, width))
    q_matrix = put(q_matrix, q_mine, 0, spot(0, 0), 0)
    q_matrix = put(q_matrix, q_own_other, 0, spot(0, 1), 0)
    q_matrix = put(q_matrix, q_one, 0, spot(first, 0), 0)
    q_matrix = put(q_matrix, q_one_other, 0, spot(3 - first, 1), 0)
    ids = lax.dynamic_index_in_dim(segment_ids, sequence, 0, False)
    ids_padded = jnp.concatenate([jnp.full((reach * own,), -1, ids.dtype), ids])
    key_ids = lax.dynamic_slice_in_dim(ids_padded, start, span, 0)
    row_ids = key_ids[reach * own :]

    (q_two, q_matrix, o_mine, o_rest, o_one, w_gate, w_up, w_down) = fence(
        q_two, q_matrix, o_mine, o_rest, o_one, w_gate, w_up, w_down
    )

    o_two = to_near(jnp.concatenate([o_mine, o_one], 0), 1)
    q_two_other = to_core(q_two)
    g_mine, g_rest = halves(w_gate, 0)
    u_mine, u_rest = halves(w_up, 0)
    gu_mine = jnp.concatenate([g_mine, u_mine], 0)
    gu_one = to_near(gu_mine, 0)
    w_mine, w_rest = halves(w_down, 1)
    o_one_other = to_core(o_one)
    kv_all = jnp.concatenate(list(kv_before) + [kv_own], 0)
    rows_two = q_two.shape[0] // 2
    for e, two in ((0, q_two), (1, q_two_other)):
        far = 3 - first if e == 0 else first
        q_matrix = put(q_matrix, two[:rows_two], 0, spot(far, e), 0)
        q_matrix = put(q_matrix, two[rows_two:], 0, spot(3, e), 0)
    q_pre = nn(normed, q_matrix)
    feeds.append(to_cols(after(feeds[-1], q_pre), 1))
    mixed, q_rows, top = attend_forward(q_pre, kv_all, cosine, sine, row_ids, key_ids)
    o_matrix = blank((width, width))
    o_matrix = put(o_matrix, o_mine, 1, spot(0, 0), 0)
    o_matrix = put(o_matrix, o_rest, 1, spot(0, 1), 0)
    o_matrix = put(o_matrix, o_one, 1, spot(first, 0), 0)
    o_matrix = put(o_matrix, o_one_other, 1, spot(3 - first, 1), 0)

    (o_two, gu_one, mixed, q_rows, top, o_matrix, w_mine, w_rest, gu_mine, feeds) = fence(
        o_two, gu_one, mixed, q_rows, top, o_matrix, w_mine, w_rest, gu_mine, feeds
    )
    gu_two = to_near(jnp.concatenate([gu_mine, gu_one], 0), 1)
    o_two_other = to_core(o_two)
    gu_one_other = to_core(gu_one)
    w_one = to_near(w_mine, 0)
    rows_two = o_two.shape[0] // 2
    for e, two in ((0, o_two), (1, o_two_other)):
        far = 3 - first if e == 0 else first
        o_matrix = put(o_matrix, two[:rows_two], 1, spot(far, e), 0)
        o_matrix = put(o_matrix, two[rows_two:], 1, spot(3, e), 0)
    branch = nn(mixed, o_matrix)
    middle = inputs + keep * branch
    factor_two = norm_factor(middle)
    hidden_own = (middle * factor_two * gain_two).astype(bf16)
    hidden_own, o_matrix, gu_one_other, gu_one, gu_mine, g_rest, u_rest = fence(
        hidden_own, o_matrix, gu_one_other, gu_one, gu_mine, g_rest, u_rest
    )
    chunks = [hidden_own, to_cols(hidden_own, 1)]
    g_matrix, u_matrix = blank((width, units)), blank((width, units))
    g_matrix = put(g_matrix, gu_mine[:step], 0, spot(0, 0), 0)
    u_matrix = put(u_matrix, gu_mine[step:], 0, spot(0, 0), 0)
    g_matrix = put(g_matrix, g_rest, 0, spot(0, 1), 0)
    u_matrix = put(u_matrix, u_rest, 0, spot(0, 1), 0)
    for e, one in ((0, gu_one), (1, gu_one_other)):
        near = first if e == 0 else 3 - first
        g_matrix = put(g_matrix, one[:step], 0, spot(near, e), 0)
        u_matrix = put(u_matrix, one[step:], 0, spot(near, e), 0)
    d_matrix = blank((units, width))
    d_matrix = put(d_matrix, w_mine, 1, spot(0, 0), 0)
    d_matrix = put(d_matrix, w_rest, 1, spot(0, 1), 0)

    gu_two, g_matrix, u_matrix, d_matrix, w_mine, w_one, chunks = fence(
        gu_two, g_matrix, u_matrix, d_matrix, w_mine, w_one, chunks
    )
    chunks = list(chunks)
    w_two = to_near(jnp.concatenate([w_mine, w_one], 0), 1)
    gu_two_other = to_core(gu_two)
    w_one_other = to_core(w_one)
    d_matrix = put(d_matrix, w_one, 1, spot(first, 0), 0)
    d_matrix = put(d_matrix, w_one_other, 1, spot(3 - first, 1), 0)
    for e, two in ((0, gu_two), (1, gu_two_other)):
        far = 3 - first if e == 0 else first
        for n, at in enumerate((spot(far, e), spot(3, e))):
            piece = two[n * 2 * step : (n + 1) * 2 * step]
            g_matrix = put(g_matrix, piece[:step], 0, at, 0)
            u_matrix = put(u_matrix, piece[step:], 0, at, 0)
    chunks.append(to_cols(chunks[1], 1))

    def gate_up(hidden):
        gate, up = nn(hidden, g_matrix), nn(hidden, u_matrix)
        return gate, up

    near_hidden = jnp.concatenate([chunks[1], chunks[0]], 0)
    near_feed = jnp.concatenate([feeds[1], feeds[0]], 0)
    gate, up = gate_up(near_hidden)
    w_two, gate, up, d_matrix, arrived = fence(w_two, gate, up, d_matrix, chunks[2])
    chunks[2] = arrived
    chunks.append(to_cols(chunks[2], 1))
    w_two_other = to_core(w_two)
    rows_two = w_two.shape[0] // 2
    for e, two in ((0, w_two), (1, w_two_other)):
        far = 3 - first if e == 0 else first
        d_matrix = put(d_matrix, two[:rows_two], 1, spot(far, e), 0)
        d_matrix = put(d_matrix, two[rows_two:], 1, spot(3, e), 0)
    weights = (g_matrix, u_matrix)
    done = [feed_finish(near_feed, gate, up, d_matrix)]
    part = rows_product(done[0][1:], weights, True, bf16, 0, own)
    part, arrived = fence(part, chunks[3])
    chunks[3] = arrived
    for k in range(2, cols - 2):
        carry = to_cols(part, 1)
        chunks.append(to_cols(chunks[k + 1], 1))
        done.append(feed_through(chunks[k], feeds[k], g_matrix, u_matrix, d_matrix))
        part = rows_product(done[-1][1:], weights, True, f32)
        part, carry, arrived, done = fence(part, carry, chunks[k + 2], done)
        done = list(done)
        chunks[k + 2] = arrived
        part = (part + carry.astype(f32)).astype(bf16)
        (part,) = fence(part)
    k = cols - 2
    carry = to_cols(part, 1)
    far_hidden = jnp.concatenate(chunks[k:], 0)
    far_feed = jnp.concatenate(feeds[k:], 0)
    done.append(feed_through(after(far_hidden, part), far_feed, g_matrix, u_matrix, d_matrix))
    hids, gbs, ubs = ([x[n] for x in done] for n in range(3))
    h_parts = [near_hidden] + chunks[2:k] + [far_hidden]
    f_parts = [near_feed] + feeds[2:k] + [far_feed]
    low, high, full = (0, half), (half, half), (0, units)
    part = rows_product((gbs[-1], ubs[-1]), weights, True, f32, 0, own)
    d_sent = token_sum(hids, full, f_parts, high)
    part, carry, d_sent, hids, gbs, ubs, h_parts, f_parts = fence(
        part, carry, d_sent, hids, gbs, ubs, h_parts, f_parts
    )
    part = (part + carry.astype(f32)).astype(bf16)
    part, d_sent, hids, gbs, ubs = fence(part, d_sent, hids, gbs, ubs)

    carry = to_cols(part, 1)
    d_received = to_core(d_sent)
    part, own_part = rows_products(
        [((gbs[-1], ubs[-1]), 1), ((gbs[0], ubs[0]), 1)], weights, True, f32, own
    )
    g_sent, u_sent = token_sums(h_parts, high, [gbs, ubs], full)
    d_sum = token_sum(hids, full, f_parts, low, d_received)
    part, own_part, carry, d_sum, g_sent, u_sent, hids, gbs, ubs = fence(
        part, own_part, carry, d_sum, g_sent, u_sent, hids, gbs, ubs
    )
    part = (part + carry.astype(f32)).astype(bf16)
    part, own_part, d_sum, g_sent, u_sent, gbs, ubs, hids = fence(
        part, own_part, d_sum, g_sent, u_sent, gbs, ubs, hids
    )

    def prepare(total, axis):
        pieces = jnp.split(total, rows, axis)
        sent = jnp.concatenate([jnp.where(d == 0, pieces[1], pieces[2]), pieces[3]], axis)
        return pieces[0], jnp.where(d == 0, pieces[2], pieces[1]), sent

    def half_way(parts, near, axis):
        mine, theirs = jnp.split(near, 2, axis)
        return (parts[0], mine), (parts[1].astype(f32) + theirs.astype(f32)).astype(bf16)

    def finish(kept, far):
        return kept[0].astype(f32) + kept[1].astype(f32) + far.astype(f32)

    def around(carry, part):
        return to_cols((part.astype(f32) + carry.astype(f32)).astype(bf16), 1)

    def col_sum(total, axis):
        pieces = xor_blocks(jnp.split(total.astype(bf16), cols, axis), c)
        return [pieces[0]] + [to_xor_cols(pieces[k], k) for k in range(1, cols)]

    def added(values):
        return tree_sum([x.astype(f32) for x in values])

    carry = to_cols(part, 1)
    d_parts = prepare(d_sum, 1)
    d_near = to_near(d_parts[2], 0)
    g_received = to_core(g_sent)
    u_received = to_core(u_sent)
    outs = jnp.split(rows_product([hids[0]], [d_matrix], False, bf16), 2, 0)
    g_sum, u_sum = token_sums(h_parts, low, [gbs, ubs], full, [g_received, u_received])
    g_parts, u_parts = prepare(g_sum, 0), prepare(u_sum, 0)
    part, carry, d_near, g_parts, u_parts, hids, outs = fence(
        own_part, carry, d_near, g_parts, u_parts, hids, outs
    )

    out_carry = to_cols(outs[0], 1)
    out_last = outs[1]
    g_near = to_near(g_parts[2], 0)
    d_kept, d_theirs = half_way(d_parts, d_near, 1)
    d_far = to_near(d_theirs, 1)
    hidden_in_back = part + carry.astype(f32)
    from_norm, mlp_gain_part = norm_back(hidden_in_back, middle, factor_two, gain_two)
    middle_grad = upstream + from_norm
    branch_back = (keep * middle_grad).astype(bf16)
    mixed_back = rows_product([branch_back], [o_matrix], True, bf16)
    o_sent = token_sum([mixed], (0, width), [branch_back], high)
    outs = [None] + [rows_product([x], [d_matrix], False, bf16) for x in hids[1:-1]]
    outs += jnp.split(rows_product([hids[-1]], [d_matrix], False, bf16), 2, 0)
    mixed_back, branch_back, o_sent, d_far, g_near, outs, out_carry = fence(
        mixed_back, branch_back, o_sent, d_far, g_near, outs, out_carry
    )

    u_near = to_near(u_parts[2], 0)
    g_kept, g_theirs = half_way(g_parts, g_near, 0)
    g_far = to_near(g_theirs, 1)
    for k in range(1, cols - 2):
        out_carry = around(out_carry, outs[k])
    o_received = to_core(o_sent)
    dq, dk, dv = attend_backward(
        q_rows, kv_all, mixed_back, top, cosine, -sine, row_ids, key_ids
    )
    o_sum = token_sum([mixed], (0, width), [branch_back], low, o_received)
    o_low, o_high = jnp.split(o_sum, 2, 0)
    o_low = prepare(o_low, 1)
    dq, dk, dv, o_low, o_high, g_far, u_near, out_carry = fence(
        dq, dk, dv, o_low, o_high, g_far, u_near, out_carry
    )

    kv_turned = jnp.concatenate([dk, dv], 1)
    kv_back_pre = kv_turned[reach * own :]
    back_parts = []
    for k in range(1, reach + 1):
        piece = kv_turned[(reach - k) * own : (reach - k + 1) * own].astype(bf16)
        back_parts.append(along(piece, -k))
    u_kept, u_theirs = half_way(u_parts, u_near, 0)
    u_far = to_near(u_theirs, 1)
    o_low_near = to_near(o_low[2], 0)
    q_sent = token_sum([normed], high, [dq], (0, width))
    o_high = prepare(o_high, 1)
    back_parts, q_sent, u_far, o_low_near, o_high = fence(
        back_parts, q_sent, u_far, o_low_near, o_high
    )

    out_carry = around(out_carry, outs[cols - 2])
    o_low_kept, o_theirs = half_way(o_low, o_low_near, 1)
    o_low_far = to_near(o_theirs, 1)
    q_received = to_core(q_sent)
    for piece in back_parts:
        kv_back_pre = kv_back_pre + piece.astype(f32)
    kv_back = jnp.concatenate(
        [rotate(kv_back_pre[:, :kv_width], cosine, -sine), kv_back_pre[:, kv_width:]], 1
    ).astype(bf16)
    kv_sent = token_sum([normed], high, [kv_back], (0, 2 * kv_width))
    kv_received = to_core(kv_sent)
    kv_sum = token_sum([normed], low, [kv_back], (0, 2 * kv_width), kv_received)
    kv_parts = prepare(kv_sum, 0)
    kv_parts, kv_back, o_low_far, q_received, o_high = fence(
        kv_parts, kv_back, o_low_far, q_received, o_high
    )

    kv_near = to_near(kv_parts[2], 0)
    o_high_near = to_near(o_high[2], 0)
    normed_back = rows_product([dq, kv_back], [q_matrix, kv_matrix], True, f32)
    from_norm, attention_gain_part = norm_back(normed_back, inputs, factor_one, gain_one)
    input_grad = xor_order(middle_grad + from_norm, target, blocks, 1)
    gains = xor_order(jnp.stack([attention_gain_part, mlp_gain_part]), target, blocks, 1)
    q_sum = token_sum([normed], low, [dq], (0, width), q_received)
    kv_near, o_high_near, input_grad, gains, q_sum, out_carry = fence(
        kv_near, o_high_near, input_grad, gains, q_sum, out_carry
    )

    kv_kept, kv_theirs = half_way(kv_parts, kv_near, 0)
    kv_far = to_near(kv_theirs, 1)
    o_high_kept, o_theirs = half_way(o_high, o_high_near, 1)
    o_high_far = to_near(o_theirs, 1)
    hops = [1 << n for n in range(cols.bit_length() - 1)]
    gains = gains + to_xor_cols(gains, hops[0])
    q_parts = prepare(q_sum, 0)
    kv_far, o_high_far, gains, q_parts = fence(kv_far, o_high_far, gains, q_parts)

    q_near = to_near(q_parts[2], 0)
    kv_sum = finish(kv_kept, kv_far).astype(bf16)
    total = [kv_sum] + [to_xor_cols(kv_sum, k) for k in range(1, cols)]
    for hop in hops[1:]:
        gains = gains + to_xor_cols(gains, hop)
    out_sum = jnp.concatenate(
        [finish(o_low_kept, o_low_far), finish(o_high_kept, o_high_far)], 0
    ).astype(bf16)
    total, q_near, gains, out_sum = fence(total, q_near, gains, out_sum)

    total = added(total).astype(bf16)
    one = to_near(total, 0)
    q_kept, q_theirs = half_way(q_parts, q_near, 0)
    q_far = to_near(q_theirs, 1)
    out_parts = col_sum(out_sum, 0)
    one, d_far, g_far, u_far, out_carry = fence(one, d_far, g_far, u_far, out_carry)
    down_grad, gate_grad, up_grad = finish(d_kept, d_far), finish(g_kept, g_far), finish(u_kept, u_far)
    piece = out_last.astype(f32) + out_carry.astype(f32)
    output = xor_order((middle + keep * piece).astype(bf16), target, blocks, 1)
    one, q_far, out_parts, output, gains, down_grad, gate_grad, up_grad = fence(
        one, q_far, out_parts, output, gains, down_grad, gate_grad, up_grad
    )

    two = to_near(jnp.concatenate([total, one], 0), 1)
    gains = gains + to_near(gains, 0)
    gains = gains + to_near(gains, 1)
    q_cols = col_sum(finish(q_kept, q_far), 1)
    out_grad = added(out_parts)
    two, q_cols, out_grad, gains = fence(two, q_cols, out_grad, gains)
    mine = jnp.concatenate([total, one, two], 0)
    theirs = to_core(mine)
    gains = gains + to_core(gains)
    query_grad = added(q_cols)
    found = blank((width, 2 * kv_width))
    for e, part in enumerate((mine, theirs)):
        near, far = (first, 3 - first) if e == 0 else (3 - first, first)
        for n, j in enumerate((0, near, far, 3)):
            at = ((d ^ e) * rows + (r ^ j)) * step
            found = put(found, part[n * step : (n + 1) * step], 0, at, 0)
    found = found.astype(f32)
    key_grad, value_grad = found[:, :kv_width], found[:, kv_width:]
    return (
        output,
        input_grad,
        gains[0],
        gains[1],
        query_grad,
        key_grad,
        value_grad,
        out_grad,
        gate_grad,
        up_grad,
        down_grad,
    )


def solution(mesh):
    return jax.shard_map(
        local,
        mesh=mesh,
        in_specs=(
            P(("dp", "rows", "cols"), None),
            P(),
            P(),
            P("rows", "cols"),
            P("rows", None),
            P("rows", None),
            P(None, "rows"),
            P("rows", "cols"),
            P("rows", "cols"),
            P("cols", "rows"),
            P(("dp", "rows"), None),
            P(("dp", "rows")),
            P(("dp", "rows", "cols"), None),
        ),
        out_specs=(
            P(("dp", "rows", "cols"), None),
            P(("dp", "rows", "cols"), None),
            P(),
            P(),
            P(("dp", "rows"), "cols"),
            P(),
            P(),
            P("cols", ("dp", "rows")),
            P(("dp", "rows"), "cols"),
            P(("dp", "rows"), "cols"),
            P("cols", ("dp", "rows")),
        ),
        check_vma=False,
    )
```

```python
import jax
import jax.numpy as jnp
from jax import lax
from jax.experimental import pallas as pl
from jax.experimental.pallas import tpu as pltpu
from jax.sharding import PartitionSpec as P

HEADS = 16
KV_HEADS = 2
HEAD_DIM = 128

epsilon = 1e-05
negative = -1e30
rope_base = 10000.0
log2e = 1.4426950408889634
bf16 = jnp.bfloat16
f32 = jnp.float32


def dot(left, right, dims):
    return lax.dot_general(left, right, ((dims[:1], dims[1:]), ((), ())), preferred_element_type=f32)


def turn(values, cosine, sine):
    return values * cosine + pltpu.roll(values, HEAD_DIM // 2, 1) * sine


def mask_bias(row_ids, key_ids):
    span, own = key_ids.shape[0], row_ids.shape[1]
    key_place = lax.broadcasted_iota(jnp.int32, (span, own), 0)
    row_place = lax.broadcasted_iota(jnp.int32, (span, own), 1) + (span - own)
    return jnp.where((key_ids == row_ids) & (row_place >= key_place), 0.0, negative)


PER = 4


def forward_kernel(pre_ref, k_ref, v_ref, cos_ref, sin_ref, rid_ref, kid_ref, mixed_ref, q_ref, top_ref, bias_ref, vt_ref):
    head = pl.program_id(0) * PER

    @pl.when(head == 0)
    def _():
        bias_ref[...] = mask_bias(rid_ref[...], kid_ref[...])

    @pl.when(head % (HEADS // KV_HEADS) == 0)
    def _():
        vt_ref[...] = v_ref[...].astype(f32).T.astype(bf16)

    for n in range(PER):
        lanes = slice(n * HEAD_DIM, (n + 1) * HEAD_DIM)
        q = turn(pre_ref[:, lanes], cos_ref[...], sin_ref[...]).astype(bf16)
        q_ref[:, lanes] = q
        scores = dot(k_ref[...], q, (1, 1)) * (HEAD_DIM ** (-0.5) * log2e) + bias_ref[...]
        top = jnp.max(scores, axis=0, keepdims=True)
        exponent = jnp.exp2(scores - top)
        total = jnp.sum(exponent, axis=0, keepdims=True)
        mixed = dot(vt_ref[...], exponent.astype(bf16), (1, 0)) * (1.0 / total)
        mixed_ref[:, lanes] = mixed.T.astype(bf16)
        top_ref[n] = top + jnp.log2(total)


def attend_forward(pre, kv_all, cosine, sine, row_ids, key_ids):
    own, width = pre.shape
    span = kv_all.shape[0]
    share = HEADS // KV_HEADS
    whole = lambda shape: pl.BlockSpec(shape, lambda h: (0, 0))
    head = pl.BlockSpec((own, PER * HEAD_DIM), lambda h: (0, h))
    return pl.pallas_call(
        forward_kernel,
        grid=(HEADS // PER,),
        in_specs=[
            head,
            pl.BlockSpec((span, HEAD_DIM), lambda h: (0, h * PER // share)),
            pl.BlockSpec((span, HEAD_DIM), lambda h: (0, KV_HEADS + h * PER // share)),
            whole((own, HEAD_DIM)),
            whole((own, HEAD_DIM)),
            whole((1, own)),
            whole((span, 1)),
        ],
        out_specs=[head, head, pl.BlockSpec((PER, 1, own), lambda h: (h, 0, 0))],
        out_shape=[
            jax.ShapeDtypeStruct((own, width), bf16),
            jax.ShapeDtypeStruct((own, width), bf16),
            jax.ShapeDtypeStruct((HEADS, 1, own), f32),
        ],
        scratch_shapes=[pltpu.VMEM((span, own), f32), pltpu.VMEM((HEAD_DIM, span), bf16)],
        compiler_params=pltpu.CompilerParams(dimension_semantics=("arbitrary",), vmem_limit_bytes=32 << 20),
        cost_estimate=pl.CostEstimate(flops=0, transcendentals=0, bytes_accessed=0),
    )(pre, kv_all, kv_all, cosine, sine, row_ids[None, :], key_ids[:, None])


def backward_kernel(q_ref, k_ref, v_ref, back_ref, top_ref, cos_ref, sin_ref, rid_ref, kid_ref, dq_ref, dk_ref, dv_ref, bias_ref, kt_ref):
    step = pl.program_id(0)

    @pl.when(step == 0)
    def _():
        bias_ref[...] = mask_bias(rid_ref[...], kid_ref[...])

    @pl.when(step % (HEADS // KV_HEADS // PER) == 0)
    def _():
        kt_ref[...] = k_ref[...].astype(f32).T.astype(bf16)
        dk_ref[...] = jnp.zeros_like(dk_ref)
        dv_ref[...] = jnp.zeros_like(dv_ref)

    scale = HEAD_DIM ** (-0.5)
    for n in range(PER):
        lanes = slice(n * HEAD_DIM, (n + 1) * HEAD_DIM)
        q = q_ref[:, lanes]
        back = back_ref[:, lanes]
        scores = dot(k_ref[...], q, (1, 1)) * (scale * log2e) + bias_ref[...]
        probs = jnp.exp2(scores - top_ref[n])
        dv_ref[...] += dot(probs.astype(bf16), back, (1, 0))
        weight_back = dot(v_ref[...], back, (1, 1))
        inner = jnp.sum(weight_back * probs, axis=0, keepdims=True)
        score_back = (probs * (weight_back - inner)).astype(bf16)
        dk_ref[...] += dot(score_back, q, (1, 0)) * scale
        turned = (dot(kt_ref[...], score_back, (1, 0)) * scale).T
        dq_ref[:, lanes] = turn(turned, cos_ref[...], sin_ref[...]).astype(bf16)


def attend_backward(q_rows, kv_all, mixed_back, top, cosine, sine, row_ids, key_ids):
    own, width = q_rows.shape
    span = kv_all.shape[0]
    steps = HEADS // KV_HEADS // PER
    whole = lambda shape: pl.BlockSpec(shape, lambda h: (0, 0))
    head = pl.BlockSpec((own, PER * HEAD_DIM), lambda h: (0, h))
    shared = pl.BlockSpec((span, HEAD_DIM), lambda h: (0, h // steps))
    return pl.pallas_call(
        backward_kernel,
        grid=(HEADS // PER,),
        in_specs=[
            head,
            shared,
            pl.BlockSpec((span, HEAD_DIM), lambda h: (0, KV_HEADS + h // steps)),
            head,
            pl.BlockSpec((PER, 1, own), lambda h: (h, 0, 0)),
            whole((own, HEAD_DIM)),
            whole((own, HEAD_DIM)),
            whole((1, own)),
            whole((span, 1)),
        ],
        out_specs=[head, shared, shared],
        out_shape=[
            jax.ShapeDtypeStruct((own, width), bf16),
            jax.ShapeDtypeStruct((span, KV_HEADS * HEAD_DIM), f32),
            jax.ShapeDtypeStruct((span, KV_HEADS * HEAD_DIM), f32),
        ],
        scratch_shapes=[pltpu.VMEM((span, own), f32), pltpu.VMEM((HEAD_DIM, span), bf16)],
        compiler_params=pltpu.CompilerParams(dimension_semantics=("arbitrary",), vmem_limit_bytes=32 << 20),
        cost_estimate=pl.CostEstimate(flops=0, transcendentals=0, bytes_accessed=0),
    )(q_rows, kv_all, kv_all, mixed_back, top, cosine, sine, row_ids[None, :], key_ids[:, None])


FREE = pl.CostEstimate(flops=0, transcendentals=0, bytes_accessed=0)


def call(kernel, grid, in_specs, out_specs, out_shape, scratch=()):
    return pl.pallas_call(
        kernel,
        grid=grid,
        in_specs=in_specs,
        out_specs=out_specs,
        out_shape=out_shape,
        scratch_shapes=list(scratch),
        compiler_params=pltpu.CompilerParams(
            dimension_semantics=("arbitrary",) * len(grid), vmem_limit_bytes=48 << 20
        ),
        cost_estimate=FREE,
    )


def fixed(shape):
    return pl.BlockSpec(shape, lambda i: (0,) * len(shape))


def through_kernel(h_ref, f_ref, g_ref, u_ref, d_ref, hid_ref, gb_ref, ub_ref):
    gate = dot(h_ref[...], g_ref[...], (1, 0))
    up = dot(h_ref[...], u_ref[...], (1, 0))
    back = dot(f_ref[...], d_ref[...], (1, 1))
    s = jax.nn.sigmoid(gate)
    swish = gate * s
    hid_ref[...] = (swish * up).astype(bf16)
    ub_ref[...] = (back * swish).astype(bf16)
    gb_ref[...] = (back * up * s * (1.0 + gate * (1.0 - s))).astype(bf16)


def feed_through(hidden, feed, g_matrix, u_matrix, d_matrix):
    count, width = hidden.shape
    units = g_matrix.shape[1]
    tile = min(256, units)
    across = pl.BlockSpec((width, tile), lambda i: (0, i))
    out = pl.BlockSpec((count, tile), lambda i: (0, i))
    return call(
        through_kernel,
        (pl.cdiv(units, tile),),
        [fixed((count, width))] * 2 + [across, across, pl.BlockSpec((tile, width), lambda i: (i, 0))],
        [out] * 3,
        [jax.ShapeDtypeStruct((count, units), bf16)] * 3,
    )(hidden, feed, g_matrix, u_matrix, d_matrix)


def finish_kernel(f_ref, gate_ref, up_ref, d_ref, hid_ref, gb_ref, ub_ref):
    gate = gate_ref[...]
    back = dot(f_ref[...], d_ref[...], (1, 1))
    s = jax.nn.sigmoid(gate)
    swish = gate * s
    hid_ref[...] = (swish * up_ref[...]).astype(bf16)
    ub_ref[...] = (back * swish).astype(bf16)
    gb_ref[...] = (back * up_ref[...] * s * (1.0 + gate * (1.0 - s))).astype(bf16)


def feed_finish(feed, gate, up, d_matrix):
    count, units = gate.shape
    width = feed.shape[1]
    tile = min(256, units)
    out = pl.BlockSpec((count, tile), lambda i: (0, i))
    return call(
        finish_kernel,
        (pl.cdiv(units, tile),),
        [fixed((count, width)), out, out, pl.BlockSpec((tile, width), lambda i: (i, 0))],
        [out] * 3,
        [jax.ShapeDtypeStruct((count, units), bf16)] * 3,
    )(feed, gate, up, d_matrix)


def rows_products(sets, rights, turned, dtype, count):
    n, many = len(rights), len(sets)
    columns = rights[0].shape[0 if turned else 1]
    tile = min(512, columns)

    def kernel(*refs):
        for m in range(many):
            total = 0.0
            for k in range(n):
                total = total + dot(refs[n + n * m + k][...], refs[k][...], (1, 1 if turned else 0))
            refs[m - many][...] = total.astype(dtype)

    specs = []
    for x in rights:
        if turned:
            specs.append(pl.BlockSpec((tile, x.shape[1]), lambda i: (i, 0)))
        else:
            specs.append(pl.BlockSpec((x.shape[0], tile), lambda i: (0, i)))
    operands = list(rights)
    for lefts, block in sets:
        specs += [pl.BlockSpec((count, x.shape[1]), lambda i, block=block: (block, 0)) for x in lefts]
        operands += list(lefts)
    return call(
        kernel,
        (columns // tile,),
        specs,
        [pl.BlockSpec((count, tile), lambda i: (0, i))] * many,
        [jax.ShapeDtypeStruct((count, columns), dtype)] * many,
    )(*operands)


def rows_product(lefts, rights, turned, dtype, block=0, count=None):
    count = lefts[0].shape[0] if count is None else count
    return rows_products([(lefts, block)], rights, turned, dtype, count)[0]


def token_sums(lefts, left_lanes, rights, right_lanes, received=None):
    n, many = len(lefts), len(rights)
    start, rows_out = left_lanes
    tile = min(512 if rows_out >= 2048 else 256, rows_out)
    base, columns = right_lanes

    def kernel(*refs):
        for k in range(n):
            left = refs[k][...]
            for m in range(many):
                part = dot(left, refs[n * (m + 1) + k][...], (0, 0))
                totals = [part] * many if k == 0 and m == 0 else totals
                totals[m] = part if k == 0 else totals[m] + part
        for m in range(many):
            total = totals[m]
            if received is not None:
                total = total + refs[n * (many + 1) + m][...].astype(f32)
            refs[m - many][...] = total.astype(bf16)

    first, second = start // tile, base // columns
    specs = [pl.BlockSpec((x.shape[0], tile), lambda i: (0, first + i)) for x in lefts]
    operands = list(lefts)
    for group in rights:
        specs += [pl.BlockSpec((x.shape[0], columns), lambda i: (0, second)) for x in group]
        operands += list(group)
    out = pl.BlockSpec((tile, columns), lambda i: (i, 0))
    if received is not None:
        specs += [out] * many
        operands += list(received)
    return call(
        kernel,
        (pl.cdiv(rows_out, tile),),
        specs,
        [out] * many,
        [jax.ShapeDtypeStruct((rows_out, columns), bf16)] * many,
    )(*operands)


def token_sum(lefts, left_lanes, rights, right_lanes, received=None):
    received = None if received is None else [received]
    return token_sums(lefts, left_lanes, [rights], right_lanes, received)[0]


def nn(left, right):
    return dot(left, right, (1, 0))


def nt(left, right):
    return dot(left, right, (1, 1))


def tn(left, right):
    return dot(left, right, (0, 0))


def after(value, *earlier):
    return lax.optimization_barrier((value,) + earlier)[0]


def fence(*values):
    return lax.optimization_barrier(values)


def blank(shape):
    return pl.pallas_call(
        lambda out: None,
        out_specs=pl.BlockSpec(memory_space=pl.ANY),
        out_shape=jax.ShapeDtypeStruct(shape, bf16),
    )()


def xor_blocks(blocks, index):
    bit = 1
    while bit < len(blocks):
        swap = (index & bit) != 0
        blocks = [jnp.where(swap, blocks[j ^ bit], blocks[j]) for j in range(len(blocks))]
        bit *= 2
    return blocks


def xor_order(value, index, count, axis):
    return jnp.concatenate(xor_blocks(jnp.split(value, count, axis), index), axis)


def tree_sum(values):
    while len(values) > 1:
        values = [values[i] + values[i + 1] for i in range(0, len(values), 2)]
    return values[0]


def rotary_tables(positions):
    half = HEAD_DIM // 2
    frequency = rope_base ** (-2.0 * jnp.arange(half, dtype=f32) / HEAD_DIM)
    angles = positions.astype(f32)[:, None] * frequency[None, :]
    cosine, sine = jnp.cos(angles), jnp.sin(angles)
    return jnp.concatenate([cosine, cosine], 1), jnp.concatenate([-sine, sine], 1)


def rotate(values, cosine, sine):
    heads = jnp.split(values, values.shape[1] // HEAD_DIM, 1)
    half = HEAD_DIM // 2
    swapped = [jnp.concatenate([h[:, half:], h[:, :half]], 1) for h in heads]
    return jnp.concatenate([h * cosine + s * sine for h, s in zip(heads, swapped)], 1)


def norm_factor(values):
    return lax.rsqrt(jnp.mean(values * values, axis=-1, keepdims=True) + epsilon)


def norm_back(grad, values, factor, gain):
    y = grad * gain
    pulled = factor * y - values * factor**3 * jnp.mean(y * values, axis=-1, keepdims=True)
    return pulled, jnp.sum(grad * values * factor, axis=0)


def local(
    tokens,
    attention_gain,
    mlp_gain,
    w_query,
    w_key,
    w_value,
    w_out,
    w_gate,
    w_up,
    w_down,
    segment_ids,
    skip_mask,
    cotangent,
):
    cols, rows = lax.axis_size("cols"), lax.axis_size("rows")
    c, r, d = lax.axis_index("cols"), lax.axis_index("rows"), lax.axis_index("dp")
    own, width = tokens.shape
    half = width // 2
    sequences, length = segment_ids.shape
    blocks = 2 * rows
    step = width // blocks
    target = d * rows + r
    kv_width = KV_HEADS * HEAD_DIM

    def to_rows(value, a):
        return lax.ppermute(value, "rows", [(i, i ^ a) for i in range(rows)])

    def to_near(value, turn):
        pairs = []
        for core in range(2):
            a = 1 + (core ^ turn)
            pairs += [(core * rows + i, core * rows + (i ^ a)) for i in range(rows)]
        return lax.ppermute(value, ("dp", "rows"), pairs)

    first = 1 + d

    def to_core(value):
        return lax.ppermute(value, "dp", [(0, 1), (1, 0)])

    def to_cols(value, k):
        return lax.ppermute(value, "cols", [(i, (i + k) % cols) for i in range(cols)])

    def along(value, k):
        return lax.ppermute(
            value, "cols", [(i, i + k) for i in range(cols) if 0 <= i + k < cols]
        )

    def to_xor_cols(value, k):
        return lax.ppermute(value, "cols", [(i, i ^ k) for i in range(cols)])

    def spot(j, e):
        return ((2 * (r ^ j) + (d ^ e)) ^ target) * step

    def put(full, piece, axis, start, offset):
        at = (start + offset, 0) if axis == 0 else (offset, start)
        return lax.dynamic_update_slice(full, piece, at)

    def fill(full, axis, one, two, e):
        near, far = (first, 3 - first) if e == 0 else (3 - first, first)
        size = two.shape[0] // 2
        full = put(full, one, axis, spot(near, e), 0)
        full = put(full, two[:size], axis, spot(far, e), 0)
        return put(full, two[size:], axis, spot(3, e), 0)

    def halves(weight, axis):
        low, high = jnp.split(weight, 2, axis)
        return jnp.where(d == 0, low, high), jnp.where(d == 0, high, low)

    sequence = (c * own) // length
    start = (c * own) % length
    reach = min(-(-(length // 2 - 1) // own), length // own - 1)
    span = (reach + 1) * own
    units = w_gate.shape[1]

    kv_mine, kv_rest = halves(jnp.concatenate([w_key, w_value], 1), 0)
    q_mine, _ = halves(w_query, 0)
    kv_one = to_near(kv_mine, 0)
    q_parts = [q_mine] + [to_xor_cols(q_mine, k) for k in range(1, cols)]
    kv_one, tokens, attention_gain, mlp_gain, w_out, segment_ids, skip_mask, cotangent = fence(
        kv_one, tokens, attention_gain, mlp_gain, w_out, segment_ids, skip_mask, cotangent
    )
    kv_two = to_near(jnp.concatenate([kv_mine, kv_one], 0), 1)
    o_mine, o_rest = halves(w_out, 1)
    o_one = to_near(o_mine, 0)
    inputs = xor_order(tokens, target, blocks, 1).astype(f32)
    gain_one = xor_order(attention_gain, target, blocks, 0)
    gain_two = xor_order(mlp_gain, target, blocks, 0)
    factor_one = norm_factor(inputs)
    normed = (inputs * factor_one * gain_one).astype(bf16)
    cosine, sine = rotary_tables(start + jnp.arange(own))
    keep = (1 - lax.dynamic_index_in_dim(skip_mask, sequence, 0, False)).astype(f32)
    upstream = xor_order(cotangent, target, blocks, 1)
    feed_own = (keep * upstream).astype(bf16)

    (kv_two, q_parts, normed, cosine, sine, feed_own, upstream, w_down, w_gate, w_up) = fence(
        kv_two, q_parts, normed, cosine, sine, feed_own, upstream, w_down, w_gate, w_up
    )
    feeds = [feed_own, to_cols(feed_own, 1)]
    q_mine = jnp.concatenate(xor_blocks(q_parts, c), 1)
    q_one = to_near(q_mine, 0)
    kv_other = (to_core(kv_one), to_core(kv_two))
    q_own_other = to_core(q_mine)
    q_one, q_own_other, kv_other, w_down, o_one = fence(
        q_one, q_own_other, kv_other, w_down, o_one
    )
    q_sent = jnp.concatenate([q_mine, q_one], 0)
    q_two = to_near(q_sent, 1)
    kv_mine, kv_rest, kv_one, kv_two, kv_other, _ = fence(
        kv_mine, kv_rest, kv_one, kv_two, kv_other, q_sent
    )
    kv_matrix = blank((width, 2 * kv_width))
    kv_matrix = put(kv_matrix, kv_mine, 0, spot(0, 0), 0)
    kv_matrix = put(kv_matrix, kv_rest, 0, spot(0, 1), 0)
    kv_matrix = fill(kv_matrix, 0, kv_one, kv_two, 0)
    kv_matrix = fill(kv_matrix, 0, *kv_other, 1)
    kv_pre = nn(normed, kv_matrix)
    kv_own = jnp.concatenate(
        [rotate(kv_pre[:, :kv_width], cosine, sine), kv_pre[:, kv_width:]], 1
    ).astype(bf16)

    kv_own, feeds[1] = fence(kv_own, feeds[1])
    kv_before = [along(kv_own, k) for k in range(reach, 0, -1)]
    for k in range(2, cols - 1):
        feeds.append(to_cols(feeds[-1], 1))
    q_one_other = to_core(q_one)
    q_matrix = blank((width, width))
    q_matrix = put(q_matrix, q_mine, 0, spot(0, 0), 0)
    q_matrix = put(q_matrix, q_own_other, 0, spot(0, 1), 0)
    q_matrix = put(q_matrix, q_one, 0, spot(first, 0), 0)
    q_matrix = put(q_matrix, q_one_other, 0, spot(3 - first, 1), 0)
    ids = lax.dynamic_index_in_dim(segment_ids, sequence, 0, False)
    ids_padded = jnp.concatenate([jnp.full((reach * own,), -1, ids.dtype), ids])
    key_ids = lax.dynamic_slice_in_dim(ids_padded, start, span, 0)
    row_ids = key_ids[reach * own :]

    (q_two, q_matrix, o_mine, o_rest, o_one, w_gate, w_up, w_down) = fence(
        q_two, q_matrix, o_mine, o_rest, o_one, w_gate, w_up, w_down
    )

    o_two = to_near(jnp.concatenate([o_mine, o_one], 0), 1)
    q_two_other = to_core(q_two)
    g_mine, g_rest = halves(w_gate, 0)
    u_mine, u_rest = halves(w_up, 0)
    gu_mine = jnp.concatenate([g_mine, u_mine], 0)
    gu_one = to_near(gu_mine, 0)
    w_mine, w_rest = halves(w_down, 1)
    o_one_other = to_core(o_one)
    kv_all = jnp.concatenate(list(kv_before) + [kv_own], 0)
    rows_two = q_two.shape[0] // 2
    for e, two in ((0, q_two), (1, q_two_other)):
        far = 3 - first if e == 0 else first
        q_matrix = put(q_matrix, two[:rows_two], 0, spot(far, e), 0)
        q_matrix = put(q_matrix, two[rows_two:], 0, spot(3, e), 0)
    q_pre = nn(normed, q_matrix)
    feeds.append(to_cols(after(feeds[-1], q_pre), 1))
    mixed, q_rows, top = attend_forward(q_pre, kv_all, cosine, sine, row_ids, key_ids)
    o_matrix = blank((width, width))
    o_matrix = put(o_matrix, o_mine, 1, spot(0, 0), 0)
    o_matrix = put(o_matrix, o_rest, 1, spot(0, 1), 0)
    o_matrix = put(o_matrix, o_one, 1, spot(first, 0), 0)
    o_matrix = put(o_matrix, o_one_other, 1, spot(3 - first, 1), 0)

    (o_two, gu_one, mixed, q_rows, top, o_matrix, w_mine, w_rest, gu_mine, feeds) = fence(
        o_two, gu_one, mixed, q_rows, top, o_matrix, w_mine, w_rest, gu_mine, feeds
    )
    gu_two = to_near(jnp.concatenate([gu_mine, gu_one], 0), 1)
    o_two_other = to_core(o_two)
    gu_one_other = to_core(gu_one)
    w_one = to_near(w_mine, 0)
    rows_two = o_two.shape[0] // 2
    for e, two in ((0, o_two), (1, o_two_other)):
        far = 3 - first if e == 0 else first
        o_matrix = put(o_matrix, two[:rows_two], 1, spot(far, e), 0)
        o_matrix = put(o_matrix, two[rows_two:], 1, spot(3, e), 0)
    branch = nn(mixed, o_matrix)
    middle = inputs + keep * branch
    factor_two = norm_factor(middle)
    hidden_own = (middle * factor_two * gain_two).astype(bf16)
    hidden_own, o_matrix, gu_one_other, gu_one, gu_mine, g_rest, u_rest = fence(
        hidden_own, o_matrix, gu_one_other, gu_one, gu_mine, g_rest, u_rest
    )
    chunks = [hidden_own, to_cols(hidden_own, 1)]
    g_matrix, u_matrix = blank((width, units)), blank((width, units))
    g_matrix = put(g_matrix, gu_mine[:step], 0, spot(0, 0), 0)
    u_matrix = put(u_matrix, gu_mine[step:], 0, spot(0, 0), 0)
    g_matrix = put(g_matrix, g_rest, 0, spot(0, 1), 0)
    u_matrix = put(u_matrix, u_rest, 0, spot(0, 1), 0)
    for e, one in ((0, gu_one), (1, gu_one_other)):
        near = first if e == 0 else 3 - first
        g_matrix = put(g_matrix, one[:step], 0, spot(near, e), 0)
        u_matrix = put(u_matrix, one[step:], 0, spot(near, e), 0)
    d_matrix = blank((units, width))
    d_matrix = put(d_matrix, w_mine, 1, spot(0, 0), 0)
    d_matrix = put(d_matrix, w_rest, 1, spot(0, 1), 0)

    gu_two, g_matrix, u_matrix, d_matrix, w_mine, w_one, chunks = fence(
        gu_two, g_matrix, u_matrix, d_matrix, w_mine, w_one, chunks
    )
    chunks = list(chunks)
    w_two = to_near(jnp.concatenate([w_mine, w_one], 0), 1)
    gu_two_other = to_core(gu_two)
    w_one_other = to_core(w_one)
    d_matrix = put(d_matrix, w_one, 1, spot(first, 0), 0)
    d_matrix = put(d_matrix, w_one_other, 1, spot(3 - first, 1), 0)
    for e, two in ((0, gu_two), (1, gu_two_other)):
        far = 3 - first if e == 0 else first
        for n, at in enumerate((spot(far, e), spot(3, e))):
            piece = two[n * 2 * step : (n + 1) * 2 * step]
            g_matrix = put(g_matrix, piece[:step], 0, at, 0)
            u_matrix = put(u_matrix, piece[step:], 0, at, 0)
    chunks.append(to_cols(chunks[1], 1))

    def gate_up(hidden):
        gate, up = nn(hidden, g_matrix), nn(hidden, u_matrix)
        return gate, up

    near_hidden = jnp.concatenate([chunks[1], chunks[0]], 0)
    near_feed = jnp.concatenate([feeds[1], feeds[0]], 0)
    gate, up = gate_up(near_hidden)
    w_two, gate, up, d_matrix, arrived = fence(w_two, gate, up, d_matrix, chunks[2])
    chunks[2] = arrived
    chunks.append(to_cols(chunks[2], 1))
    w_two_other = to_core(w_two)
    rows_two = w_two.shape[0] // 2
    for e, two in ((0, w_two), (1, w_two_other)):
        far = 3 - first if e == 0 else first
        d_matrix = put(d_matrix, two[:rows_two], 1, spot(far, e), 0)
        d_matrix = put(d_matrix, two[rows_two:], 1, spot(3, e), 0)
    weights = (g_matrix, u_matrix)
    done = [feed_finish(near_feed, gate, up, d_matrix)]
    part = rows_product(done[0][1:], weights, True, bf16, 0, own)
    part, arrived = fence(part, chunks[3])
    chunks[3] = arrived
    for k in range(2, cols - 2):
        carry = to_cols(part, 1)
        chunks.append(to_cols(chunks[k + 1], 1))
        done.append(feed_through(chunks[k], feeds[k], g_matrix, u_matrix, d_matrix))
        part = rows_product(done[-1][1:], weights, True, f32)
        part, carry, arrived, done = fence(part, carry, chunks[k + 2], done)
        done = list(done)
        chunks[k + 2] = arrived
        part = (part.astype(f32) + carry.astype(f32)).astype(bf16)
        (part,) = fence(part)
    k = cols - 2
    carry = to_cols(part, 1)
    far_hidden = jnp.concatenate(chunks[k:], 0)
    far_feed = jnp.concatenate(feeds[k:], 0)
    done.append(feed_through(after(far_hidden, part), far_feed, g_matrix, u_matrix, d_matrix))
    hids, gbs, ubs = ([x[n] for x in done] for n in range(3))
    h_parts = [near_hidden] + chunks[2:k] + [far_hidden]
    f_parts = [near_feed] + feeds[2:k] + [far_feed]
    low, high, full = (0, half), (half, half), (0, units)
    part = rows_product((gbs[-1], ubs[-1]), weights, True, bf16, 0, own)
    d_sent = token_sum(hids, full, f_parts, high)
    part, carry, d_sent, hids, gbs, ubs, h_parts, f_parts = fence(
        part, carry, d_sent, hids, gbs, ubs, h_parts, f_parts
    )
    part = (part.astype(f32) + carry.astype(f32)).astype(bf16)
    part, d_sent, hids, gbs, ubs = fence(part, d_sent, hids, gbs, ubs)

    carry = to_cols(part, 1)
    d_received = to_core(d_sent)
    part, own_part = rows_products(
        [((gbs[-1], ubs[-1]), 1), ((gbs[0], ubs[0]), 1)], weights, True, f32, own
    )
    g_sent, u_sent = token_sums(h_parts, high, [gbs, ubs], full)
    d_sum = token_sum(hids, full, f_parts, low, d_received)
    part, own_part, carry, d_sum, g_sent, u_sent, hids, gbs, ubs = fence(
        part, own_part, carry, d_sum, g_sent, u_sent, hids, gbs, ubs
    )
    part = (part.astype(f32) + carry.astype(f32)).astype(bf16)
    part, own_part, d_sum, g_sent, u_sent, gbs, ubs, hids = fence(
        part, own_part, d_sum, g_sent, u_sent, gbs, ubs, hids
    )

    def prepare(total, axis):
        pieces = jnp.split(total, rows, axis)
        sent = jnp.concatenate([jnp.where(d == 0, pieces[1], pieces[2]), pieces[3]], axis)
        return pieces[0], jnp.where(d == 0, pieces[2], pieces[1]), sent

    def half_way(parts, near, axis):
        mine, theirs = jnp.split(near, 2, axis)
        return (parts[0], mine), (parts[1].astype(f32) + theirs.astype(f32)).astype(bf16)

    def finish(kept, far):
        return kept[0].astype(f32) + kept[1].astype(f32) + far.astype(f32)

    def around(carry, part):
        return to_cols((part.astype(f32) + carry.astype(f32)).astype(bf16), 1)

    def col_pieces(total, axis):
        return xor_blocks(jnp.split(total.astype(bf16), cols, axis), c)

    def col_sum(pieces):
        return [pieces[0]] + [to_xor_cols(pieces[k], k) for k in range(1, cols)]

    def added(values):
        return tree_sum([x.astype(f32) for x in values])

    carry = to_cols(part, 1)
    d_parts = prepare(d_sum, 1)
    d_near = to_near(d_parts[2], 0)
    g_received = to_core(g_sent)
    u_received = to_core(u_sent)
    outs = jnp.split(rows_product([hids[0]], [d_matrix], False, bf16), 2, 0)
    g_sum, u_sum = token_sums(h_parts, low, [gbs, ubs], full, [g_received, u_received])
    g_parts, u_parts = prepare(g_sum, 0), prepare(u_sum, 0)
    part, carry, d_near, g_parts, u_parts, hids, outs = fence(
        own_part, carry, d_near, g_parts, u_parts, hids, outs
    )

    out_carry = to_cols(outs[0], 1)
    out_last = outs[1]
    g_near = to_near(g_parts[2], 0)
    d_kept, d_theirs = half_way(d_parts, d_near, 1)
    d_far = to_near(d_theirs, 1)
    hidden_in_back = part + carry.astype(f32)
    from_norm, mlp_gain_part = norm_back(hidden_in_back, middle, factor_two, gain_two)
    middle_grad = upstream + from_norm
    branch_back = (keep * middle_grad).astype(bf16)
    mixed_back = rows_product([branch_back], [o_matrix], True, bf16)
    o_sent = token_sum([mixed], (0, width), [branch_back], high)
    outs = [None] + [rows_product([x], [d_matrix], False, bf16) for x in hids[1:-1]]
    outs += jnp.split(rows_product([hids[-1]], [d_matrix], False, bf16), 2, 0)
    mixed_back, branch_back, o_sent, d_far, g_near, outs, out_carry = fence(
        mixed_back, branch_back, o_sent, d_far, g_near, outs, out_carry
    )

    u_near = to_near(u_parts[2], 0)
    g_kept, g_theirs = half_way(g_parts, g_near, 0)
    g_far = to_near(g_theirs, 1)
    for k in range(1, cols - 2):
        out_carry = around(out_carry, outs[k])
    o_received = to_core(o_sent)
    dq, dk, dv = attend_backward(
        q_rows, kv_all, mixed_back, top, cosine, -sine, row_ids, key_ids
    )
    o_sum = token_sum([mixed], (0, width), [branch_back], low, o_received)
    o_low, o_high = jnp.split(o_sum, 2, 0)
    o_low = prepare(o_low, 1)
    dq, dk, dv, o_low, o_high, g_far, u_near, out_carry = fence(
        dq, dk, dv, o_low, o_high, g_far, u_near, out_carry
    )

    kv_turned = jnp.concatenate([dk, dv], 1)
    kv_back_pre = kv_turned[reach * own :]
    back_parts = []
    for k in range(1, reach + 1):
        piece = kv_turned[(reach - k) * own : (reach - k + 1) * own].astype(bf16)
        back_parts.append(along(piece, -k))
    u_kept, u_theirs = half_way(u_parts, u_near, 0)
    u_far = to_near(u_theirs, 1)
    o_low_near = to_near(o_low[2], 0)
    q_sent = token_sum([normed], high, [dq], (0, width))
    o_high = prepare(o_high, 1)
    back_parts, q_sent, u_far, o_low_near, o_high = fence(
        back_parts, q_sent, u_far, o_low_near, o_high
    )

    out_carry = around(out_carry, outs[cols - 2])
    o_low_kept, o_theirs = half_way(o_low, o_low_near, 1)
    o_low_far = to_near(o_theirs, 1)
    q_received = to_core(q_sent)
    for piece in back_parts:
        kv_back_pre = kv_back_pre + piece.astype(f32)
    kv_back = jnp.concatenate(
        [rotate(kv_back_pre[:, :kv_width], cosine, -sine), kv_back_pre[:, kv_width:]], 1
    ).astype(bf16)
    kv_sent = token_sum([normed], high, [kv_back], (0, 2 * kv_width))
    kv_received = to_core(kv_sent)
    kv_sum = token_sum([normed], low, [kv_back], (0, 2 * kv_width), kv_received)
    kv_parts = prepare(kv_sum, 0)
    kv_parts, kv_back, o_low_far, q_received, o_high = fence(
        kv_parts, kv_back, o_low_far, q_received, o_high
    )

    kv_near = to_near(kv_parts[2], 0)
    o_high_near = to_near(o_high[2], 0)
    normed_back = rows_product([dq, kv_back], [q_matrix, kv_matrix], True, f32)
    from_norm, attention_gain_part = norm_back(normed_back, inputs, factor_one, gain_one)
    input_grad = xor_order(middle_grad + from_norm, target, blocks, 1)
    gains = xor_order(jnp.stack([attention_gain_part, mlp_gain_part]), target, blocks, 1)
    q_sum = token_sum([normed], low, [dq], (0, width), q_received)
    kv_near, o_high_near, input_grad, gains, q_sum, out_carry = fence(
        kv_near, o_high_near, input_grad, gains, q_sum, out_carry
    )

    kv_kept, kv_theirs = half_way(kv_parts, kv_near, 0)
    kv_far = to_near(kv_theirs, 1)
    o_high_kept, o_theirs = half_way(o_high, o_high_near, 1)
    o_high_far = to_near(o_theirs, 1)
    hops = [1 << n for n in range(cols.bit_length() - 1)]
    gains = gains + to_xor_cols(gains, hops[0])
    q_parts = prepare(q_sum, 0)
    kv_far, o_high_far, gains, q_parts = fence(kv_far, o_high_far, gains, q_parts)

    q_near = to_near(q_parts[2], 0)
    kv_sum = finish(kv_kept, kv_far).astype(bf16)
    total = [kv_sum] + [to_xor_cols(kv_sum, k) for k in range(1, cols)]
    for hop in hops[1:]:
        gains = gains + to_xor_cols(gains, hop)
    out_sum = jnp.concatenate(
        [finish(o_low_kept, o_low_far), finish(o_high_kept, o_high_far)], 0
    ).astype(bf16)
    out_pieces = col_pieces(out_sum, 0)
    total, q_near, gains, out_pieces = fence(total, q_near, gains, out_pieces)

    total = added(total).astype(bf16)
    one = to_near(total, 0)
    q_kept, q_theirs = half_way(q_parts, q_near, 0)
    q_far = to_near(q_theirs, 1)
    out_parts = col_sum(out_pieces)
    one, d_far, g_far, u_far, out_carry = fence(one, d_far, g_far, u_far, out_carry)
    down_grad, gate_grad, up_grad = finish(d_kept, d_far), finish(g_kept, g_far), finish(u_kept, u_far)
    piece = out_last.astype(f32) + out_carry.astype(f32)
    output = xor_order((middle + keep * piece).astype(bf16), target, blocks, 1)
    one, q_far, out_parts, output, gains, down_grad, gate_grad, up_grad = fence(
        one, q_far, out_parts, output, gains, down_grad, gate_grad, up_grad
    )

    two = to_near(jnp.concatenate([total, one], 0), 1)
    gains = gains + to_near(gains, 0)
    gains = gains + to_near(gains, 1)
    q_cols = col_sum(col_pieces(finish(q_kept, q_far), 1))
    out_grad = added(out_parts)
    two, q_cols, out_grad, gains = fence(two, q_cols, out_grad, gains)
    mine = jnp.concatenate([total, one, two], 0)
    theirs = to_core(mine)
    gains = gains + to_core(gains)
    query_grad = added(q_cols)
    found = blank((width, 2 * kv_width))
    for e, part in enumerate((mine, theirs)):
        near, far = (first, 3 - first) if e == 0 else (3 - first, first)
        for n, j in enumerate((0, near, far, 3)):
            at = ((d ^ e) * rows + (r ^ j)) * step
            found = put(found, part[n * step : (n + 1) * step], 0, at, 0)
    found = found.astype(f32)
    key_grad, value_grad = found[:, :kv_width], found[:, kv_width:]
    return (
        output,
        input_grad,
        gains[0],
        gains[1],
        query_grad,
        key_grad,
        value_grad,
        out_grad,
        gate_grad,
        up_grad,
        down_grad,
    )


def solution(mesh):
    return jax.shard_map(
        local,
        mesh=mesh,
        in_specs=(
            P(("dp", "rows", "cols"), None),
            P(),
            P(),
            P("rows", "cols"),
            P("rows", None),
            P("rows", None),
            P(None, "rows"),
            P("rows", "cols"),
            P("rows", "cols"),
            P("cols", "rows"),
            P(("dp", "rows"), None),
            P(("dp", "rows")),
            P(("dp", "rows", "cols"), None),
        ),
        out_specs=(
            P(("dp", "rows", "cols"), None),
            P(("dp", "rows", "cols"), None),
            P(),
            P(),
            P(("dp", "rows"), "cols"),
            P(),
            P(),
            P("cols", ("dp", "rows")),
            P(("dp", "rows"), "cols"),
            P(("dp", "rows"), "cols"),
            P("cols", ("dp", "rows")),
        ),
        check_vma=False,
    )
```

```python
import jax
import jax.numpy as jnp
from jax import lax
from jax.experimental import pallas as pl
from jax.experimental.pallas import tpu as pltpu
from jax.sharding import PartitionSpec as P

HEADS = 16
KV_HEADS = 2
HEAD_DIM = 128

epsilon = 1e-05
negative = -1e30
rope_base = 10000.0
log2e = 1.4426950408889634
bf16 = jnp.bfloat16
f32 = jnp.float32


def dot(left, right, dims):
    return lax.dot_general(left, right, ((dims[:1], dims[1:]), ((), ())), preferred_element_type=f32)


def turn(values, cosine, sine):
    return values * cosine + pltpu.roll(values, HEAD_DIM // 2, 1) * sine


def mask_bias(row_ids, key_ids):
    span, own = key_ids.shape[0], row_ids.shape[1]
    key_place = lax.broadcasted_iota(jnp.int32, (span, own), 0)
    row_place = lax.broadcasted_iota(jnp.int32, (span, own), 1) + (span - own)
    return jnp.where((key_ids == row_ids) & (row_place >= key_place), 0.0, negative)


PER = 4


def forward_kernel(pre_ref, k_ref, v_ref, cos_ref, sin_ref, rid_ref, kid_ref, mixed_ref, q_ref, top_ref, bias_ref, vt_ref):
    head = pl.program_id(0) * PER

    @pl.when(head == 0)
    def _():
        bias_ref[...] = mask_bias(rid_ref[...], kid_ref[...])

    @pl.when(head % (HEADS // KV_HEADS) == 0)
    def _():
        vt_ref[...] = v_ref[...].astype(f32).T.astype(bf16)

    for n in range(PER):
        lanes = slice(n * HEAD_DIM, (n + 1) * HEAD_DIM)
        q = turn(pre_ref[:, lanes], cos_ref[...], sin_ref[...]).astype(bf16)
        q_ref[:, lanes] = q
        scores = dot(k_ref[...], q, (1, 1)) * (HEAD_DIM ** (-0.5) * log2e) + bias_ref[...]
        top = jnp.max(scores, axis=0, keepdims=True)
        exponent = jnp.exp2(scores - top)
        total = jnp.sum(exponent, axis=0, keepdims=True)
        mixed = dot(vt_ref[...], exponent.astype(bf16), (1, 0)) * (1.0 / total)
        mixed_ref[:, lanes] = mixed.T.astype(bf16)
        top_ref[n] = top + jnp.log2(total)


def attend_forward(pre, kv_all, cosine, sine, row_ids, key_ids):
    own, width = pre.shape
    span = kv_all.shape[0]
    share = HEADS // KV_HEADS
    whole = lambda shape: pl.BlockSpec(shape, lambda h: (0, 0))
    head = pl.BlockSpec((own, PER * HEAD_DIM), lambda h: (0, h))
    return pl.pallas_call(
        forward_kernel,
        grid=(HEADS // PER,),
        in_specs=[
            head,
            pl.BlockSpec((span, HEAD_DIM), lambda h: (0, h * PER // share)),
            pl.BlockSpec((span, HEAD_DIM), lambda h: (0, KV_HEADS + h * PER // share)),
            whole((own, HEAD_DIM)),
            whole((own, HEAD_DIM)),
            whole((1, own)),
            whole((span, 1)),
        ],
        out_specs=[head, head, pl.BlockSpec((PER, 1, own), lambda h: (h, 0, 0))],
        out_shape=[
            jax.ShapeDtypeStruct((own, width), bf16),
            jax.ShapeDtypeStruct((own, width), bf16),
            jax.ShapeDtypeStruct((HEADS, 1, own), f32),
        ],
        scratch_shapes=[pltpu.VMEM((span, own), f32), pltpu.VMEM((HEAD_DIM, span), bf16)],
        compiler_params=pltpu.CompilerParams(dimension_semantics=("arbitrary",), vmem_limit_bytes=32 << 20),
        cost_estimate=pl.CostEstimate(flops=0, transcendentals=0, bytes_accessed=0),
    )(pre, kv_all, kv_all, cosine, sine, row_ids[None, :], key_ids[:, None])


def backward_kernel(q_ref, k_ref, v_ref, back_ref, top_ref, cos_ref, sin_ref, rid_ref, kid_ref, dq_ref, dk_ref, dv_ref, bias_ref, kt_ref):
    step = pl.program_id(0)

    @pl.when(step == 0)
    def _():
        bias_ref[...] = mask_bias(rid_ref[...], kid_ref[...])

    @pl.when(step % (HEADS // KV_HEADS // PER) == 0)
    def _():
        kt_ref[...] = k_ref[...].astype(f32).T.astype(bf16)
        dk_ref[...] = jnp.zeros_like(dk_ref)
        dv_ref[...] = jnp.zeros_like(dv_ref)

    scale = HEAD_DIM ** (-0.5)
    for n in range(PER):
        lanes = slice(n * HEAD_DIM, (n + 1) * HEAD_DIM)
        q = q_ref[:, lanes]
        back = back_ref[:, lanes]
        scores = dot(k_ref[...], q, (1, 1)) * (scale * log2e) + bias_ref[...]
        probs = jnp.exp2(scores - top_ref[n])
        dv_ref[...] += dot(probs.astype(bf16), back, (1, 0))
        weight_back = dot(v_ref[...], back, (1, 1))
        inner = jnp.sum(weight_back * probs, axis=0, keepdims=True)
        score_back = (probs * (weight_back - inner)).astype(bf16)
        dk_ref[...] += dot(score_back, q, (1, 0)) * scale
        turned = (dot(kt_ref[...], score_back, (1, 0)) * scale).T
        dq_ref[:, lanes] = turn(turned, cos_ref[...], sin_ref[...]).astype(bf16)


def attend_backward(q_rows, kv_all, mixed_back, top, cosine, sine, row_ids, key_ids):
    own, width = q_rows.shape
    span = kv_all.shape[0]
    steps = HEADS // KV_HEADS // PER
    whole = lambda shape: pl.BlockSpec(shape, lambda h: (0, 0))
    head = pl.BlockSpec((own, PER * HEAD_DIM), lambda h: (0, h))
    shared = pl.BlockSpec((span, HEAD_DIM), lambda h: (0, h // steps))
    return pl.pallas_call(
        backward_kernel,
        grid=(HEADS // PER,),
        in_specs=[
            head,
            shared,
            pl.BlockSpec((span, HEAD_DIM), lambda h: (0, KV_HEADS + h // steps)),
            head,
            pl.BlockSpec((PER, 1, own), lambda h: (h, 0, 0)),
            whole((own, HEAD_DIM)),
            whole((own, HEAD_DIM)),
            whole((1, own)),
            whole((span, 1)),
        ],
        out_specs=[head, shared, shared],
        out_shape=[
            jax.ShapeDtypeStruct((own, width), bf16),
            jax.ShapeDtypeStruct((span, KV_HEADS * HEAD_DIM), f32),
            jax.ShapeDtypeStruct((span, KV_HEADS * HEAD_DIM), f32),
        ],
        scratch_shapes=[pltpu.VMEM((span, own), f32), pltpu.VMEM((HEAD_DIM, span), bf16)],
        compiler_params=pltpu.CompilerParams(dimension_semantics=("arbitrary",), vmem_limit_bytes=32 << 20),
        cost_estimate=pl.CostEstimate(flops=0, transcendentals=0, bytes_accessed=0),
    )(q_rows, kv_all, kv_all, mixed_back, top, cosine, sine, row_ids[None, :], key_ids[:, None])


FREE = pl.CostEstimate(flops=0, transcendentals=0, bytes_accessed=0)


def call(kernel, grid, in_specs, out_specs, out_shape, scratch=()):
    return pl.pallas_call(
        kernel,
        grid=grid,
        in_specs=in_specs,
        out_specs=out_specs,
        out_shape=out_shape,
        scratch_shapes=list(scratch),
        compiler_params=pltpu.CompilerParams(
            dimension_semantics=("arbitrary",) * len(grid), vmem_limit_bytes=48 << 20
        ),
        cost_estimate=FREE,
    )


def fixed(shape):
    return pl.BlockSpec(shape, lambda i: (0,) * len(shape))


def through_kernel(h_ref, f_ref, g_ref, u_ref, d_ref, hid_ref, gb_ref, ub_ref):
    gate = dot(h_ref[...], g_ref[...], (1, 0))
    up = dot(h_ref[...], u_ref[...], (1, 0))
    back = dot(f_ref[...], d_ref[...], (1, 1))
    s = jax.nn.sigmoid(gate)
    swish = gate * s
    hid_ref[...] = (swish * up).astype(bf16)
    ub_ref[...] = (back * swish).astype(bf16)
    gb_ref[...] = (back * up * s * (1.0 + gate * (1.0 - s))).astype(bf16)


def feed_through(hidden, feed, g_matrix, u_matrix, d_matrix):
    count, width = hidden.shape
    units = g_matrix.shape[1]
    tile = min(256, units)
    across = pl.BlockSpec((width, tile), lambda i: (0, i))
    out = pl.BlockSpec((count, tile), lambda i: (0, i))
    return call(
        through_kernel,
        (pl.cdiv(units, tile),),
        [fixed((count, width))] * 2 + [across, across, pl.BlockSpec((tile, width), lambda i: (i, 0))],
        [out] * 3,
        [jax.ShapeDtypeStruct((count, units), bf16)] * 3,
    )(hidden, feed, g_matrix, u_matrix, d_matrix)


def finish_kernel(f_ref, gate_ref, up_ref, d_ref, hid_ref, gb_ref, ub_ref):
    gate = gate_ref[...]
    back = dot(f_ref[...], d_ref[...], (1, 1))
    s = jax.nn.sigmoid(gate)
    swish = gate * s
    hid_ref[...] = (swish * up_ref[...]).astype(bf16)
    ub_ref[...] = (back * swish).astype(bf16)
    gb_ref[...] = (back * up_ref[...] * s * (1.0 + gate * (1.0 - s))).astype(bf16)


def feed_finish(feed, gate, up, d_matrix):
    count, units = gate.shape
    width = feed.shape[1]
    tile = min(256, units)
    out = pl.BlockSpec((count, tile), lambda i: (0, i))
    return call(
        finish_kernel,
        (pl.cdiv(units, tile),),
        [fixed((count, width)), out, out, pl.BlockSpec((tile, width), lambda i: (i, 0))],
        [out] * 3,
        [jax.ShapeDtypeStruct((count, units), bf16)] * 3,
    )(feed, gate, up, d_matrix)


def rows_products(sets, rights, turned, dtype, count):
    n, many = len(rights), len(sets)
    columns = rights[0].shape[0 if turned else 1]
    tile = min(512, columns)

    def kernel(*refs):
        for m in range(many):
            total = 0.0
            for k in range(n):
                total = total + dot(refs[n + n * m + k][...], refs[k][...], (1, 1 if turned else 0))
            refs[m - many][...] = total.astype(dtype)

    specs = []
    for x in rights:
        if turned:
            specs.append(pl.BlockSpec((tile, x.shape[1]), lambda i: (i, 0)))
        else:
            specs.append(pl.BlockSpec((x.shape[0], tile), lambda i: (0, i)))
    operands = list(rights)
    for lefts, block in sets:
        specs += [pl.BlockSpec((count, x.shape[1]), lambda i, block=block: (block, 0)) for x in lefts]
        operands += list(lefts)
    return call(
        kernel,
        (columns // tile,),
        specs,
        [pl.BlockSpec((count, tile), lambda i: (0, i))] * many,
        [jax.ShapeDtypeStruct((count, columns), dtype)] * many,
    )(*operands)


def rows_product(lefts, rights, turned, dtype, block=0, count=None):
    count = lefts[0].shape[0] if count is None else count
    return rows_products([(lefts, block)], rights, turned, dtype, count)[0]


def token_sums(lefts, left_lanes, rights, right_lanes, received=None):
    n, many = len(lefts), len(rights)
    start, rows_out = left_lanes
    tile = min(512 if rows_out >= 2048 else 256, rows_out)
    base, columns = right_lanes

    def kernel(*refs):
        for k in range(n):
            left = refs[k][...]
            for m in range(many):
                part = dot(left, refs[n * (m + 1) + k][...], (0, 0))
                totals = [part] * many if k == 0 and m == 0 else totals
                totals[m] = part if k == 0 else totals[m] + part
        for m in range(many):
            total = totals[m]
            if received is not None:
                total = total + refs[n * (many + 1) + m][...].astype(f32)
            refs[m - many][...] = total.astype(bf16)

    first, second = start // tile, base // columns
    specs = [pl.BlockSpec((x.shape[0], tile), lambda i: (0, first + i)) for x in lefts]
    operands = list(lefts)
    for group in rights:
        specs += [pl.BlockSpec((x.shape[0], columns), lambda i: (0, second)) for x in group]
        operands += list(group)
    out = pl.BlockSpec((tile, columns), lambda i: (i, 0))
    if received is not None:
        specs += [out] * many
        operands += list(received)
    return call(
        kernel,
        (pl.cdiv(rows_out, tile),),
        specs,
        [out] * many,
        [jax.ShapeDtypeStruct((rows_out, columns), bf16)] * many,
    )(*operands)


def token_sum(lefts, left_lanes, rights, right_lanes, received=None):
    received = None if received is None else [received]
    return token_sums(lefts, left_lanes, [rights], right_lanes, received)[0]


def nn(left, right):
    return dot(left, right, (1, 0))


def nt(left, right):
    return dot(left, right, (1, 1))


def tn(left, right):
    return dot(left, right, (0, 0))


def after(value, *earlier):
    return lax.optimization_barrier((value,) + earlier)[0]


def fence(*values):
    return lax.optimization_barrier(values)


def blank(shape):
    return pl.pallas_call(
        lambda out: None,
        out_specs=pl.BlockSpec(memory_space=pl.ANY),
        out_shape=jax.ShapeDtypeStruct(shape, bf16),
    )()


def xor_blocks(blocks, index):
    bit = 1
    while bit < len(blocks):
        swap = (index & bit) != 0
        blocks = [jnp.where(swap, blocks[j ^ bit], blocks[j]) for j in range(len(blocks))]
        bit *= 2
    return blocks


def xor_order(value, index, count, axis):
    return jnp.concatenate(xor_blocks(jnp.split(value, count, axis), index), axis)


def tree_sum(values):
    while len(values) > 1:
        values = [values[i] + values[i + 1] for i in range(0, len(values), 2)]
    return values[0]


def rotary_tables(positions):
    half = HEAD_DIM // 2
    frequency = rope_base ** (-2.0 * jnp.arange(half, dtype=f32) / HEAD_DIM)
    angles = positions.astype(f32)[:, None] * frequency[None, :]
    cosine, sine = jnp.cos(angles), jnp.sin(angles)
    return jnp.concatenate([cosine, cosine], 1), jnp.concatenate([-sine, sine], 1)


def rotate(values, cosine, sine):
    heads = jnp.split(values, values.shape[1] // HEAD_DIM, 1)
    half = HEAD_DIM // 2
    swapped = [jnp.concatenate([h[:, half:], h[:, :half]], 1) for h in heads]
    return jnp.concatenate([h * cosine + s * sine for h, s in zip(heads, swapped)], 1)


def norm_factor(values):
    return lax.rsqrt(jnp.mean(values * values, axis=-1, keepdims=True) + epsilon)


def norm_back(grad, values, factor, gain):
    y = grad * gain
    pulled = factor * y - values * factor**3 * jnp.mean(y * values, axis=-1, keepdims=True)
    return pulled, jnp.sum(grad * values * factor, axis=0)


def local(
    tokens,
    attention_gain,
    mlp_gain,
    w_query,
    w_key,
    w_value,
    w_out,
    w_gate,
    w_up,
    w_down,
    segment_ids,
    skip_mask,
    cotangent,
):
    cols, rows = lax.axis_size("cols"), lax.axis_size("rows")
    c, r, d = lax.axis_index("cols"), lax.axis_index("rows"), lax.axis_index("dp")
    own, width = tokens.shape
    half = width // 2
    sequences, length = segment_ids.shape
    blocks = 2 * rows
    step = width // blocks
    target = d * rows + r
    kv_width = KV_HEADS * HEAD_DIM

    def to_rows(value, a):
        return lax.ppermute(value, "rows", [(i, i ^ a) for i in range(rows)])

    def to_near(value, turn):
        pairs = []
        for core in range(2):
            a = 1 + (core ^ turn)
            pairs += [(core * rows + i, core * rows + (i ^ a)) for i in range(rows)]
        return lax.ppermute(value, ("dp", "rows"), pairs)

    first = 1 + d

    def to_core(value):
        return lax.ppermute(value, "dp", [(0, 1), (1, 0)])

    def to_cols(value, k):
        return lax.ppermute(value, "cols", [(i, (i + k) % cols) for i in range(cols)])

    def along(value, k):
        return lax.ppermute(
            value, "cols", [(i, i + k) for i in range(cols) if 0 <= i + k < cols]
        )

    def to_xor_cols(value, k):
        return lax.ppermute(value, "cols", [(i, i ^ k) for i in range(cols)])

    def spot(j, e):
        return ((2 * (r ^ j) + (d ^ e)) ^ target) * step

    def put(full, piece, axis, start, offset):
        at = (start + offset, 0) if axis == 0 else (offset, start)
        return lax.dynamic_update_slice(full, piece, at)

    def fill(full, axis, one, two, e):
        near, far = (first, 3 - first) if e == 0 else (3 - first, first)
        size = two.shape[0] // 2
        full = put(full, one, axis, spot(near, e), 0)
        full = put(full, two[:size], axis, spot(far, e), 0)
        return put(full, two[size:], axis, spot(3, e), 0)

    def halves(weight, axis):
        low, high = jnp.split(weight, 2, axis)
        return jnp.where(d == 0, low, high), jnp.where(d == 0, high, low)

    sequence = (c * own) // length
    start = (c * own) % length
    reach = min(-(-(length // 2 - 1) // own), length // own - 1)
    span = (reach + 1) * own
    units = w_gate.shape[1]

    kv_mine, kv_rest = halves(jnp.concatenate([w_key, w_value], 1), 0)
    q_mine, _ = halves(w_query, 0)
    kv_one = to_near(kv_mine, 0)
    q_parts = [q_mine] + [to_xor_cols(q_mine, k) for k in range(1, cols)]
    kv_one, tokens, attention_gain, mlp_gain, w_out, segment_ids, skip_mask, cotangent = fence(
        kv_one, tokens, attention_gain, mlp_gain, w_out, segment_ids, skip_mask, cotangent
    )
    kv_two = to_near(jnp.concatenate([kv_mine, kv_one], 0), 1)
    o_mine, o_rest = halves(w_out, 1)
    o_one = to_near(o_mine, 0)
    inputs = xor_order(tokens, target, blocks, 1).astype(f32)
    gain_one = xor_order(attention_gain, target, blocks, 0)
    gain_two = xor_order(mlp_gain, target, blocks, 0)
    factor_one = norm_factor(inputs)
    normed = (inputs * factor_one * gain_one).astype(bf16)
    cosine, sine = rotary_tables(start + jnp.arange(own))
    keep = (1 - lax.dynamic_index_in_dim(skip_mask, sequence, 0, False)).astype(f32)
    upstream = xor_order(cotangent, target, blocks, 1)
    feed_own = (keep * upstream).astype(bf16)

    (kv_two, q_parts, normed, cosine, sine, feed_own, upstream, w_down, w_gate, w_up) = fence(
        kv_two, q_parts, normed, cosine, sine, feed_own, upstream, w_down, w_gate, w_up
    )
    feeds = [feed_own, to_cols(feed_own, 1)]
    q_mine = jnp.concatenate(xor_blocks(q_parts, c), 1)
    q_one = to_near(q_mine, 0)
    kv_other = (to_core(kv_one), to_core(kv_two))
    q_own_other = to_core(q_mine)
    q_one, q_own_other, kv_other, w_down, o_one = fence(
        q_one, q_own_other, kv_other, w_down, o_one
    )
    q_sent = jnp.concatenate([q_mine, q_one], 0)
    q_two = to_near(q_sent, 1)
    kv_mine, kv_rest, kv_one, kv_two, kv_other, _ = fence(
        kv_mine, kv_rest, kv_one, kv_two, kv_other, q_sent
    )
    kv_matrix = blank((width, 2 * kv_width))
    kv_matrix = put(kv_matrix, kv_mine, 0, spot(0, 0), 0)
    kv_matrix = put(kv_matrix, kv_rest, 0, spot(0, 1), 0)
    kv_matrix = fill(kv_matrix, 0, kv_one, kv_two, 0)
    kv_matrix = fill(kv_matrix, 0, *kv_other, 1)
    kv_pre = nn(normed, kv_matrix)
    kv_own = jnp.concatenate(
        [rotate(kv_pre[:, :kv_width], cosine, sine), kv_pre[:, kv_width:]], 1
    ).astype(bf16)

    kv_own, feeds[1] = fence(kv_own, feeds[1])
    kv_before = [along(kv_own, k) for k in range(reach, 0, -1)]
    for k in range(2, cols - 1):
        feeds.append(to_cols(feeds[-1], 1))
    q_one_other = to_core(q_one)
    q_matrix = blank((width, width))
    q_matrix = put(q_matrix, q_mine, 0, spot(0, 0), 0)
    q_matrix = put(q_matrix, q_own_other, 0, spot(0, 1), 0)
    q_matrix = put(q_matrix, q_one, 0, spot(first, 0), 0)
    q_matrix = put(q_matrix, q_one_other, 0, spot(3 - first, 1), 0)
    ids = lax.dynamic_index_in_dim(segment_ids, sequence, 0, False)
    ids_padded = jnp.concatenate([jnp.full((reach * own,), -1, ids.dtype), ids])
    key_ids = lax.dynamic_slice_in_dim(ids_padded, start, span, 0)
    row_ids = key_ids[reach * own :]

    (q_two, q_matrix, o_mine, o_rest, o_one, w_gate, w_up, w_down) = fence(
        q_two, q_matrix, o_mine, o_rest, o_one, w_gate, w_up, w_down
    )

    o_two = to_near(jnp.concatenate([o_mine, o_one], 0), 1)
    q_two_other = to_core(q_two)
    g_mine, g_rest = halves(w_gate, 0)
    u_mine, u_rest = halves(w_up, 0)
    gu_mine = jnp.concatenate([g_mine, u_mine], 0)
    gu_one = to_near(gu_mine, 0)
    w_mine, w_rest = halves(w_down, 1)
    o_one_other = to_core(o_one)
    kv_all = jnp.concatenate(list(kv_before) + [kv_own], 0)
    rows_two = q_two.shape[0] // 2
    for e, two in ((0, q_two), (1, q_two_other)):
        far = 3 - first if e == 0 else first
        q_matrix = put(q_matrix, two[:rows_two], 0, spot(far, e), 0)
        q_matrix = put(q_matrix, two[rows_two:], 0, spot(3, e), 0)
    q_pre = nn(normed, q_matrix)
    feeds.append(to_cols(after(feeds[-1], q_pre), 1))
    mixed, q_rows, top = attend_forward(q_pre, kv_all, cosine, sine, row_ids, key_ids)
    o_matrix = blank((width, width))
    o_matrix = put(o_matrix, o_mine, 1, spot(0, 0), 0)
    o_matrix = put(o_matrix, o_rest, 1, spot(0, 1), 0)
    o_matrix = put(o_matrix, o_one, 1, spot(first, 0), 0)
    o_matrix = put(o_matrix, o_one_other, 1, spot(3 - first, 1), 0)

    (o_two, gu_one, mixed, q_rows, top, o_matrix, w_mine, w_rest, gu_mine, feeds) = fence(
        o_two, gu_one, mixed, q_rows, top, o_matrix, w_mine, w_rest, gu_mine, feeds
    )
    gu_two = to_near(jnp.concatenate([gu_mine, gu_one], 0), 1)
    o_two_other = to_core(o_two)
    gu_one_other = to_core(gu_one)
    w_one = to_near(w_mine, 0)
    rows_two = o_two.shape[0] // 2
    for e, two in ((0, o_two), (1, o_two_other)):
        far = 3 - first if e == 0 else first
        o_matrix = put(o_matrix, two[:rows_two], 1, spot(far, e), 0)
        o_matrix = put(o_matrix, two[rows_two:], 1, spot(3, e), 0)
    branch = nn(mixed, o_matrix)
    middle = inputs + keep * branch
    factor_two = norm_factor(middle)
    hidden_own = (middle * factor_two * gain_two).astype(bf16)
    hidden_own, o_matrix, gu_one_other, gu_one, gu_mine, g_rest, u_rest = fence(
        hidden_own, o_matrix, gu_one_other, gu_one, gu_mine, g_rest, u_rest
    )
    chunks = [hidden_own, to_cols(hidden_own, 1)]
    g_matrix, u_matrix = blank((width, units)), blank((width, units))
    g_matrix = put(g_matrix, gu_mine[:step], 0, spot(0, 0), 0)
    u_matrix = put(u_matrix, gu_mine[step:], 0, spot(0, 0), 0)
    g_matrix = put(g_matrix, g_rest, 0, spot(0, 1), 0)
    u_matrix = put(u_matrix, u_rest, 0, spot(0, 1), 0)
    for e, one in ((0, gu_one), (1, gu_one_other)):
        near = first if e == 0 else 3 - first
        g_matrix = put(g_matrix, one[:step], 0, spot(near, e), 0)
        u_matrix = put(u_matrix, one[step:], 0, spot(near, e), 0)
    d_matrix = blank((units, width))
    d_matrix = put(d_matrix, w_mine, 1, spot(0, 0), 0)
    d_matrix = put(d_matrix, w_rest, 1, spot(0, 1), 0)

    gu_two, g_matrix, u_matrix, d_matrix, w_mine, w_one, chunks = fence(
        gu_two, g_matrix, u_matrix, d_matrix, w_mine, w_one, chunks
    )
    chunks = list(chunks)
    w_two = to_near(jnp.concatenate([w_mine, w_one], 0), 1)
    gu_two_other = to_core(gu_two)
    w_one_other = to_core(w_one)
    d_matrix = put(d_matrix, w_one, 1, spot(first, 0), 0)
    d_matrix = put(d_matrix, w_one_other, 1, spot(3 - first, 1), 0)
    for e, two in ((0, gu_two), (1, gu_two_other)):
        far = 3 - first if e == 0 else first
        for n, at in enumerate((spot(far, e), spot(3, e))):
            piece = two[n * 2 * step : (n + 1) * 2 * step]
            g_matrix = put(g_matrix, piece[:step], 0, at, 0)
            u_matrix = put(u_matrix, piece[step:], 0, at, 0)
    chunks.append(to_cols(chunks[1], 1))

    def gate_up(hidden):
        gate, up = nn(hidden, g_matrix), nn(hidden, u_matrix)
        return gate, up

    near_hidden = jnp.concatenate([chunks[1], chunks[0]], 0)
    near_feed = jnp.concatenate([feeds[1], feeds[0]], 0)
    gate, up = gate_up(near_hidden)
    w_two, gate, up, d_matrix, arrived = fence(w_two, gate, up, d_matrix, chunks[2])
    chunks[2] = arrived
    chunks.append(to_cols(chunks[2], 1))
    w_two_other = to_core(w_two)
    rows_two = w_two.shape[0] // 2
    for e, two in ((0, w_two), (1, w_two_other)):
        far = 3 - first if e == 0 else first
        d_matrix = put(d_matrix, two[:rows_two], 1, spot(far, e), 0)
        d_matrix = put(d_matrix, two[rows_two:], 1, spot(3, e), 0)
    weights = (g_matrix, u_matrix)
    done = [feed_finish(near_feed, gate, up, d_matrix)]
    part = rows_product(done[0][1:], weights, True, bf16, 0, own)
    part, arrived = fence(part, chunks[3])
    chunks[3] = arrived
    for k in range(2, cols - 2):
        carry = to_cols(part, 1)
        chunks.append(to_cols(chunks[k + 1], 1))
        done.append(feed_through(chunks[k], feeds[k], g_matrix, u_matrix, d_matrix))
        part = rows_product(done[-1][1:], weights, True, f32)
        part, carry, arrived, done = fence(part, carry, chunks[k + 2], done)
        done = list(done)
        chunks[k + 2] = arrived
        part = (part + carry.astype(f32)).astype(bf16)
        (part,) = fence(part)
    k = cols - 2
    carry = to_cols(part, 1)
    far_hidden = jnp.concatenate(chunks[k:], 0)
    far_feed = jnp.concatenate(feeds[k:], 0)
    done.append(feed_through(after(far_hidden, part), far_feed, g_matrix, u_matrix, d_matrix))
    hids, gbs, ubs = ([x[n] for x in done] for n in range(3))
    h_parts = [near_hidden] + chunks[2:k] + [far_hidden]
    f_parts = [near_feed] + feeds[2:k] + [far_feed]
    low, high, full = (0, half), (half, half), (0, units)
    part = rows_product((gbs[-1], ubs[-1]), weights, True, f32, 0, own)
    d_sent = token_sum(hids, full, f_parts, high)
    part, carry, d_sent, hids, gbs, ubs, h_parts, f_parts = fence(
        part, carry, d_sent, hids, gbs, ubs, h_parts, f_parts
    )
    part = (part + carry.astype(f32)).astype(bf16)
    part, d_sent, hids, gbs, ubs = fence(part, d_sent, hids, gbs, ubs)

    carry = to_cols(part, 1)
    d_received = to_core(d_sent)
    part, own_part = rows_products(
        [((gbs[-1], ubs[-1]), 1), ((gbs[0], ubs[0]), 1)], weights, True, f32, own
    )
    g_sent, u_sent = token_sums(h_parts, high, [gbs, ubs], full)
    d_sum = token_sum(hids, full, f_parts, low, d_received)
    part, own_part, carry, d_sum, g_sent, u_sent, hids, gbs, ubs = fence(
        part, own_part, carry, d_sum, g_sent, u_sent, hids, gbs, ubs
    )
    part = (part + carry.astype(f32)).astype(bf16)
    part, own_part, d_sum, g_sent, u_sent, gbs, ubs, hids = fence(
        part, own_part, d_sum, g_sent, u_sent, gbs, ubs, hids
    )

    def prepare(total, axis):
        pieces = jnp.split(total, rows, axis)
        sent = jnp.concatenate([jnp.where(d == 0, pieces[1], pieces[2]), pieces[3]], axis)
        return pieces[0], jnp.where(d == 0, pieces[2], pieces[1]), sent

    def half_way(parts, near, axis):
        mine, theirs = jnp.split(near, 2, axis)
        return (parts[0], mine), (parts[1].astype(f32) + theirs.astype(f32)).astype(bf16)

    def finish(kept, far):
        return kept[0].astype(f32) + kept[1].astype(f32) + far.astype(f32)

    def around(carry, part):
        return to_cols((part.astype(f32) + carry.astype(f32)).astype(bf16), 1)

    def col_sum(total, axis):
        pieces = xor_blocks(jnp.split(total.astype(bf16), cols, axis), c)
        return [pieces[0]] + [to_xor_cols(pieces[k], k) for k in range(1, cols)]

    def added(values):
        return tree_sum([x.astype(f32) for x in values])

    carry = to_cols(part, 1)
    d_parts = prepare(d_sum, 1)
    d_near = to_near(d_parts[2], 0)
    g_received = to_core(g_sent)
    u_received = to_core(u_sent)
    outs = jnp.split(rows_product([hids[0]], [d_matrix], False, bf16), 2, 0)
    g_sum, u_sum = token_sums(h_parts, low, [gbs, ubs], full, [g_received, u_received])
    g_parts, u_parts = prepare(g_sum, 0), prepare(u_sum, 0)
    part, carry, d_near, g_parts, u_parts, hids, outs = fence(
        own_part, carry, d_near, g_parts, u_parts, hids, outs
    )

    out_carry = to_cols(outs[0], 1)
    out_last = outs[1]
    g_near = to_near(g_parts[2], 0)
    d_kept, d_theirs = half_way(d_parts, d_near, 1)
    d_far = to_near(d_theirs, 1)
    hidden_in_back = part + carry.astype(f32)
    from_norm, mlp_gain_part = norm_back(hidden_in_back, middle, factor_two, gain_two)
    middle_grad = upstream + from_norm
    branch_back = (keep * middle_grad).astype(bf16)
    mixed_back = rows_product([branch_back], [o_matrix], True, bf16)
    o_sent = token_sum([mixed], (0, width), [branch_back], high)
    outs = [None] + [rows_product([x], [d_matrix], False, bf16) for x in hids[1:-1]]
    outs += jnp.split(rows_product([hids[-1]], [d_matrix], False, bf16), 2, 0)
    mixed_back, branch_back, o_sent, d_far, g_near, outs, out_carry = fence(
        mixed_back, branch_back, o_sent, d_far, g_near, outs, out_carry
    )

    u_near = to_near(u_parts[2], 0)
    g_kept, g_theirs = half_way(g_parts, g_near, 0)
    g_far = to_near(g_theirs, 1)
    for k in range(1, cols - 2):
        out_carry = around(out_carry, outs[k])
    o_received = to_core(o_sent)
    dq, dk, dv = attend_backward(
        q_rows, kv_all, mixed_back, top, cosine, -sine, row_ids, key_ids
    )
    o_sum = token_sum([mixed], (0, width), [branch_back], low, o_received)
    o_low, o_high = jnp.split(o_sum, 2, 0)
    o_low = prepare(o_low, 1)
    dq, dk, dv, o_low, o_high, g_far, u_near, out_carry = fence(
        dq, dk, dv, o_low, o_high, g_far, u_near, out_carry
    )

    kv_turned = jnp.concatenate([dk, dv], 1)
    kv_back_pre = kv_turned[reach * own :]
    back_parts = []
    for k in range(1, reach + 1):
        piece = kv_turned[(reach - k) * own : (reach - k + 1) * own].astype(bf16)
        back_parts.append(along(piece, -k))
    u_kept, u_theirs = half_way(u_parts, u_near, 0)
    u_far = to_near(u_theirs, 1)
    o_low_near = to_near(o_low[2], 0)
    q_sent = token_sum([normed], high, [dq], (0, width))
    o_high = prepare(o_high, 1)
    back_parts, q_sent, u_far, o_low_near, o_high = fence(
        back_parts, q_sent, u_far, o_low_near, o_high
    )

    out_carry = around(out_carry, outs[cols - 2])
    o_low_kept, o_theirs = half_way(o_low, o_low_near, 1)
    o_low_far = to_near(o_theirs, 1)
    q_received = to_core(q_sent)
    for piece in back_parts:
        kv_back_pre = kv_back_pre + piece.astype(f32)
    kv_back = jnp.concatenate(
        [rotate(kv_back_pre[:, :kv_width], cosine, -sine), kv_back_pre[:, kv_width:]], 1
    ).astype(bf16)
    kv_sent = token_sum([normed], high, [kv_back], (0, 2 * kv_width))
    kv_received = to_core(kv_sent)
    kv_sum = token_sum([normed], low, [kv_back], (0, 2 * kv_width), kv_received)
    kv_parts = prepare(kv_sum, 0)
    kv_parts, kv_back, o_low_far, q_received, o_high = fence(
        kv_parts, kv_back, o_low_far, q_received, o_high
    )

    kv_near = to_near(kv_parts[2], 0)
    o_high_near = to_near(o_high[2], 0)
    normed_back = rows_product([dq, kv_back], [q_matrix, kv_matrix], True, f32)
    from_norm, attention_gain_part = norm_back(normed_back, inputs, factor_one, gain_one)
    input_grad = xor_order(middle_grad + from_norm, target, blocks, 1)
    gains = xor_order(jnp.stack([attention_gain_part, mlp_gain_part]), target, blocks, 1)
    q_sum = token_sum([normed], low, [dq], (0, width), q_received)
    kv_near, o_high_near, input_grad, gains, q_sum, out_carry = fence(
        kv_near, o_high_near, input_grad, gains, q_sum, out_carry
    )

    kv_kept, kv_theirs = half_way(kv_parts, kv_near, 0)
    kv_far = to_near(kv_theirs, 1)
    o_high_kept, o_theirs = half_way(o_high, o_high_near, 1)
    o_high_far = to_near(o_theirs, 1)
    hops = [1 << n for n in range(cols.bit_length() - 1)]
    gains = gains + to_xor_cols(gains, hops[0])
    q_parts = prepare(q_sum, 0)
    kv_far, o_high_far, gains, q_parts = fence(kv_far, o_high_far, gains, q_parts)

    q_near = to_near(q_parts[2], 0)
    kv_sum = finish(kv_kept, kv_far).astype(bf16)
    total = [kv_sum] + [to_xor_cols(kv_sum, k) for k in range(1, cols)]
    for hop in hops[1:]:
        gains = gains + to_xor_cols(gains, hop)
    out_sum = jnp.concatenate(
        [finish(o_low_kept, o_low_far), finish(o_high_kept, o_high_far)], 0
    ).astype(bf16)
    total, q_near, gains, out_sum = fence(total, q_near, gains, out_sum)

    total = added(total).astype(bf16)
    one = to_near(total, 0)
    q_kept, q_theirs = half_way(q_parts, q_near, 0)
    q_far = to_near(q_theirs, 1)
    out_parts = col_sum(out_sum, 0)
    one, d_far, g_far, u_far, out_carry = fence(one, d_far, g_far, u_far, out_carry)
    down_grad, gate_grad, up_grad = finish(d_kept, d_far), finish(g_kept, g_far), finish(u_kept, u_far)
    piece = out_last.astype(f32) + out_carry.astype(f32)
    output = xor_order((middle + keep * piece).astype(bf16), target, blocks, 1)
    one, q_far, out_parts, output, gains, down_grad, gate_grad, up_grad = fence(
        one, q_far, out_parts, output, gains, down_grad, gate_grad, up_grad
    )

    two = to_near(jnp.concatenate([total, one], 0), 1)
    gains = gains + to_near(gains, 0)
    gains = gains + to_near(gains, 1)
    q_cols = col_sum(finish(q_kept, q_far), 1)
    out_grad = added(out_parts)
    two, q_cols, out_grad, gains = fence(two, q_cols, out_grad, gains)
    mine = jnp.concatenate([total, one, two], 0)
    theirs = to_core(mine)
    gains = gains + to_core(gains)
    query_grad = added(q_cols)
    found = blank((width, 2 * kv_width))
    for e, part in enumerate((mine, theirs)):
        near, far = (first, 3 - first) if e == 0 else (3 - first, first)
        for n, j in enumerate((0, near, far, 3)):
            at = ((d ^ e) * rows + (r ^ j)) * step
            found = put(found, part[n * step : (n + 1) * step], 0, at, 0)
    found = found.astype(f32)
    key_grad, value_grad = found[:, :kv_width], found[:, kv_width:]
    return (
        output,
        input_grad,
        gains[0],
        gains[1],
        query_grad,
        key_grad,
        value_grad,
        out_grad,
        gate_grad,
        up_grad,
        down_grad,
    )


def solution(mesh):
    return jax.shard_map(
        local,
        mesh=mesh,
        in_specs=(
            P(("dp", "rows", "cols"), None),
            P(),
            P(),
            P("rows", "cols"),
            P("rows", None),
            P("rows", None),
            P(None, "rows"),
            P("rows", "cols"),
            P("rows", "cols"),
            P("cols", "rows"),
            P(("dp", "rows"), None),
            P(("dp", "rows")),
            P(("dp", "rows", "cols"), None),
        ),
        out_specs=(
            P(("dp", "rows", "cols"), None),
            P(("dp", "rows", "cols"), None),
            P(),
            P(),
            P(("dp", "rows"), "cols"),
            P(),
            P(),
            P("cols", ("dp", "rows")),
            P(("dp", "rows"), "cols"),
            P(("dp", "rows"), "cols"),
            P("cols", ("dp", "rows")),
        ),
        check_vma=False,
    )
```
